256 devices in a mesh: head: 8 (over y, core), doc: 32 (over x, z).
Axes of the slice: x: 4, y: 4, z: 8, core: 2. Of those that a mesh axis runs over, the one named last changes fastest.
Arguments:
- tokens: bfloat16 [12288, 1024], P('doc'), may hold values from -6 to 6
- w_qkv: bfloat16 [1024, 3, 1024], P(None, None, 'head'), may hold values from -0.1875 to 0.1875
- w_out: bfloat16 [1024, 1024], P('head'), may hold values from -0.1875 to 0.1875
- w_up: bfloat16 [1024, 4096], P(None, 'head'), may hold values from -0.1875 to 0.1875
- w_down: bfloat16 [4096, 1024], P('head'), may hold values from -0.09375 to 0.09375
- gain_one: float32 [1024], replicated, may hold values from 0.5 to 1.5
- gain_two: float32 [1024], replicated, may hold values from 0.5 to 1.5
- rel_table: bfloat16 [512, 1024], replicated, may hold values from -6 to 6
- prompt_cache: bfloat16 [2, 4096, 1024], P(None, 'doc', 'head'), may hold values from -480 to 480
- w_proj: bfloat16 [1024, 128], replicated, may hold values from -0.1875 to 0.1875
- doc_vectors: bfloat16 [2048, 256, 128], P('doc'), may hold values from -0.5 to 0.5
- doc_lengths: int32 [2048], P('doc'), may hold values from 8 to 256, as said below
- group_ids: int32 [384], P('doc'), may hold values from 0 to 63
- candidates: int32 [384, 64], P('doc', 'head'), may hold values from 0 to 2047, as said below
Outputs:
- query_vectors: bfloat16 [12288, 128], P('doc')
- scores: float32 [384, 64], P('doc', 'head')
The draws below stay inside these ranges and needn't reach their ends.
Inputs may be any that keep to these rules, and one draw needn't show every extreme that they name: Split candidates into aligned blocks of 12 requests by 8 columns (one index of doc with one of head). Index o of doc holds documents o * 64 to o * 64 + 63. In each block at most 6 entries name documents held by one index of doc, and one index of doc, the same for all blocks, is named by exactly 6 entries of every block. The documents named within one block are distinct. Some document has exactly 256 tokens; token slots from doc_lengths on are padding.
All inputs are finite; a program needn't handle non-finite values.
Results may differ from the reference program's by a relative error of at most 0.02.
Values may be sent and summed in bfloat16 or wider, within the bound.
A program may use at most 128 MiB of HBM per device.

```python
import math
import jax
import jax.numpy as jnp
from jax import lax

D = 1024
HEADS = 16
HD = 64
FF = 4096
RELS = 512
EMB = 128
QLEN = 32
PLEN = 64
DLEN = 256
DOC_DEV = 64
CAND_DEV = 8
REQ_DEV = 12
REQ = 384
TOKENS = 12288
CAND = 64
GROUPS = 64
DOCS = 2048
CAP = 6
N_HEAD = 8
N_DOC = 32


def draw_prompt_cache(key, part):
    base_key = jax.random.fold_in(key, 0)
    values = jnp.clip(jax.random.normal(base_key, (2, GROUPS * PLEN, D), jnp.float32), -6.0, 6.0)
    return values.astype(jnp.bfloat16)


def draw_doc_lengths(key, part):
    first_key, second_key = jax.random.split(key, 2)
    lengths = jax.random.randint(first_key, (DOCS,), 8, DLEN + 1, dtype=jnp.int32)
    longest = jax.random.randint(second_key, (), 0, DOCS, dtype=jnp.int32)
    return jnp.where(jnp.arange(DOCS, dtype=jnp.int32) == longest, DLEN, lengths).astype(jnp.int32)


def draw_candidates(key, part):
    shards = REQ // REQ_DEV
    columns = CAND // CAND_DEV
    pairs = REQ_DEV * CAND_DEV
    slot_count = shards * CAP
    forced_key, block_key = jax.random.split(key, 2)
    forced = jax.random.randint(forced_key, (), 0, shards, dtype=jnp.int32)

    def one_block(block_seed):
        first_key, second_key, third_key = jax.random.split(block_seed, 3)
        shuffled = jax.random.permutation(first_key, slot_count).astype(jnp.int32)
        holder = shuffled // CAP
        priority = jnp.where(holder == forced, 0, 1) * slot_count + jnp.arange(slot_count, dtype=jnp.int32)
        order = jnp.argsort(priority, stable=True)
        picked = shuffled[order][:pairs]
        mixing = jax.random.permutation(second_key, pairs)
        picked = picked[mixing]
        owners = picked // CAP
        within = picked % CAP
        offsets = jax.random.randint(third_key, (shards,), 0, DOC_DEV, dtype=jnp.int32)
        local_doc = (within + offsets[owners]) % DOC_DEV
        return (owners * DOC_DEV + local_doc).reshape(REQ_DEV, CAND_DEV).astype(jnp.int32)
    seeds = jax.random.split(block_key, shards * columns)
    blocks = jax.vmap(one_block)(seeds).reshape(shards, columns, REQ_DEV, CAND_DEV)
    return jnp.transpose(blocks, (0, 2, 1, 3)).reshape(REQ, CAND).astype(jnp.int32)


def plant(array, stream_key, least, high):
    index_at = [jax.random.randint(jax.random.fold_in(stream_key, axis), (), 0, length) for axis, length in enumerate(array.shape)]
    widest = array.shape.index(max(array.shape))
    next_to = index_at[:widest] + [(index_at[widest] + 1) % array.shape[widest]] + index_at[widest + 1:]
    return array.at[tuple(index_at)].set(least).at[tuple(next_to)].set(high)


def levels(own_key, dims, cuts, smallest, high):
    def one(dim, blocks):
        heights = jax.random.uniform(jax.random.fold_in(jax.random.fold_in(own_key, 6), dim), (blocks,), jnp.float32, smallest / len(cuts), high / len(cuts))
        return jnp.repeat(jnp.exp(heights), dims[dim] // blocks).reshape((-1,) + (1,) * (len(dims) - dim - 1))

    factor_of = one(*cuts[0])
    for cut in cuts[1:]:
        factor_of = factor_of * one(*cut)
    return factor_of


def noise(key, dims, scale, reach, cuts=(), kind=jnp.bfloat16):
    array = scale * jax.random.normal(key, dims, jnp.float32)
    if cuts:
        array = array * levels(key, dims, cuts, -0.22, 0.18)
    return jnp.clip(array, -reach, reach).astype(kind)


def setup_inputs(seed: int = 0) -> dict:
    key_of = jax.random.split(jax.random.key(seed), 15)
    tokens = noise(key_of[0], (TOKENS, D), 1.0, 6.0, ((0, 32),))
    w_qkv = noise(key_of[1], (D, 3, D), D ** -0.5, 0.1875, ((2, 8),))
    w_out = noise(key_of[2], (D, D), D ** -0.5, 0.1875, ((0, 8),))
    w_up = noise(key_of[3], (D, FF), D ** -0.5, 0.1875, ((1, 8),))
    w_down = noise(key_of[4], (FF, D), FF ** -0.5, 0.09375, ((0, 8),))
    gain_one = jnp.clip(1.0 + 0.1 * jax.random.normal(key_of[5], (D,), jnp.float32), 0.5, 1.5)
    gain_two = jnp.clip(1.0 + 0.1 * jax.random.normal(key_of[6], (D,), jnp.float32), 0.5, 1.5)
    rel_table = noise(key_of[7], (RELS, D), 1.0, 6.0)
    prompt_cache = draw_prompt_cache(jax.random.fold_in(key_of[14], 71), 0)
    w_proj = noise(key_of[9], (D, EMB), D ** -0.5, 0.1875)
    doc_vectors = noise(key_of[10], (DOCS, DLEN, EMB), 0.0884, 0.5, ((0, 32),))
    doc_lengths = draw_doc_lengths(jax.random.fold_in(key_of[14], 71), 0)
    group_ids = plant(jax.random.randint(key_of[12], (REQ,), 0, GROUPS), jax.random.fold_in(key_of[12], 1), 0, GROUPS - 1).astype(jnp.int32)
    candidates = draw_candidates(jax.random.fold_in(key_of[14], 71), 0)
    return {"tokens": tokens, "w_qkv": w_qkv, "w_out": w_out, "w_up": w_up, "w_down": w_down, "gain_one": gain_one, "gain_two": gain_two, "rel_table": rel_table, "prompt_cache": prompt_cache, "w_proj": w_proj, "doc_vectors": doc_vectors, "doc_lengths": doc_lengths, "group_ids": group_ids, "candidates": candidates}


def layer_norm(values, gain):
    centre = values - lax.optimization_barrier(jnp.mean(values, axis=-1, keepdims=True))
    spread = lax.optimization_barrier(jnp.mean(centre * centre, axis=-1, keepdims=True))
    return centre * lax.rsqrt(spread + 1e-07) * gain.astype(jnp.float32)

def attend_request(query, keys_own, values_own, group, prompt_cache, rel_q, rel_k):
    start = (group * PLEN).astype(jnp.int32)
    cache_keys = lax.dynamic_slice_in_dim(prompt_cache[0], start, PLEN, 0).reshape(PLEN, HEADS, HD)
    cache_values = lax.dynamic_slice_in_dim(prompt_cache[1], start, PLEN, 0).reshape(PLEN, HEADS, HD)
    keys = jnp.concatenate([keys_own, cache_keys], axis=0).astype(jnp.float32)
    values = jnp.concatenate([values_own, cache_values], axis=0).astype(jnp.float32)
    query_f = query.astype(jnp.float32)
    pos_query = PLEN + jnp.arange(QLEN, dtype=jnp.int32)
    pos_key = jnp.concatenate([pos_query, jnp.arange(PLEN, dtype=jnp.int32)])
    total_keys = QLEN + PLEN
    query_rel = jnp.einsum('qhd,rhd->qhr', query_f, rel_k.astype(jnp.float32))
    index_one = pos_query[:, None] - pos_key[None, :] + RELS // 2
    c2p = jnp.take_along_axis(query_rel, jnp.broadcast_to(index_one[:, None, :], (QLEN, HEADS, total_keys)), axis=2)
    key_rel = jnp.einsum('khd,rhd->khr', keys, rel_q.astype(jnp.float32))
    index_two = pos_key[:, None] - pos_query[None, :] + RELS // 2
    p2c = jnp.take_along_axis(key_rel, jnp.broadcast_to(index_two[:, None, :], (total_keys, HEADS, QLEN)), axis=2)
    p2c = jnp.transpose(p2c, (2, 1, 0))
    logits = (jnp.einsum('qhd,khd->qhk', query_f, keys) + c2p + p2c) / math.sqrt(3 * HD)
    largest = lax.optimization_barrier(jnp.max(logits, axis=-1, keepdims=True))
    weights = jnp.exp(logits - largest)
    denominator = lax.optimization_barrier(jnp.sum(weights, axis=-1))
    rounded = lax.optimization_barrier(weights.astype(jnp.bfloat16)).astype(jnp.float32)
    output = jnp.einsum('qhk,khd->qhd', rounded, values) / denominator[..., None]
    return output.reshape(QLEN, D).astype(jnp.bfloat16)

def score_pair(request_vectors, cand, doc_vectors, doc_lengths):
    document = doc_vectors[cand]
    sims = jnp.dot(request_vectors, document.T, preferred_element_type=jnp.float32)
    live = jnp.arange(DLEN, dtype=jnp.int32) < doc_lengths[cand]
    best = lax.optimization_barrier(jnp.max(jnp.where(live[None, :], sims, -jnp.inf), axis=1))
    return jnp.sum(best)

def reference(tokens, w_qkv, w_out, w_up, w_down, gain_one, gain_two, rel_table, prompt_cache, w_proj, doc_vectors, doc_lengths, group_ids, candidates):
    projected_all = jnp.einsum('td,dcf->ctf', tokens.astype(jnp.float32), w_qkv.astype(jnp.float32)).astype(jnp.bfloat16)
    rel_both = jnp.einsum('rd,dcf->crf', rel_table.astype(jnp.float32), w_qkv[:, :2].astype(jnp.float32)).astype(jnp.bfloat16)
    rel_q = rel_both[0].reshape(RELS, HEADS, HD)
    rel_k = rel_both[1].reshape(RELS, HEADS, HD)
    shape = (N_DOC, REQ_DEV, QLEN, HEADS, HD)
    queries = projected_all[0].reshape(shape)
    keys_all = projected_all[1].reshape(shape)
    values_all = projected_all[2].reshape(shape)
    groups = group_ids.reshape(N_DOC, REQ_DEV)

    def per_shard(inputs):
        inner_fn = jax.vmap(attend_request, in_axes=(0, 0, 0, 0, None, None, None))
        return inner_fn(inputs[0], inputs[1], inputs[2], inputs[3], prompt_cache, rel_q, rel_k)
    attended = lax.map(per_shard, (queries, keys_all, values_all, groups)).reshape(TOKENS, D)
    width = D // N_HEAD
    total = jnp.zeros((TOKENS, D), jnp.float32)
    for block in range(N_HEAD):
        partial_sum = jnp.dot(attended[:, block * width:(block + 1) * width], w_out[block * width:(block + 1) * width], preferred_element_type=jnp.float32)
        total = total + lax.optimization_barrier(partial_sum.astype(jnp.bfloat16)).astype(jnp.float32)
    hidden_one = layer_norm(tokens.astype(jnp.float32) + total, gain_one).astype(jnp.bfloat16)
    inner = jax.nn.gelu(jnp.dot(hidden_one, w_up, preferred_element_type=jnp.float32), approximate=False).astype(jnp.bfloat16)
    hidden_width = FF // N_HEAD
    total_two = jnp.zeros((TOKENS, D), jnp.float32)
    for block in range(N_HEAD):
        partial_sum = jnp.dot(inner[:, block * hidden_width:(block + 1) * hidden_width], w_down[block * hidden_width:(block + 1) * hidden_width], preferred_element_type=jnp.float32)
        total_two = total_two + lax.optimization_barrier(partial_sum.astype(jnp.bfloat16)).astype(jnp.float32)
    hidden_two = layer_norm(hidden_one.astype(jnp.float32) + total_two, gain_two).astype(jnp.bfloat16)
    projected = jnp.dot(hidden_two, w_proj, preferred_element_type=jnp.float32)
    query_vectors = (projected * lax.rsqrt(lax.optimization_barrier(jnp.sum(projected * projected, axis=-1, keepdims=True)) + 1e-06)).astype(jnp.bfloat16)

    def score_shard(inputs):
        by_cand = jax.vmap(score_pair, in_axes=(None, 0, None, None))
        by_request = jax.vmap(by_cand, in_axes=(0, 0, None, None))
        return by_request(inputs[0], inputs[1], doc_vectors, doc_lengths)
    scores = lax.map(score_shard, (query_vectors.reshape(N_DOC, REQ_DEV, QLEN, EMB), candidates.reshape(N_DOC, REQ_DEV, CAND)))
    return (query_vectors, scores.reshape(REQ, CAND))
```

```python
import functools
import math

import jax
import jax.numpy as jnp
from jax import lax
from jax.experimental import pallas as pl
from jax.experimental.pallas import tpu as pltpu
from jax.sharding import PartitionSpec as P

HD = 64
RELS = 512
QLEN = 32
PLEN = 64
DOC_DEV = 64
NX = 4
NZ = 8
NY = 4
MESH = pl.DeviceIdType.MESH
F32 = jnp.float32
BF16 = jnp.bfloat16
NT = (((1,), (1,)), ((), ()))


def mod(value, size):
    return lax.rem(value + 4 * size, size)


class Message:
    def __init__(self, kv, axis, sign, dx, dz, low, rows, parent):
        self.kv, self.axis, self.sign, self.dx, self.dz = kv, axis, sign, dx, dz
        self.low, self.rows, self.parent = low, rows, parent
        self.children = []
        self.time = None
        self.index = None


def plan_gather():
    made = []

    def add(kv, axis, sign, dx, dz, low, rows, parent):
        message = Message(kv, axis, sign, dx, dz, low, rows, parent)
        made.append(message)
        return message

    def along_x(kv, dz, low, rows, parent):
        out = []
        for sign in (1, -1):
            near = add(kv, "x", sign, sign, dz, low, rows, parent)
            half = rows // 2
            far = add(kv, "x", sign, 2 * sign, dz, low if sign > 0 else low + half, half, near)
            out += [near, far]
        return out

    def along_z(kv, dx, low, rows, parent):
        out = []
        for sign in (1, -1):
            previous = parent
            for step in range(1, 4):
                previous = add(kv, "z", sign, dx, sign * step, low, rows, previous)
                out.append(previous)
            half = rows // 2
            out.append(add(kv, "z", sign, dx, sign * 4, low if sign > 0 else low + half, half, previous))
        return out

    firsts = along_z(0, 0, 0, 128, None)
    along_x(0, 0, 0, 128, None)
    for first in firsts:
        along_x(0, first.dz, first.low, first.rows, first)
    firsts = along_x(1, 0, 0, 128, None)
    along_z(1, 0, 0, 128, None)
    for first in firsts:
        along_z(1, first.dx, first.low, first.rows, first)
    for message in made:
        if message.parent is not None:
            message.parent.children.append(message)
    free = {}
    ready = [(0.0, i) for i, m in enumerate(made) if m.parent is None]
    while ready:
        ready.sort()
        start, i = ready.pop(0)
        message = made[i]
        link = (message.axis, message.sign)
        begin = max(start, free.get(link, 0.0))
        free[link] = begin + message.rows * 256 / 46500.0
        message.time = free[link] + 1.6
        ready += [(message.time, made.index(child)) for child in message.children]
    order = sorted(made, key=lambda m: m.time)
    for index, message in enumerate(order):
        message.index = index
    return order


def norm_rows(values, gain):
    centre = values - jnp.mean(values, axis=-1, keepdims=True)
    spread = jnp.mean(centre * centre, axis=-1, keepdims=True)
    return centre * lax.rsqrt(spread + 1e-07) * gain


def gelu(values):
    return 0.5 * values * (1.0 + lax.erf(values * (1.0 / math.sqrt(2.0))))


def encoder_kernel(
    plan,
    group_ref,
    tokens_hbm,
    w_qkv_hbm,
    w_out_hbm,
    w_up_hbm,
    w_down_hbm,
    gain_one_ref,
    gain_two_ref,
    rel_hbm,
    cache_hbm,
    w_proj_ref,
    query_out,
    cache,
    tokens,
    w_qkv,
    w_out,
    w_up,
    w_down,
    rel,
    q_mask,
    k_own,
    v_own,
    q_rel,
    rel_two,
    att,
    att_send,
    opp_send,
    side_send,
    opp_recv,
    side_recv,
    hidden,
    vectors,
    load_sem,
    gather_send,
    gather_recv,
    swap_send,
    swap_recv,
    att_sem,
    opp_send_sem,
    opp_recv_sem,
    side_send_sem,
    side_recv_sem,
    hid_send_sem,
    hid_recv_sem,
    vec_send_sem,
    vec_recv_sem,
):
    head = lax.axis_index("head")
    doc = lax.axis_index("doc")
    y, core = lax.div(head, 2), lax.rem(head, 2)
    x, z = lax.div(doc, NZ), lax.rem(doc, NZ)
    partner = (2 * y + 1 - core, doc)
    y_up, y_down = mod(y + 1, NY), mod(y - 1, NY)
    y_far = mod(y + 2, NY)

    def at_y(other):
        return (2 * other + core, doc)

    def at_link(axis, sign):
        if axis == "x":
            return (head, mod(x + sign, NX) * NZ + z)
        return (head, x * NZ + mod(z + sign, NZ))

    peers = [partner]
    for other in (y_up, y_down, y_far):
        peers += [(2 * other + core, doc), (2 * other + 1 - core, doc)]
    links = [at_link(axis, sign) for axis in ("x", "z") for sign in (1, -1)]
    barrier = pltpu.get_barrier_semaphore()
    for device in peers + links:
        pl.semaphore_signal(barrier, inc=1, device_id=device, device_id_type=MESH)

    loads = [
        pltpu.make_async_copy(tokens_hbm, tokens, load_sem.at[0]),
        pltpu.make_async_copy(w_qkv_hbm, w_qkv, load_sem.at[1]),
        pltpu.make_async_copy(rel_hbm.at[pl.ds(RELS // 2 - 96, 128)], rel.at[0], load_sem.at[2]),
        pltpu.make_async_copy(rel_hbm.at[pl.ds(RELS // 2 - 32, 128)], rel.at[1], load_sem.at[3]),
        pltpu.make_async_copy(
            cache_hbm, cache.at[:, pl.ds(doc * 2, 2)], load_sem.at[4]
        ),
        pltpu.make_async_copy(w_out_hbm, w_out.at[core], load_sem.at[5]),
        pltpu.make_async_copy(w_up_hbm, w_up.at[core], load_sem.at[6]),
        pltpu.make_async_copy(w_down_hbm, w_down.at[core], load_sem.at[7]),
    ]
    for load in loads:
        load.start()
    pl.semaphore_wait(barrier, len(peers) + len(links))

    def gather_copy(message):
        dx, dz = message.dx, message.dz
        if message.axis == "x":
            dx -= message.sign
        else:
            dz -= message.sign
        block = mod(x - dx, NX) * NZ + mod(z - dz, NZ)
        group, low = block * 2 + message.low // PLEN, message.low % PLEN
        if message.rows == 2 * PLEN:
            target = cache.at[message.kv, pl.ds(group, 2)]
        else:
            target = cache.at[message.kv, group, pl.ds(low, message.rows)]
        source = cache_hbm.at[message.kv] if message.parent is None else target
        return pltpu.make_async_remote_copy(
            src_ref=source,
            dst_ref=target,
            send_sem=gather_send.at[message.index],
            recv_sem=gather_recv.at[message.index],
            device_id=at_link(message.axis, message.sign),
            device_id_type=MESH,
        )

    copies = {message.index: gather_copy(message) for message in plan}
    for message in plan:
        if message.parent is None:
            copies[message.index].start()

    swaps = []
    for i, (source, target) in enumerate(((w_out_hbm, w_out), (w_up_hbm, w_up), (w_down_hbm, w_down))):
        swaps.append(
            pltpu.make_async_remote_copy(
                src_ref=source,
                dst_ref=target.at[core],
                send_sem=swap_send.at[i],
                recv_sem=swap_recv.at[i],
                device_id=partner,
                device_id_type=MESH,
            )
        )
        swaps[-1].start()

    loads[0].wait()
    loads[1].wait()
    low_head = lax.broadcasted_iota(jnp.int32, (128, 128), 1) < HD
    for block in range(3):
        rows = slice(block * 128, block * 128 + 128)
        made = jnp.dot(tokens[rows, :], w_qkv[...], preferred_element_type=F32)
        q_made = made[:, :128]
        q_mask[0, rows, :] = jnp.where(low_head, q_made, 0.0).astype(BF16)
        q_mask[1, rows, :] = jnp.where(low_head, 0.0, q_made).astype(BF16)
        k_own[rows, :] = made[:, 128:256].astype(BF16)
        v_own[rows, :] = made[:, 256:].astype(BF16)
    loads[2].wait()
    loads[3].wait()
    flip = (
        lax.broadcasted_iota(jnp.int32, (128, 128), 0) + lax.broadcasted_iota(jnp.int32, (128, 128), 1)
        == 127
    ).astype(F32).astype(BF16)
    for i in range(2):
        row = jnp.dot(
            rel[i], w_qkv[:, i * 128 : i * 128 + 128], preferred_element_type=F32
        ).astype(BF16)
        turned = jnp.dot(flip, row, preferred_element_type=F32)
        rel_two[i, 0:128, :] = jnp.where(low_head, turned, 0.0).astype(BF16)
        rel_two[i, 128:256, :] = jnp.where(low_head, 0.0, turned).astype(BF16)
    for block in range(3):
        rows = slice(block * 128, block * 128 + 128)
        q_all = q_mask[0, rows, :] + q_mask[1, rows, :]
        q_rel[rows, :] = lax.dot_general(q_all, rel_two[1], NT, preferred_element_type=F32)
    loads[4].wait()

    for message in plan:
        copies[message.index].wait_recv()
        for child in message.children:
            copies[child.index].start()

    low_lane = lax.broadcasted_iota(jnp.int32, (96, 128), 1) < QLEN
    low_half = lax.broadcasted_iota(jnp.int32, (QLEN, 128), 1) < HD

    def attend(request):
        group = group_ref[request]
        own = pl.ds(pl.multiple_of(request * QLEN, QLEN), QLEN)
        keys = jnp.concatenate([cache[0, group], k_own[own, :]], axis=0)
        values = jnp.concatenate([cache[1, group], v_own[own, :]], axis=0)
        query = jnp.concatenate([q_mask[0, own, :], q_mask[1, own, :]], axis=0)
        content = lax.dot_general(query, keys, NT, preferred_element_type=F32)
        key_rel = lax.dot_general(keys, rel_two[0], NT, preferred_element_type=F32)
        first = pltpu.roll(key_rel[:, :128], 33, 1, stride=1, stride_axis=0)
        second = pltpu.roll(key_rel[:, 128:], 65, 1, stride=1, stride_axis=0)
        p2c = jnp.transpose(jnp.where(low_lane, first, second))[: 2 * QLEN, :]
        mine = q_rel[own, :]
        c2p = jnp.concatenate(
            [
                pltpu.roll(mine[:, :128], 97, 1, stride=1, stride_axis=0),
                pltpu.roll(mine[:, 128:], 97, 1, stride=1, stride_axis=0),
            ],
            axis=0,
        )[:, :96]
        logits = (content + c2p + p2c) * (1.0 / math.sqrt(3 * HD))
        weights = jnp.exp(logits - jnp.max(logits, axis=-1, keepdims=True))
        total = jnp.sum(weights, axis=-1, keepdims=True)
        out = jnp.dot(weights.astype(BF16), values, preferred_element_type=F32) / total
        return jnp.where(low_half, out[:QLEN], out[QLEN:]).astype(BF16)

    half = tokens.shape[0] // 2
    per_core = half // QLEN
    for i in range(per_core):
        att_send[i * QLEN : i * QLEN + QLEN, :] = attend((1 - core) * per_core + i)
    att_copy = pltpu.make_async_remote_copy(
        src_ref=att_send,
        dst_ref=att.at[core],
        send_sem=att_sem.at[0],
        recv_sem=att_sem.at[1],
        device_id=partner,
        device_id_type=MESH,
    )
    att_copy.start()
    for i in range(per_core):
        att[core, i * QLEN : i * QLEN + QLEN, :] = attend(core * per_core + i)
    att_copy.wait_recv()
    loads[5].wait()
    swaps[0].wait_recv()
    part = half // NY

    def chunk_rows(other):
        return pl.ds(pl.multiple_of(other * part, 16), part)

    def out_part(other):
        rows = chunk_rows(other)
        return jnp.dot(att[0, rows, :], w_out[0], preferred_element_type=F32) + jnp.dot(
            att[1, rows, :], w_out[1], preferred_element_type=F32
        )

    def side_copy(phase, side, piece):
        return pltpu.make_async_remote_copy(
            src_ref=side_send.at[phase, side, piece],
            dst_ref=side_recv.at[phase, side, piece],
            send_sem=side_send_sem.at[phase, side, piece],
            recv_sem=side_recv_sem.at[phase, side, piece],
            device_id=at_y(y_down if side else y_up),
            device_id_type=MESH,
        )

    def far_copy(phase, piece):
        return pltpu.make_async_remote_copy(
            src_ref=opp_send.at[phase, piece],
            dst_ref=opp_recv.at[phase, piece],
            send_sem=opp_send_sem.at[phase, piece],
            recv_sem=opp_recv_sem.at[phase, piece],
            device_id=at_y(y_down if piece else y_up),
            device_id_type=MESH,
        )

    wide = 512

    def reduce_rows(phase, far, up, down, own):
        sent = []
        share = far()
        for piece in range(2):
            opp_send[phase, piece] = share[:, piece * wide : piece * wide + wide].astype(BF16)
            copy = far_copy(phase, piece)
            copy.start()
            sent.append(copy)
        share_up, share_down = up(), down()
        side_send[phase, 0, 1] = share_up[:, wide:].astype(BF16)
        side_send[phase, 1, 0] = share_down[:, :wide].astype(BF16)
        for side, piece in ((0, 1), (1, 0)):
            copy = side_copy(phase, side, piece)
            copy.start()
            sent.append(copy)
        share_own = own()
        far_copy(phase, 0).wait_recv()
        side_send[phase, 0, 0] = (share_up[:, :wide] + opp_recv[phase, 0].astype(F32)).astype(BF16)
        copy = side_copy(phase, 0, 0)
        copy.start()
        sent.append(copy)
        far_copy(phase, 1).wait_recv()
        side_send[phase, 1, 1] = (share_down[:, wide:] + opp_recv[phase, 1].astype(F32)).astype(BF16)
        copy = side_copy(phase, 1, 1)
        copy.start()
        sent.append(copy)
        for side, piece in ((0, 1), (1, 0), (0, 0), (1, 1)):
            side_copy(phase, side, piece).wait_recv()
        halves = [
            share_own[:, piece * wide : piece * wide + wide]
            + side_recv[phase, 0, piece].astype(F32)
            + side_recv[phase, 1, piece].astype(F32)
            for piece in range(2)
        ]
        return jnp.concatenate(halves, axis=1), sent

    total, sent_one = reduce_rows(
        0,
        lambda: out_part(y_far),
        lambda: out_part(y_up),
        lambda: out_part(y_down),
        lambda: out_part(y),
    )
    own_rows = pl.ds(pl.multiple_of(core * half + y * part, 16), part)
    one = norm_rows(tokens[own_rows, :].astype(F32) + total, gain_one_ref[...]).astype(BF16)
    for piece in range(2):
        hidden[y, piece] = one[:, piece * wide : piece * wide + wide]

    def hidden_copy(side, hop, piece):
        block = y if hop == 0 else (y_up if side else y_down)
        return pltpu.make_async_remote_copy(
            src_ref=hidden.at[block, piece],
            dst_ref=hidden.at[block, piece],
            send_sem=hid_send_sem.at[side, hop, piece],
            recv_sem=hid_recv_sem.at[side, hop, piece],
            device_id=at_y(y_down if side else y_up),
            device_id_type=MESH,
        )

    sent_two = []

    def send_hidden(side, hop, piece):
        copy = hidden_copy(side, hop, piece)
        copy.start()
        sent_two.append(copy)

    send_hidden(0, 0, 0)
    send_hidden(1, 0, 1)
    send_hidden(0, 0, 1)
    send_hidden(1, 0, 0)
    for i in (6, 7):
        loads[i].wait()
    swaps[1].wait_recv()
    swaps[2].wait_recv()

    def feed(other):
        rows = jnp.concatenate([hidden[other, 0], hidden[other, 1]], axis=1)
        made = None
        for i in range(2):
            inner = gelu(jnp.dot(rows, w_up[i], preferred_element_type=F32)).astype(BF16)
            term = jnp.dot(inner, w_down[i], preferred_element_type=F32)
            made = term if made is None else made + term
        return made

    feed_own = feed(y)
    hidden_copy(0, 0, 0).wait_recv()
    send_hidden(0, 1, 0)
    hidden_copy(1, 0, 1).wait_recv()
    send_hidden(1, 1, 1)
    hidden_copy(0, 0, 1).wait_recv()
    hidden_copy(1, 0, 0).wait_recv()
    feed_up, feed_down = feed(y_up), feed(y_down)
    hidden_copy(0, 1, 0).wait_recv()
    hidden_copy(1, 1, 1).wait_recv()
    total_two, sent_three = reduce_rows(
        1, lambda: feed(y_far), lambda: feed_up, lambda: feed_down, lambda: feed_own
    )
    two = norm_rows(one.astype(F32) + total_two, gain_two_ref[...]).astype(BF16)
    projected = jnp.dot(two, w_proj_ref[...], preferred_element_type=F32)
    unit = projected * lax.rsqrt(jnp.sum(projected * projected, axis=-1, keepdims=True) + 1e-06)
    vectors[head] = unit.astype(BF16)

    sent_four = []
    for i, device in enumerate(peers):
        copy = pltpu.make_async_remote_copy(
            src_ref=vectors.at[head],
            dst_ref=vectors.at[head],
            send_sem=vec_send_sem.at[i],
            recv_sem=vec_recv_sem.at[i],
            device_id=device,
            device_id_type=MESH,
        )
        copy.start()
        sent_four.append(copy)
    for copy in sent_four:
        copy.wait_recv()
    for block in range(2 * NY):
        place = (block % 2) * half + (block // 2) * part
        query_out[place : place + part, :] = vectors[block]

    for copy in list(copies.values()) + swaps + [att_copy] + sent_one + sent_two + sent_three + sent_four:
        copy.wait_send()


def encode(tokens, w_qkv, w_out, w_up, w_down, gain_one, gain_two, rel_table, prompt_cache, w_proj, group_ids):
    plan = plan_gather()
    rows, width = tokens.shape
    half = rows // 2
    part = half // NY
    anywhere = pl.BlockSpec(memory_space=pl.ANY)
    vmem = pl.BlockSpec(memory_space=pltpu.VMEM)
    smem = pl.BlockSpec(memory_space=pltpu.SMEM)
    dma = pltpu.SemaphoreType.DMA
    return pl.pallas_call(
        functools.partial(encoder_kernel, plan),
        out_shape=jax.ShapeDtypeStruct((rows, 128), BF16),
        in_specs=[smem] + [anywhere] * 5 + [vmem, vmem, anywhere, anywhere, vmem],
        out_specs=vmem,
        scratch_shapes=[
            pltpu.VMEM((2, 64, PLEN, 128), BF16),
            pltpu.VMEM((rows, width), BF16),
            pltpu.VMEM((width, 384), BF16),
            pltpu.VMEM((2, 128, width), BF16),
            pltpu.VMEM((2, width, 512), BF16),
            pltpu.VMEM((2, 512, width), BF16),
            pltpu.VMEM((2, 128, width), BF16),
            pltpu.VMEM((2, rows, 128), BF16),
            pltpu.VMEM((rows, 128), BF16),
            pltpu.VMEM((rows, 128), BF16),
            pltpu.VMEM((rows, 256), F32),
            pltpu.VMEM((2, 256, 128), BF16),
            pltpu.VMEM((2, half, 128), BF16),
            pltpu.VMEM((half, 128), BF16),
            pltpu.VMEM((2, 2, part, 512), BF16),
            pltpu.VMEM((2, 2, 2, part, 512), BF16),
            pltpu.VMEM((2, 2, part, 512), BF16),
            pltpu.VMEM((2, 2, 2, part, 512), BF16),
            pltpu.VMEM((NY, 2, part, 512), BF16),
            pltpu.VMEM((2 * NY, part, 128), BF16),
            dma((8,)),
            dma((len(plan),)),
            dma((len(plan),)),
            dma((3,)),
            dma((3,)),
            dma((2,)),
            dma((2, 2)),
            dma((2, 2)),
            dma((2, 2, 2)),
            dma((2, 2, 2)),
            dma((2, 2, 2)),
            dma((2, 2, 2)),
            dma((7,)),
            dma((7,)),
        ],
        compiler_params=pltpu.CompilerParams(collective_id=0, has_side_effects=True),
        name="encoder",
    )(
        group_ids,
        tokens,
        w_qkv.reshape(width, 384),
        w_out,
        w_up,
        w_down,
        gain_one.reshape(1, -1),
        gain_two.reshape(1, -1),
        rel_table,
        prompt_cache.reshape(2, 2, PLEN, 128),
        w_proj,
    )


def slot_order(holders):
    count = holders.shape[0]
    same = holders[:, None] == holders[None, :]
    earlier = jnp.arange(count)[:, None] > jnp.arange(count)[None, :]
    return jnp.sum(same & earlier, axis=1)


def rate_slots(slot_query, slot_doc, doc_vectors, doc_lengths):
    shape = slot_doc.shape
    flat_doc = slot_doc.reshape(-1)
    flat_query = slot_query.reshape((flat_doc.shape[0],) + slot_query.shape[-2:])
    safe_doc = jnp.maximum(flat_doc, 0)
    documents = doc_vectors[safe_doc]
    lengths = doc_lengths[safe_doc]
    sims = jnp.einsum("sqe,sje->sqj", flat_query, documents, preferred_element_type=jnp.float32)
    live = jnp.arange(documents.shape[1], dtype=jnp.int32)[None, None, :] < lengths[:, None, None]
    best = jnp.max(jnp.where(live, sims, -jnp.inf), axis=2)
    totals = jnp.where(flat_doc >= 0, jnp.sum(best, axis=1), 0.0)
    return totals.reshape(shape)


def body(
    tokens,
    w_qkv,
    w_out,
    w_up,
    w_down,
    gain_one,
    gain_two,
    rel_table,
    prompt_cache,
    w_proj,
    doc_vectors,
    doc_lengths,
    group_ids,
    candidates,
):
    req_dev = tokens.shape[0] // QLEN
    query_vectors = encode(
        tokens, w_qkv, w_out, w_up, w_down, gain_one, gain_two, rel_table, prompt_cache, w_proj, group_ids
    )
    shards = lax.axis_size("doc")
    cand_dev = candidates.shape[1]
    pairs = req_dev * cand_dev
    capacity = max(2, 2 * pairs // shards)
    flat_cand = candidates.reshape(-1)
    holders = flat_cand // DOC_DEV
    request_of = jnp.arange(pairs, dtype=jnp.int32) // cand_dev
    slot_rank = slot_order(holders)
    copies, cand_copies = (
        lax.all_gather(query_vectors, "doc", axis=0, tiled=True),
        lax.all_gather(candidates, "doc", axis=0, tiled=True),
    )
    all_query = copies.reshape(shards, req_dev, QLEN, copies.shape[1])
    all_cand = cand_copies.reshape(shards, pairs)
    holder_all = all_cand // DOC_DEV
    local_all = all_cand % DOC_DEV
    rank_all = jax.vmap(slot_order)(holder_all)
    own_index = lax.axis_index("doc")
    chosen = (holder_all[:, None, :] == own_index) & (
        rank_all[:, None, :] == jnp.arange(capacity, dtype=jnp.int32)[None, :, None]
    )
    filled = jnp.any(chosen, axis=2)
    slot_request = jnp.sum(jnp.where(chosen, request_of[None, None, :], 0), axis=2)
    slot_doc = jnp.where(
        filled, jnp.sum(jnp.where(chosen, local_all[:, None, :], 0), axis=2), -1
    ).astype(jnp.int32)
    slot_query = all_query[jnp.arange(shards)[:, None], slot_request]
    slot_scores = rate_slots(slot_query, slot_doc, doc_vectors, doc_lengths)
    returned = lax.all_to_all(slot_scores, "doc", split_axis=0, concat_axis=0, tiled=True)
    scores = returned.reshape(-1)[holders * capacity + slot_rank].reshape(candidates.shape)
    return (query_vectors, scores)


def solution(mesh):
    placed = (
        P("doc", None),
        P(None, None, "head"),
        P("head", None),
        P(None, "head"),
        P("head", None),
        P(),
        P(),
        P(),
        P(None, "doc", "head"),
        P(),
        P("doc", None, None),
        P("doc"),
        P("doc"),
        P("doc", "head"),
    )
    return jax.shard_map(
        body,
        mesh=mesh,
        in_specs=placed,
        out_specs=(P("doc", None), P("doc", "head")),
        check_vma=False,
    )
```

```python
import functools
import math

import jax
import jax.numpy as jnp
from jax import lax
from jax.experimental import pallas as pl
from jax.experimental.pallas import tpu as pltpu
from jax.sharding import PartitionSpec as P

HD = 64
RELS = 512
QLEN = 32
PLEN = 64
DOC_DEV = 64
NX = 4
NZ = 8
NY = 4
SLOTS = 6
MESH = pl.DeviceIdType.MESH
F32 = jnp.float32
BF16 = jnp.bfloat16
NT = (((1,), (1,)), ((), ()))


def mod(value, size):
    return lax.rem(value + 4 * size, size)


class Message:
    def __init__(self, kv, axis, sign, dx, dz, low, rows, parent):
        self.kv, self.axis, self.sign, self.dx, self.dz = kv, axis, sign, dx, dz
        self.low, self.rows, self.parent = low, rows, parent
        self.children = []
        self.time = None
        self.index = None


def plan_gather():
    made = []

    def add(kv, axis, sign, dx, dz, low, rows, parent):
        message = Message(kv, axis, sign, dx, dz, low, rows, parent)
        made.append(message)
        return message

    def along_x(kv, dz, low, rows, parent):
        out = []
        for sign in (1, -1):
            near = add(kv, "x", sign, sign, dz, low, rows, parent)
            half = rows // 2
            far = add(kv, "x", sign, 2 * sign, dz, low if sign > 0 else low + half, half, near)
            out += [near, far]
        return out

    def along_z(kv, dx, low, rows, parent):
        out = []
        for sign in (1, -1):
            previous = parent
            for step in range(1, 4):
                previous = add(kv, "z", sign, dx, sign * step, low, rows, previous)
                out.append(previous)
            half = rows // 2
            out.append(add(kv, "z", sign, dx, sign * 4, low if sign > 0 else low + half, half, previous))
        return out

    firsts = along_z(0, 0, 0, 128, None)
    along_x(0, 0, 0, 128, None)
    for first in firsts:
        along_x(0, first.dz, first.low, first.rows, first)
    firsts = along_x(1, 0, 0, 128, None)
    along_z(1, 0, 0, 128, None)
    for first in firsts:
        along_z(1, first.dx, first.low, first.rows, first)
    for message in made:
        if message.parent is not None:
            message.parent.children.append(message)
    free = {}
    ready = [(0.0, i) for i, m in enumerate(made) if m.parent is None]
    while ready:
        ready.sort()
        start, i = ready.pop(0)
        message = made[i]
        link = (message.axis, message.sign)
        begin = max(start, free.get(link, 0.0))
        free[link] = begin + message.rows * 256 / 46500.0
        message.time = free[link] + 1.6
        ready += [(message.time, made.index(child)) for child in message.children]
    order = sorted(made, key=lambda m: m.time)
    for index, message in enumerate(order):
        message.index = index
    return order


def norm_rows(values, gain):
    centre = values - jnp.mean(values, axis=-1, keepdims=True)
    spread = jnp.mean(centre * centre, axis=-1, keepdims=True)
    return centre * lax.rsqrt(spread + 1e-07) * gain


def gelu(values):
    return 0.5 * values * (1.0 + lax.erf(values * (1.0 / math.sqrt(2.0))))


def encoder_kernel(
    plan,
    group_ref,
    tokens_hbm,
    w_qkv_hbm,
    w_out_hbm,
    w_up_hbm,
    w_down_hbm,
    gain_one_ref,
    gain_two_ref,
    rel_hbm,
    cache_hbm,
    w_proj_ref,
    docs_hbm,
    lengths_ref,
    cand_hbm,
    query_out,
    score_out,
    cache,
    tokens,
    w_qkv,
    w_out,
    w_up,
    w_down,
    rel,
    q_mask,
    k_own,
    v_own,
    q_rel,
    rel_two,
    att,
    att_send,
    opp_send,
    side_send,
    opp_recv,
    side_recv,
    hidden,
    vectors,
    load_sem,
    gather_send,
    gather_recv,
    swap_send,
    swap_recv,
    att_sem,
    opp_send_sem,
    opp_recv_sem,
    side_send_sem,
    side_recv_sem,
    hid_send_sem,
    hid_recv_sem,
    vec_send_sem,
    vec_recv_sem,
    docs,
    queries,
    cand_rows,
    table,
    table_smem,
    best_rows,
    back_send,
    back_recv,
    table_sem,
    cand_send_sem,
    cand_recv_sem,
    spread_send_sem,
    spread_recv_sem,
    across_send_sem,
    across_recv_sem,
    share_send_sem,
    share_recv_sem,
    back_send_sem,
    back_recv_sem,
):
    head = lax.axis_index("head")
    doc = lax.axis_index("doc")
    y, core = lax.div(head, 2), lax.rem(head, 2)
    x, z = lax.div(doc, NZ), lax.rem(doc, NZ)
    partner = (2 * y + 1 - core, doc)
    y_up, y_down = mod(y + 1, NY), mod(y - 1, NY)
    y_far = mod(y + 2, NY)

    def at_y(other):
        return (2 * other + core, doc)

    def at_link(axis, sign):
        if axis == "x":
            return (head, mod(x + sign, NX) * NZ + z)
        return (head, x * NZ + mod(z + sign, NZ))

    peers = [partner]
    for other in (y_up, y_down, y_far):
        peers += [(2 * other + core, doc), (2 * other + 1 - core, doc)]
    links = [at_link(axis, sign) for axis in ("x", "z") for sign in (1, -1)]
    barrier = pltpu.get_barrier_semaphore()
    for device in peers + links:
        pl.semaphore_signal(barrier, inc=1, device_id=device, device_id_type=MESH)

    loads = [
        pltpu.make_async_copy(tokens_hbm, tokens, load_sem.at[0]),
        pltpu.make_async_copy(w_qkv_hbm, w_qkv, load_sem.at[1]),
        pltpu.make_async_copy(rel_hbm.at[pl.ds(RELS // 2 - 96, 128)], rel.at[0], load_sem.at[2]),
        pltpu.make_async_copy(rel_hbm.at[pl.ds(RELS // 2 - 32, 128)], rel.at[1], load_sem.at[3]),
        pltpu.make_async_copy(
            cache_hbm, cache.at[:, pl.ds(doc * 2, 2)], load_sem.at[4]
        ),
        pltpu.make_async_copy(w_out_hbm, w_out.at[core], load_sem.at[5]),
        pltpu.make_async_copy(w_up_hbm, w_up.at[core], load_sem.at[6]),
        pltpu.make_async_copy(w_down_hbm, w_down.at[core], load_sem.at[7]),
        pltpu.make_async_copy(docs_hbm, docs, load_sem.at[8]),
    ]
    for load in loads:
        load.start()
    pl.semaphore_wait(barrier, len(peers) + len(links))

    def gather_copy(message):
        dx, dz = message.dx, message.dz
        if message.axis == "x":
            dx -= message.sign
        else:
            dz -= message.sign
        block = mod(x - dx, NX) * NZ + mod(z - dz, NZ)
        group, low = block * 2 + message.low // PLEN, message.low % PLEN
        if message.rows == 2 * PLEN:
            target = cache.at[message.kv, pl.ds(group, 2)]
        else:
            target = cache.at[message.kv, group, pl.ds(low, message.rows)]
        source = cache_hbm.at[message.kv] if message.parent is None else target
        return pltpu.make_async_remote_copy(
            src_ref=source,
            dst_ref=target,
            send_sem=gather_send.at[message.index],
            recv_sem=gather_recv.at[message.index],
            device_id=at_link(message.axis, message.sign),
            device_id_type=MESH,
        )

    copies = {message.index: gather_copy(message) for message in plan}
    for message in plan:
        if message.parent is None:
            copies[message.index].start()

    swaps = []
    for i, (source, target) in enumerate(((w_out_hbm, w_out), (w_up_hbm, w_up), (w_down_hbm, w_down))):
        swaps.append(
            pltpu.make_async_remote_copy(
                src_ref=source,
                dst_ref=target.at[core],
                send_sem=swap_send.at[i],
                recv_sem=swap_recv.at[i],
                device_id=partner,
                device_id_type=MESH,
            )
        )
        swaps[-1].start()

    loads[0].wait()
    loads[1].wait()
    low_head = lax.broadcasted_iota(jnp.int32, (128, 128), 1) < HD
    for block in range(3):
        rows = slice(block * 128, block * 128 + 128)
        made = jnp.dot(tokens[rows, :], w_qkv[...], preferred_element_type=F32)
        q_made = made[:, :128]
        q_mask[0, rows, :] = jnp.where(low_head, q_made, 0.0).astype(BF16)
        q_mask[1, rows, :] = jnp.where(low_head, 0.0, q_made).astype(BF16)
        k_own[rows, :] = made[:, 128:256].astype(BF16)
        v_own[rows, :] = made[:, 256:].astype(BF16)
    loads[2].wait()
    loads[3].wait()
    flip = (
        lax.broadcasted_iota(jnp.int32, (128, 128), 0) + lax.broadcasted_iota(jnp.int32, (128, 128), 1)
        == 127
    ).astype(F32).astype(BF16)
    for i in range(2):
        row = jnp.dot(
            rel[i], w_qkv[:, i * 128 : i * 128 + 128], preferred_element_type=F32
        ).astype(BF16)
        turned = jnp.dot(flip, row, preferred_element_type=F32)
        rel_two[i, 0:128, :] = jnp.where(low_head, turned, 0.0).astype(BF16)
        rel_two[i, 128:256, :] = jnp.where(low_head, 0.0, turned).astype(BF16)
    for block in range(3):
        rows = slice(block * 128, block * 128 + 128)
        q_all = q_mask[0, rows, :] + q_mask[1, rows, :]
        q_rel[rows, :] = lax.dot_general(q_all, rel_two[1], NT, preferred_element_type=F32)
    loads[4].wait()

    for message in plan:
        copies[message.index].wait_recv()
        for child in message.children:
            copies[child.index].start()

    low_lane = lax.broadcasted_iota(jnp.int32, (96, 128), 1) < QLEN
    low_half = lax.broadcasted_iota(jnp.int32, (QLEN, 128), 1) < HD

    def attend(request):
        group = group_ref[request]
        own = pl.ds(pl.multiple_of(request * QLEN, QLEN), QLEN)
        keys = jnp.concatenate([cache[0, group], k_own[own, :]], axis=0)
        values = jnp.concatenate([cache[1, group], v_own[own, :]], axis=0)
        query = jnp.concatenate([q_mask[0, own, :], q_mask[1, own, :]], axis=0)
        content = lax.dot_general(query, keys, NT, preferred_element_type=F32)
        key_rel = lax.dot_general(keys, rel_two[0], NT, preferred_element_type=F32)
        first = pltpu.roll(key_rel[:, :128], 33, 1, stride=1, stride_axis=0)
        second = pltpu.roll(key_rel[:, 128:], 65, 1, stride=1, stride_axis=0)
        p2c = jnp.transpose(jnp.where(low_lane, first, second))[: 2 * QLEN, :]
        mine = q_rel[own, :]
        c2p = jnp.concatenate(
            [
                pltpu.roll(mine[:, :128], 97, 1, stride=1, stride_axis=0),
                pltpu.roll(mine[:, 128:], 97, 1, stride=1, stride_axis=0),
            ],
            axis=0,
        )[:, :96]
        logits = (content + c2p + p2c) * (1.0 / math.sqrt(3 * HD))
        weights = jnp.exp(logits - jnp.max(logits, axis=-1, keepdims=True))
        total = jnp.sum(weights, axis=-1, keepdims=True)
        out = jnp.dot(weights.astype(BF16), values, preferred_element_type=F32) / total
        return jnp.where(low_half, out[:QLEN], out[QLEN:]).astype(BF16)

    half = tokens.shape[0] // 2
    per_core = half // QLEN
    for i in range(per_core):
        att_send[i * QLEN : i * QLEN + QLEN, :] = attend((1 - core) * per_core + i)
    att_copy = pltpu.make_async_remote_copy(
        src_ref=att_send,
        dst_ref=att.at[core],
        send_sem=att_sem.at[0],
        recv_sem=att_sem.at[1],
        device_id=partner,
        device_id_type=MESH,
    )
    att_copy.start()
    for i in range(per_core):
        att[core, i * QLEN : i * QLEN + QLEN, :] = attend(core * per_core + i)
    att_copy.wait_recv()
    loads[5].wait()
    swaps[0].wait_recv()
    part = half // NY

    def chunk_rows(other):
        return pl.ds(pl.multiple_of(other * part, 16), part)

    def out_part(other):
        rows = chunk_rows(other)
        return jnp.dot(att[0, rows, :], w_out[0], preferred_element_type=F32) + jnp.dot(
            att[1, rows, :], w_out[1], preferred_element_type=F32
        )

    def side_copy(phase, side, piece):
        return pltpu.make_async_remote_copy(
            src_ref=side_send.at[phase, side, piece],
            dst_ref=side_recv.at[phase, side, piece],
            send_sem=side_send_sem.at[phase, side, piece],
            recv_sem=side_recv_sem.at[phase, side, piece],
            device_id=at_y(y_down if side else y_up),
            device_id_type=MESH,
        )

    def far_copy(phase, piece):
        return pltpu.make_async_remote_copy(
            src_ref=opp_send.at[phase, piece],
            dst_ref=opp_recv.at[phase, piece],
            send_sem=opp_send_sem.at[phase, piece],
            recv_sem=opp_recv_sem.at[phase, piece],
            device_id=at_y(y_down if piece else y_up),
            device_id_type=MESH,
        )

    wide = 512

    def reduce_rows(phase, far, up, down, own):
        sent = []
        share = far()
        for piece in range(2):
            opp_send[phase, piece] = share[:, piece * wide : piece * wide + wide].astype(BF16)
            copy = far_copy(phase, piece)
            copy.start()
            sent.append(copy)
        share_up, share_down = up(), down()
        side_send[phase, 0, 1] = share_up[:, wide:].astype(BF16)
        side_send[phase, 1, 0] = share_down[:, :wide].astype(BF16)
        for side, piece in ((0, 1), (1, 0)):
            copy = side_copy(phase, side, piece)
            copy.start()
            sent.append(copy)
        share_own = own()
        far_copy(phase, 0).wait_recv()
        side_send[phase, 0, 0] = (share_up[:, :wide] + opp_recv[phase, 0].astype(F32)).astype(BF16)
        copy = side_copy(phase, 0, 0)
        copy.start()
        sent.append(copy)
        far_copy(phase, 1).wait_recv()
        side_send[phase, 1, 1] = (share_down[:, wide:] + opp_recv[phase, 1].astype(F32)).astype(BF16)
        copy = side_copy(phase, 1, 1)
        copy.start()
        sent.append(copy)
        for side, piece in ((0, 1), (1, 0), (0, 0), (1, 1)):
            side_copy(phase, side, piece).wait_recv()
        halves = [
            share_own[:, piece * wide : piece * wide + wide]
            + side_recv[phase, 0, piece].astype(F32)
            + side_recv[phase, 1, piece].astype(F32)
            for piece in range(2)
        ]
        return jnp.concatenate(halves, axis=1), sent

    total, sent_one = reduce_rows(
        0,
        lambda: out_part(y_far),
        lambda: out_part(y_up),
        lambda: out_part(y_down),
        lambda: out_part(y),
    )
    own_rows = pl.ds(pl.multiple_of(core * half + y * part, 16), part)
    one = norm_rows(tokens[own_rows, :].astype(F32) + total, gain_one_ref[...]).astype(BF16)
    for piece in range(2):
        hidden[y, piece] = one[:, piece * wide : piece * wide + wide]

    def hidden_copy(side, hop, piece):
        block = y if hop == 0 else (y_up if side else y_down)
        return pltpu.make_async_remote_copy(
            src_ref=hidden.at[block, piece],
            dst_ref=hidden.at[block, piece],
            send_sem=hid_send_sem.at[side, hop, piece],
            recv_sem=hid_recv_sem.at[side, hop, piece],
            device_id=at_y(y_down if side else y_up),
            device_id_type=MESH,
        )

    sent_two = []

    def send_hidden(side, hop, piece):
        copy = hidden_copy(side, hop, piece)
        copy.start()
        sent_two.append(copy)

    send_hidden(0, 0, 0)
    send_hidden(1, 0, 1)
    send_hidden(0, 0, 1)
    send_hidden(1, 0, 0)
    home = mod(x + z, NY)
    at_home = home == y
    my_row = (x * 2 + lax.div(z, 4)) * NY + y

    def cand_copy(offset):
        return pltpu.make_async_remote_copy(
            src_ref=cand_hbm,
            dst_ref=cand_rows.at[my_row],
            send_sem=cand_send_sem.at[offset],
            recv_sem=cand_recv_sem.at[my_row],
            device_id=(2 * home + core, mod(doc + offset, NX * NZ)),
            device_id_type=MESH,
        )

    cand_local = pltpu.make_async_copy(cand_hbm, cand_rows.at[my_row], cand_recv_sem.at[my_row])
    pl.when(at_home)(lambda: cand_local.start())
    pl.when(jnp.logical_not(at_home))(lambda: cand_copy(0).start())
    pl.loop(1, NX * NZ)(lambda offset: cand_copy(offset).start())
    for i in (6, 7):
        loads[i].wait()
    swaps[1].wait_recv()
    swaps[2].wait_recv()

    def feed(other):
        rows = jnp.concatenate([hidden[other, 0], hidden[other, 1]], axis=1)
        made = None
        for i in range(2):
            inner = gelu(jnp.dot(rows, w_up[i], preferred_element_type=F32)).astype(BF16)
            term = jnp.dot(inner, w_down[i], preferred_element_type=F32)
            made = term if made is None else made + term
        return made

    feed_own = feed(y)
    hidden_copy(0, 0, 0).wait_recv()
    send_hidden(0, 1, 0)
    hidden_copy(1, 0, 1).wait_recv()
    send_hidden(1, 1, 1)
    hidden_copy(0, 0, 1).wait_recv()
    hidden_copy(1, 0, 0).wait_recv()
    feed_up, feed_down = feed(y_up), feed(y_down)
    @pl.loop(0, NX * NZ)
    def _(row):
        pltpu.make_async_copy(cand_hbm, cand_rows.at[row], cand_recv_sem.at[row]).wait()

    lane = lax.broadcasted_iota(jnp.int32, (NX * NZ, 128), 1)
    named = cand_rows[...].reshape(NX * NZ, 128)
    mine = jnp.logical_and(lax.shift_right_logical(named, 6) == doc, lane < 96)
    mine_f = jnp.where(mine, 1.0, 0.0)
    before = (
        lax.broadcasted_iota(jnp.int32, (128, 128), 0) < lax.broadcasted_iota(jnp.int32, (128, 128), 1)
    ).astype(F32).astype(BF16)
    rank = jnp.dot(mine_f.astype(BF16), before, preferred_element_type=F32)
    rows_table = jnp.zeros((NX * NZ, 128), jnp.int32)
    places = []
    for slot in range(SLOTS):
        chosen = jnp.where(rank == float(slot), mine_f, 0.0)
        some = jnp.sum(chosen, axis=1, keepdims=True)
        place = jnp.sum(chosen * lane.astype(F32), axis=1, keepdims=True).astype(jnp.int32)
        which = jnp.sum(
            chosen * lax.bitwise_and(named, DOC_DEV - 1).astype(F32), axis=1, keepdims=True
        ).astype(jnp.int32)
        places.append(jnp.where(some > 0.5, place, 127))
        rows_table = jnp.where(lane == slot, lax.shift_right_logical(place, 3) * 2, rows_table)
        rows_table = jnp.where(lane == slot + 8, which, rows_table)
    table[...] = rows_table
    table_copy = pltpu.make_async_copy(table, table_smem, table_sem.at[0])
    table_copy.start()
    hidden_copy(0, 1, 0).wait_recv()
    hidden_copy(1, 1, 1).wait_recv()
    total_two, sent_three = reduce_rows(
        1, lambda: feed(y_far), lambda: feed_up, lambda: feed_down, lambda: feed_own
    )
    two = norm_rows(one.astype(F32) + total_two, gain_two_ref[...]).astype(BF16)
    projected = jnp.dot(two, w_proj_ref[...], preferred_element_type=F32)
    unit = projected * lax.rsqrt(jnp.sum(projected * projected, axis=-1, keepdims=True) + 1e-06)
    vectors[head] = unit.astype(BF16).reshape(3, 16, 128)

    sent_four = []
    for i, device in enumerate(peers):
        copy = pltpu.make_async_remote_copy(
            src_ref=vectors.at[head],
            dst_ref=vectors.at[head],
            send_sem=vec_send_sem.at[i],
            recv_sem=vec_recv_sem.at[i],
            device_id=device,
            device_id_type=MESH,
        )
        copy.start()
        sent_four.append(copy)
    half_doc = lax.div(z, 4)
    piece_rows = pl.ds(core * 12 + y * 3, 3)

    def spread_copy(offset):
        return pltpu.make_async_remote_copy(
            src_ref=vectors.at[head],
            dst_ref=queries.at[x * 2 + half_doc, piece_rows],
            send_sem=spread_send_sem.at[offset],
            recv_sem=spread_recv_sem.at[half_doc, y],
            device_id=(2 * home + core, x * NZ + mod(z + offset, NZ)),
            device_id_type=MESH,
        )

    def across_copy(half_index, source_y, offset, index):
        rows = queries.at[index, pl.ds(core * 12 + source_y * 3, 3)]
        return pltpu.make_async_remote_copy(
            src_ref=rows,
            dst_ref=rows,
            send_sem=across_send_sem.at[half_index, source_y, offset - 1],
            recv_sem=across_recv_sem.at[half_index, source_y, offset - 1],
            device_id=(head, mod(x + offset, NX) * NZ + z),
            device_id_type=MESH,
        )

    def share_copy(place, index):
        rows = queries.at[index, pl.ds(core * 12, 12)]
        return pltpu.make_async_remote_copy(
            src_ref=rows,
            dst_ref=rows,
            send_sem=share_send_sem.at[place],
            recv_sem=share_recv_sem.at[place],
            device_id=partner,
            device_id_type=MESH,
        )

    spread_local = pltpu.make_async_copy(
        vectors.at[head], queries.at[x * 2 + half_doc, piece_rows], spread_recv_sem.at[half_doc, y]
    )
    pl.when(at_home)(lambda: spread_local.start())
    pl.when(jnp.logical_not(at_home))(lambda: spread_copy(0).start())
    for offset in (4, 3, 5, 2, 6, 1, 7):
        spread_copy(offset).start()
    crossing = []
    shared = []
    for source_y in range(NY):
        for half_index in range(2):
            pltpu.make_async_copy(
                vectors.at[head],
                queries.at[x * 2 + half_index, pl.ds(core * 12 + source_y * 3, 3)],
                spread_recv_sem.at[half_index, source_y],
            ).wait()
            for offset in (2, 1, 3):
                crossing.append(across_copy(half_index, source_y, offset, x * 2 + half_index))
                crossing[-1].start()
    for half_index in range(2):
        shared.append(share_copy(half_index, x * 2 + half_index))
        shared[-1].start()
    for copy in sent_four:
        copy.wait_recv()
    for block in range(2 * NY):
        place = (block % 2) * half + (block // 2) * part
        query_out[place : place + part, :] = vectors[block].reshape(part, 128)
    for offset in (1, 3, 2):
        for half_index in range(2):
            index = mod(x - offset, NX) * 2 + half_index
            for source_y in range(NY):
                across_copy(half_index, source_y, offset, index).wait_recv()
            shared.append(share_copy(2 * offset + half_index, index))
            shared[-1].start()
    table_copy.wait()
    loads[8].wait()
    for copy in shared:
        copy.wait_recv()

    zeros = jnp.zeros((QLEN, 128), BF16)
    row_index = lax.broadcasted_iota(jnp.int32, (256, 2 * QLEN), 0)
    first_lanes = lax.broadcasted_iota(jnp.int32, (1, 2 * QLEN), 1) < QLEN

    @pl.loop(0, NX * NZ)
    def _(row):
        source = lax.div(row, NY)
        for pair in range(SLOTS // 2):
            found = []
            for slot in (2 * pair, 2 * pair + 1):
                which = jnp.clip(table_smem[row, slot + 8], 0, DOC_DEV - 1)
                request = jnp.clip(table_smem[row, slot], 0, 22)
                query = jnp.concatenate([queries[source, request], queries[source, request + 1]], axis=0)
                found.append((docs[which], query, lengths_ref[which]))
            (doc_a, query_a, len_a), (doc_b, query_b, len_b) = found
            left = jnp.concatenate([doc_a, doc_b], axis=1)
            right = jnp.concatenate(
                [
                    jnp.concatenate([query_a, zeros], axis=1),
                    jnp.concatenate([zeros, query_b], axis=1),
                ],
                axis=0,
            )
            sims = lax.dot_general(left, right, NT, preferred_element_type=F32)
            live = row_index < jnp.where(first_lanes, len_a, len_b)
            best_rows[pair, pl.ds(row, 1), : 2 * QLEN] = jnp.max(
                jnp.where(live, sims, -jnp.inf), axis=0, keepdims=True
            )

    rated = jnp.zeros((NX * NZ, 128), F32)
    for slot in range(SLOTS):
        low = (slot % 2) * QLEN
        value = jnp.sum(best_rows[slot // 2][:, low : low + QLEN], axis=1, keepdims=True)
        rated = rated + jnp.where(lane == places[slot], value, 0.0)
    back_send[...] = rated.reshape(NX * NZ, 1, 128)

    def back_to(row):
        source_x, source_half, source_y = lax.div(row, 8), lax.rem(lax.div(row, NY), 2), lax.rem(row, NY)
        source = source_x * NZ + mod(y - source_x, NY) + 4 * source_half
        return source, source_y

    def back_copy(row):
        source, source_y = back_to(row)
        return pltpu.make_async_remote_copy(
            src_ref=back_send.at[row],
            dst_ref=back_recv.at[doc],
            send_sem=back_send_sem.at[row],
            recv_sem=back_recv_sem.at[doc],
            device_id=(2 * source_y + core, source),
            device_id_type=MESH,
        )

    def is_own(row):
        source, source_y = back_to(row)
        return jnp.logical_and(source == doc, source_y == y)

    @pl.loop(0, NX * NZ)
    def _(row):
        own_row = is_own(row)
        pl.when(own_row)(
            lambda: pltpu.make_async_copy(
                back_send.at[row], back_recv.at[doc], back_recv_sem.at[doc]
            ).start()
        )
        pl.when(jnp.logical_not(own_row))(lambda: back_copy(row).start())

    @pl.loop(0, NX * NZ)
    def _(row):
        pltpu.make_async_copy(back_send.at[0], back_recv.at[row], back_recv_sem.at[row]).wait()

    score_out[...] = jnp.sum(back_recv[...], axis=0)

    @pl.loop(0, NX * NZ)
    def _(row):
        pl.when(jnp.logical_not(is_own(row)))(lambda: back_copy(row).wait_send())

    pl.when(jnp.logical_not(at_home))(lambda: cand_copy(0).wait_send())
    pl.loop(1, NX * NZ)(lambda offset: cand_copy(offset).wait_send())
    pl.when(jnp.logical_not(at_home))(lambda: spread_copy(0).wait_send())
    for offset in range(1, NZ):
        spread_copy(offset).wait_send()
    for copy in list(copies.values()) + swaps + [att_copy] + sent_one + sent_two + sent_three + sent_four + crossing + shared:
        copy.wait_send()


def encode(tokens, w_qkv, w_out, w_up, w_down, gain_one, gain_two, rel_table, prompt_cache, w_proj, docs, lengths, named, group_ids):
    plan = plan_gather()
    rows, width = tokens.shape
    half = rows // 2
    part = half // NY
    anywhere = pl.BlockSpec(memory_space=pl.ANY)
    vmem = pl.BlockSpec(memory_space=pltpu.VMEM)
    smem = pl.BlockSpec(memory_space=pltpu.SMEM)
    dma = pltpu.SemaphoreType.DMA
    return pl.pallas_call(
        functools.partial(encoder_kernel, plan),
        out_shape=(jax.ShapeDtypeStruct((rows, 128), BF16), jax.ShapeDtypeStruct((1, 128), F32)),
        in_specs=[smem] + [anywhere] * 5 + [vmem, vmem, anywhere, anywhere, vmem, anywhere, smem, anywhere],
        out_specs=(vmem, vmem),
        scratch_shapes=[
            pltpu.VMEM((2, 64, PLEN, 128), BF16),
            pltpu.VMEM((rows, width), BF16),
            pltpu.VMEM((width, 384), BF16),
            pltpu.VMEM((2, 128, width), BF16),
            pltpu.VMEM((2, width, 512), BF16),
            pltpu.VMEM((2, 512, width), BF16),
            pltpu.VMEM((2, 128, width), BF16),
            pltpu.VMEM((2, rows, 128), BF16),
            pltpu.VMEM((rows, 128), BF16),
            pltpu.VMEM((rows, 128), BF16),
            pltpu.VMEM((rows, 256), F32),
            pltpu.VMEM((2, 256, 128), BF16),
            pltpu.VMEM((2, half, 128), BF16),
            pltpu.VMEM((half, 128), BF16),
            pltpu.VMEM((2, 2, part, 512), BF16),
            pltpu.VMEM((2, 2, 2, part, 512), BF16),
            pltpu.VMEM((2, 2, part, 512), BF16),
            pltpu.VMEM((2, 2, 2, part, 512), BF16),
            pltpu.VMEM((NY, 2, part, 512), BF16),
            pltpu.VMEM((2 * NY, 3, 16, 128), BF16),
            dma((9,)),
            dma((len(plan),)),
            dma((len(plan),)),
            dma((3,)),
            dma((3,)),
            dma((2,)),
            dma((2, 2)),
            dma((2, 2)),
            dma((2, 2, 2)),
            dma((2, 2, 2)),
            dma((2, 2, 2)),
            dma((2, 2, 2)),
            dma((7,)),
            dma((7,)),
            pltpu.VMEM((64, 256, 128), BF16),
            pltpu.VMEM((8, 24, 16, 128), BF16),
            pltpu.VMEM((32, 1, 128), jnp.int32),
            pltpu.VMEM((32, 128), jnp.int32),
            pltpu.SMEM((32, 128), jnp.int32),
            pltpu.VMEM((SLOTS // 2, 32, 128), F32),
            pltpu.VMEM((32, 1, 128), F32),
            pltpu.VMEM((32, 1, 128), F32),
            dma((1,)),
            dma((32,)),
            dma((32,)),
            dma((8,)),
            dma((2, 4)),
            dma((2, 4, 3)),
            dma((2, 4, 3)),
            dma((8,)),
            dma((8,)),
            dma((32,)),
            dma((32,)),
        ],
        compiler_params=pltpu.CompilerParams(collective_id=0, has_side_effects=True),
        name="encoder",
    )(
        group_ids,
        tokens,
        w_qkv.reshape(width, 384),
        w_out,
        w_up,
        w_down,
        gain_one.reshape(1, -1),
        gain_two.reshape(1, -1),
        rel_table,
        prompt_cache.reshape(2, 2, PLEN, 128),
        w_proj,
        docs,
        lengths,
        named,
    )


def body(
    tokens,
    w_qkv,
    w_out,
    w_up,
    w_down,
    gain_one,
    gain_two,
    rel_table,
    prompt_cache,
    w_proj,
    doc_vectors,
    doc_lengths,
    group_ids,
    candidates,
):
    named = jnp.pad(candidates.reshape(1, -1), ((0, 0), (0, 128 - candidates.size)), constant_values=-1)
    query_vectors, rated = encode(
        tokens,
        w_qkv,
        w_out,
        w_up,
        w_down,
        gain_one,
        gain_two,
        rel_table,
        prompt_cache,
        w_proj,
        doc_vectors,
        doc_lengths,
        named,
        group_ids,
    )
    return (query_vectors, rated[0, : candidates.size].reshape(candidates.shape))


def solution(mesh):
    placed = (
        P("doc", None),
        P(None, None, "head"),
        P("head", None),
        P(None, "head"),
        P("head", None),
        P(),
        P(),
        P(),
        P(None, "doc", "head"),
        P(),
        P("doc", None, None),
        P("doc"),
        P("doc"),
        P("doc", "head"),
    )
    return jax.shard_map(
        body,
        mesh=mesh,
        in_specs=placed,
        out_specs=(P("doc", None), P("doc", "head")),
        check_vma=False,
    )
```

```python
import functools
import math

import jax
import jax.numpy as jnp
from jax import lax
from jax.experimental import pallas as pl
from jax.experimental.pallas import tpu as pltpu
from jax.sharding import PartitionSpec as P

HD = 64
RELS = 512
QLEN = 32
PLEN = 64
DOC_DEV = 64
NX = 4
NZ = 8
NY = 4
SLOTS = 6
ROWS = 4
MESH = pl.DeviceIdType.MESH
F32 = jnp.float32
BF16 = jnp.bfloat16
NT = (((1,), (1,)), ((), ()))


def mod(value, size):
    return lax.rem(value + 4 * size, size)


HOP_US = 2.3
ROUTE_US = 0.65
ROWS_US = 256 / 46500.0
Z_FIRST = ((0, 0, 128),)
X_FIRST = ((1, 0, 128),)


class Message:
    def __init__(self, kv, axis, sign, hops, dx, dz, low, rows, parent):
        self.kv, self.axis, self.sign, self.hops = kv, axis, sign, hops
        self.dx, self.dz, self.low, self.rows, self.parent = dx, dz, low, rows, parent
        self.children = []
        self.time = None
        self.index = None


def plan_gather():
    made = []

    def add(*fields):
        made.append(Message(*fields))
        return made[-1]

    def along_x(kv, dz, low, rows, parent, direct):
        out = []
        half = rows // 2
        for sign in (1, -1):
            near = add(kv, "x", sign, 1, sign, dz, low, rows, parent)
            part = low if sign > 0 else low + half
            hops = 2 if direct else 1
            out += [near, add(kv, "x", sign, hops, 2 * sign, dz, part, half, parent if direct else near)]
        return out

    def along_z(kv, dx, low, rows, parent, jump):
        out = []
        half = rows // 2
        for sign in (1, -1):
            one = add(kv, "z", sign, 1, dx, sign, low, rows, parent)
            two = add(kv, "z", sign, 2 if jump else 1, dx, 2 * sign, low, rows, parent if jump else one)
            three = add(kv, "z", sign, 1, dx, 3 * sign, low, rows, two)
            part = low if sign > 0 else low + half
            out += [one, two, three, add(kv, "z", sign, 1, dx, 4 * sign, part, half, three)]
        return out

    for kv, low, rows in Z_FIRST:
        firsts = along_z(kv, 0, low, rows, None, True)
        along_x(kv, 0, low, rows, None, False)
        for first in firsts:
            along_x(kv, first.dz, first.low, first.rows, first, False)
    for kv, low, rows in X_FIRST:
        firsts = along_x(kv, 0, low, rows, None, True)
        along_z(kv, 0, low, rows, None, False)
        for first in firsts:
            along_z(kv, first.dx, first.low, first.rows, first, False)
    for message in made:
        if message.parent is not None:
            message.parent.children.append(message)
    free = {}
    ready = [(0.0, i) for i, m in enumerate(made) if m.parent is None]
    while ready:
        ready.sort()
        start, i = ready.pop(0)
        message = made[i]
        link = (message.axis, message.sign)
        free[link] = max(start, free.get(link, 0.0)) + message.rows * ROWS_US * message.hops
        message.time = free[link] + HOP_US + ROUTE_US * (message.hops - 1)
        ready += [(message.time, made.index(child)) for child in message.children]
    order = sorted(made, key=lambda m: m.time)
    for index, message in enumerate(order):
        message.index = index
    return order


def norm_rows(values, gain):
    centre = values - jnp.mean(values, axis=-1, keepdims=True)
    spread = jnp.mean(centre * centre, axis=-1, keepdims=True)
    return centre * lax.rsqrt(spread + 1e-07) * gain


def gelu(values):
    return 0.5 * values * (1.0 + lax.erf(values * (1.0 / math.sqrt(2.0))))


def encoder_kernel(
    plan,
    group_hbm,
    tokens_hbm,
    w_qkv_hbm,
    w_out_hbm,
    w_up_hbm,
    w_down_hbm,
    gain_one_hbm,
    gain_two_hbm,
    rel_hbm,
    cache_hbm,
    w_proj_hbm,
    docs_hbm,
    lengths_hbm,
    cand_hbm,
    query_out,
    score_out,
    group_ref,
    gains,
    w_proj,
    lengths_ref,
    cand_tile,
    cand_wide,
    cand_mine,
    score_tile,
    cache,
    tokens,
    w_qkv,
    w_out,
    w_up,
    w_down,
    rel,
    q_mask,
    k_own,
    v_own,
    q_rel,
    rel_two,
    att,
    att_send,
    opp_send,
    side_send,
    opp_recv,
    side_recv,
    hidden,
    vectors,
    load_sem,
    gather_send,
    gather_recv,
    swap_send,
    swap_recv,
    att_sem,
    opp_send_sem,
    opp_recv_sem,
    side_send_sem,
    side_recv_sem,
    hid_send_sem,
    hid_recv_sem,
    vec_send_sem,
    vec_recv_sem,
    docs,
    queries,
    cand_rows,
    table,
    table_smem,
    best_rows,
    back_send,
    back_recv,
    table_sem,
    cand_send_sem,
    cand_recv_sem,
    spread_send_sem,
    spread_recv_sem,
    across_send_sem,
    across_recv_sem,
    share_send_sem,
    share_recv_sem,
    back_send_sem,
    back_recv_sem,
):
    head = lax.axis_index("head")
    doc = lax.axis_index("doc")
    y, core = lax.div(head, 2), lax.rem(head, 2)
    x, z = lax.div(doc, NZ), lax.rem(doc, NZ)
    partner = (2 * y + 1 - core, doc)
    y_up, y_down = mod(y + 1, NY), mod(y - 1, NY)
    y_far = mod(y + 2, NY)

    def at_y(other):
        return (2 * other + core, doc)

    def at_link(axis, sign):
        if axis == "x":
            return (head, mod(x + sign, NX) * NZ + z)
        return (head, x * NZ + mod(z + sign, NZ))

    peers = [partner]
    for other in (y_up, y_down, y_far):
        peers += [(2 * other + core, doc), (2 * other + 1 - core, doc)]
    links = [at_link(axis, sign * hops) for axis in ("x", "z") for sign in (1, -1) for hops in (1, 2)]
    barrier = pltpu.get_barrier_semaphore()
    for device in peers + links:
        pl.semaphore_signal(barrier, inc=1, device_id=device, device_id_type=MESH)

    loads = [
        pltpu.make_async_copy(tokens_hbm, tokens, load_sem.at[0]),
        pltpu.make_async_copy(w_qkv_hbm, w_qkv, load_sem.at[1]),
        pltpu.make_async_copy(rel_hbm.at[pl.ds(RELS // 2 - 96, 128)], rel.at[0], load_sem.at[2]),
        pltpu.make_async_copy(rel_hbm.at[pl.ds(RELS // 2 - 32, 128)], rel.at[1], load_sem.at[3]),
        pltpu.make_async_copy(
            cache_hbm, cache.at[:, pl.ds(doc * 2, 2)], load_sem.at[4]
        ),
        pltpu.make_async_copy(w_out_hbm, w_out.at[core], load_sem.at[5]),
        pltpu.make_async_copy(w_up_hbm, w_up.at[core], load_sem.at[6]),
        pltpu.make_async_copy(w_down_hbm, w_down.at[core], load_sem.at[7]),
        pltpu.make_async_copy(docs_hbm, docs, load_sem.at[8]),
        pltpu.make_async_copy(gain_one_hbm, gains.at[pl.ds(0, 1)], load_sem.at[9]),
        pltpu.make_async_copy(gain_two_hbm, gains.at[pl.ds(8, 1)], load_sem.at[10]),
        pltpu.make_async_copy(w_proj_hbm, w_proj, load_sem.at[11]),
        pltpu.make_async_copy(lengths_hbm, lengths_ref, load_sem.at[12]),
        pltpu.make_async_copy(cand_hbm, cand_tile, load_sem.at[13]),
        pltpu.make_async_copy(group_hbm, group_ref, load_sem.at[14]),
    ]
    for load in loads:
        load.start()
    pl.semaphore_wait(barrier, len(peers) + len(links))

    def gather_copy(message):
        dx, dz = message.dx, message.dz
        if message.axis == "x":
            dx -= message.sign * message.hops
        else:
            dz -= message.sign * message.hops
        block = mod(x - dx, NX) * NZ + mod(z - dz, NZ)
        group, low = block * 2 + message.low // PLEN, message.low % PLEN
        if message.rows == 2 * PLEN:
            target = cache.at[message.kv, pl.ds(group, 2)]
        else:
            target = cache.at[message.kv, group, pl.ds(low, message.rows)]
        source = target
        if message.parent is None:
            source = cache_hbm.at[message.kv]
            if message.rows < 2 * PLEN:
                source = source.at[message.low // PLEN, pl.ds(low, message.rows)]
        return pltpu.make_async_remote_copy(
            src_ref=source,
            dst_ref=target,
            send_sem=gather_send.at[message.index],
            recv_sem=gather_recv.at[message.index],
            device_id=at_link(message.axis, message.sign * message.hops),
            device_id_type=MESH,
        )

    copies = {message.index: gather_copy(message) for message in plan}
    for message in plan:
        if message.parent is None:
            copies[message.index].start()

    swaps = []
    for i, (source, target) in enumerate(((w_out_hbm, w_out), (w_up_hbm, w_up), (w_down_hbm, w_down))):
        swaps.append(
            pltpu.make_async_remote_copy(
                src_ref=source,
                dst_ref=target.at[core],
                send_sem=swap_send.at[i],
                recv_sem=swap_recv.at[i],
                device_id=partner,
                device_id_type=MESH,
            )
        )
        swaps[-1].start()

    loads[0].wait()
    loads[1].wait()
    low_head = lax.broadcasted_iota(jnp.int32, (128, 128), 1) < HD
    for block in range(3):
        rows = slice(block * 128, block * 128 + 128)
        q_made, k_made, v_made = (
            jnp.dot(tokens[rows, :], w_qkv[i], preferred_element_type=F32) for i in range(3)
        )
        q_mask[0, rows, :] = jnp.where(low_head, q_made, 0.0).astype(BF16)
        q_mask[1, rows, :] = jnp.where(low_head, 0.0, q_made).astype(BF16)
        k_own[rows, :] = k_made.astype(BF16)
        v_own[rows, :] = v_made.astype(BF16)
    loads[2].wait()
    loads[3].wait()
    flip = (
        lax.broadcasted_iota(jnp.int32, (128, 128), 0) + lax.broadcasted_iota(jnp.int32, (128, 128), 1)
        == 127
    ).astype(F32).astype(BF16)
    for i in range(2):
        row = jnp.dot(
            rel[i], w_qkv[i], preferred_element_type=F32
        ).astype(BF16)
        turned = jnp.dot(flip, row, preferred_element_type=F32)
        rel_two[i, 0:128, :] = jnp.where(low_head, turned, 0.0).astype(BF16)
        rel_two[i, 128:256, :] = jnp.where(low_head, 0.0, turned).astype(BF16)
    for block in range(3):
        rows = slice(block * 128, block * 128 + 128)
        q_all = q_mask[0, rows, :] + q_mask[1, rows, :]
        q_rel[rows, :] = lax.dot_general(q_all, rel_two[1], NT, preferred_element_type=F32)
    loads[4].wait()
    for i in range(9, 15):
        loads[i].wait()
    cand_wide[...] = jnp.zeros_like(cand_wide)
    cand_wide[:, : cand_tile.shape[1]] = cand_tile[...]
    cand_mine[...] = jnp.sum(pltpu.roll(cand_wide[...], 0, 1, stride=16, stride_axis=0), axis=0, keepdims=True)

    for message in plan:
        copies[message.index].wait_recv()
        for child in message.children:
            copies[child.index].start()

    low_lane = lax.broadcasted_iota(jnp.int32, (96, 128), 1) < QLEN
    low_half = lax.broadcasted_iota(jnp.int32, (QLEN, 128), 1) < HD

    def attend(request):
        group = group_ref[request]
        own = pl.ds(pl.multiple_of(request * QLEN, QLEN), QLEN)
        keys = jnp.concatenate([cache[0, group], k_own[own, :]], axis=0)
        values = jnp.concatenate([cache[1, group], v_own[own, :]], axis=0)
        query = jnp.concatenate([q_mask[0, own, :], q_mask[1, own, :]], axis=0)
        content = lax.dot_general(query, keys, NT, preferred_element_type=F32)
        key_rel = lax.dot_general(keys, rel_two[0], NT, preferred_element_type=F32)
        first = pltpu.roll(key_rel[:, :128], 33, 1, stride=1, stride_axis=0)
        second = pltpu.roll(key_rel[:, 128:], 65, 1, stride=1, stride_axis=0)
        p2c = jnp.transpose(jnp.where(low_lane, first, second))[: 2 * QLEN, :]
        mine = q_rel[own, :]
        c2p = jnp.concatenate(
            [
                pltpu.roll(mine[:, :128], 97, 1, stride=1, stride_axis=0),
                pltpu.roll(mine[:, 128:], 97, 1, stride=1, stride_axis=0),
            ],
            axis=0,
        )[:, :96]
        logits = (content + c2p + p2c) * (1.0 / math.sqrt(3 * HD))
        weights = jnp.exp(logits - jnp.max(logits, axis=-1, keepdims=True))
        total = jnp.sum(weights, axis=-1, keepdims=True)
        out = jnp.dot(weights.astype(BF16), values, preferred_element_type=F32) / total
        return jnp.where(low_half, out[:QLEN], out[QLEN:]).astype(BF16)

    half = tokens.shape[0] // 2
    per_core = half // QLEN
    for i in range(per_core):
        att_send[i * QLEN : i * QLEN + QLEN, :] = attend((1 - core) * per_core + i)
    att_copy = pltpu.make_async_remote_copy(
        src_ref=att_send,
        dst_ref=att.at[core],
        send_sem=att_sem.at[0],
        recv_sem=att_sem.at[1],
        device_id=partner,
        device_id_type=MESH,
    )
    att_copy.start()
    for i in range(per_core):
        att[core, i * QLEN : i * QLEN + QLEN, :] = attend(core * per_core + i)
    att_copy.wait_recv()
    loads[5].wait()
    swaps[0].wait_recv()
    part = half // NY

    def chunk_rows(other):
        return pl.ds(pl.multiple_of(other * part, 16), part)

    def out_part(other):
        rows = chunk_rows(other)
        return jnp.dot(att[0, rows, :], w_out[0], preferred_element_type=F32) + jnp.dot(
            att[1, rows, :], w_out[1], preferred_element_type=F32
        )

    def side_copy(phase, side, piece):
        return pltpu.make_async_remote_copy(
            src_ref=side_send.at[phase, side, piece],
            dst_ref=side_recv.at[phase, side, piece],
            send_sem=side_send_sem.at[phase, side, piece],
            recv_sem=side_recv_sem.at[phase, side, piece],
            device_id=at_y(y_down if side else y_up),
            device_id_type=MESH,
        )

    def far_copy(phase, piece):
        return pltpu.make_async_remote_copy(
            src_ref=opp_send.at[phase, piece],
            dst_ref=opp_recv.at[phase, piece],
            send_sem=opp_send_sem.at[phase, piece],
            recv_sem=opp_recv_sem.at[phase, piece],
            device_id=at_y(y_down if piece else y_up),
            device_id_type=MESH,
        )

    wide = 512

    def reduce_rows(phase, far, up, down, own):
        sent = []
        share = far()
        for piece in range(2):
            opp_send[phase, piece] = share[:, piece * wide : piece * wide + wide].astype(BF16)
            copy = far_copy(phase, piece)
            copy.start()
            sent.append(copy)
        share_up, share_down = up(), down()
        side_send[phase, 0, 1] = share_up[:, wide:].astype(BF16)
        side_send[phase, 1, 0] = share_down[:, :wide].astype(BF16)
        for side, piece in ((0, 1), (1, 0)):
            copy = side_copy(phase, side, piece)
            copy.start()
            sent.append(copy)
        share_own = own()
        far_copy(phase, 0).wait_recv()
        side_send[phase, 0, 0] = (share_up[:, :wide] + opp_recv[phase, 0].astype(F32)).astype(BF16)
        copy = side_copy(phase, 0, 0)
        copy.start()
        sent.append(copy)
        far_copy(phase, 1).wait_recv()
        side_send[phase, 1, 1] = (share_down[:, wide:] + opp_recv[phase, 1].astype(F32)).astype(BF16)
        copy = side_copy(phase, 1, 1)
        copy.start()
        sent.append(copy)
        for side, piece in ((0, 1), (1, 0), (0, 0), (1, 1)):
            side_copy(phase, side, piece).wait_recv()
        halves = [
            share_own[:, piece * wide : piece * wide + wide]
            + side_recv[phase, 0, piece].astype(F32)
            + side_recv[phase, 1, piece].astype(F32)
            for piece in range(2)
        ]
        return jnp.concatenate(halves, axis=1), sent

    total, sent_one = reduce_rows(
        0,
        lambda: out_part(y_far),
        lambda: out_part(y_up),
        lambda: out_part(y_down),
        lambda: out_part(y),
    )
    own_rows = pl.ds(pl.multiple_of(core * half + y * part, 16), part)
    one = norm_rows(tokens[own_rows, :].astype(F32) + total, gains[0:1, :]).astype(BF16)
    for piece in range(2):
        hidden[y, piece] = one[:, piece * wide : piece * wide + wide]

    def hidden_copy(side, hop, piece):
        block = y if hop == 0 else (y_up if side else y_down)
        return pltpu.make_async_remote_copy(
            src_ref=hidden.at[block, piece],
            dst_ref=hidden.at[block, piece],
            send_sem=hid_send_sem.at[side, hop, piece],
            recv_sem=hid_recv_sem.at[side, hop, piece],
            device_id=at_y(y_down if side else y_up),
            device_id_type=MESH,
        )

    sent_two = []

    def send_hidden(side, hop, piece):
        copy = hidden_copy(side, hop, piece)
        copy.start()
        sent_two.append(copy)

    send_hidden(0, 0, 0)
    send_hidden(1, 0, 1)
    send_hidden(0, 0, 1)
    send_hidden(1, 0, 0)
    home = mod(x + z, NY)
    at_home = home == y
    my_row = (x * 2 + lax.div(z, 4)) * NY + y

    def cand_copy(offset):
        return pltpu.make_async_remote_copy(
            src_ref=cand_mine,
            dst_ref=cand_rows.at[my_row],
            send_sem=cand_send_sem.at[offset],
            recv_sem=cand_recv_sem.at[my_row],
            device_id=(2 * home + core, mod(doc + offset, NX * NZ)),
            device_id_type=MESH,
        )

    cand_local = pltpu.make_async_copy(cand_mine, cand_rows.at[my_row], cand_recv_sem.at[my_row])
    for i in (6, 7):
        loads[i].wait()
    swaps[1].wait_recv()
    swaps[2].wait_recv()

    def feed(other):
        rows = jnp.concatenate([hidden[other, 0], hidden[other, 1]], axis=1)
        made = None
        for i in range(2):
            inner = gelu(jnp.dot(rows, w_up[i], preferred_element_type=F32)).astype(BF16)
            term = jnp.dot(inner, w_down[i], preferred_element_type=F32)
            made = term if made is None else made + term
        return made

    feed_own = feed(y)
    pl.when(at_home)(lambda: cand_local.start())
    pl.when(jnp.logical_not(at_home))(lambda: cand_copy(0).start())
    pl.loop(1, NX * NZ)(lambda offset: cand_copy(offset).start())
    hidden_copy(0, 0, 0).wait_recv()
    send_hidden(0, 1, 0)
    hidden_copy(1, 0, 1).wait_recv()
    send_hidden(1, 1, 1)
    hidden_copy(0, 0, 1).wait_recv()
    hidden_copy(1, 0, 0).wait_recv()
    feed_up, feed_down = feed(y_up), feed(y_down)
    hidden_copy(0, 1, 0).wait_recv()
    hidden_copy(1, 1, 1).wait_recv()
    lane = lax.broadcasted_iota(jnp.int32, (NX * NZ, 128), 1)
    places = []
    table_copy = pltpu.make_async_copy(table, table_smem, table_sem.at[0])

    def slots_then_own():
        @pl.loop(0, NX * NZ)
        def _(row):
            pltpu.make_async_copy(cand_mine, cand_rows.at[row], cand_recv_sem.at[row]).wait()

        named = cand_rows[...].reshape(NX * NZ, 128)
        mine = jnp.logical_and(lax.shift_right_logical(named, 6) == doc, lax.bitwise_and(lane, 15) < 12)
        mine_f = jnp.where(mine, 1.0, 0.0)
        before = (
            lax.broadcasted_iota(jnp.int32, (128, 128), 0) < lax.broadcasted_iota(jnp.int32, (128, 128), 1)
        ).astype(F32).astype(BF16)
        rank = jnp.dot(mine_f.astype(BF16), before, preferred_element_type=F32)
        rows_table = jnp.zeros((NX * NZ, 128), jnp.int32)
        for slot in range(SLOTS):
            chosen = jnp.where(rank == float(slot), mine_f, 0.0)
            some = jnp.sum(chosen, axis=1, keepdims=True)
            place = jnp.sum(chosen * lane.astype(F32), axis=1, keepdims=True).astype(jnp.int32)
            which = jnp.sum(
                chosen * lax.bitwise_and(named, DOC_DEV - 1).astype(F32), axis=1, keepdims=True
            ).astype(jnp.int32)
            places.append(jnp.where(some > 0.5, place, 127))
            rows_table = jnp.where(lane == slot, lax.bitwise_and(place, 15) * 2, rows_table)
            rows_table = jnp.where(lane == slot + 8, which, rows_table)
        table[...] = rows_table
        table_copy.start()
        return feed_own

    total_two, sent_three = reduce_rows(
        1, lambda: feed(y_far), lambda: feed_up, lambda: feed_down, slots_then_own
    )
    two = norm_rows(one.astype(F32) + total_two, gains[8:9, :]).astype(BF16)
    projected = jnp.dot(two, w_proj[...], preferred_element_type=F32)
    unit = projected * lax.rsqrt(jnp.sum(projected * projected, axis=-1, keepdims=True) + 1e-06)
    vectors[head] = unit.astype(BF16).reshape(3, 16, 128)

    sent_four = []
    for i, device in enumerate(peers):
        copy = pltpu.make_async_remote_copy(
            src_ref=vectors.at[head],
            dst_ref=vectors.at[head],
            send_sem=vec_send_sem.at[i],
            recv_sem=vec_recv_sem.at[i],
            device_id=device,
            device_id_type=MESH,
        )
        copy.start()
        sent_four.append(copy)
    half_doc = lax.div(z, 4)
    piece_rows = pl.ds(core * 12 + y * 3, 3)

    def spread_copy(offset):
        return pltpu.make_async_remote_copy(
            src_ref=vectors.at[head],
            dst_ref=queries.at[x * 2 + half_doc, piece_rows],
            send_sem=spread_send_sem.at[offset],
            recv_sem=spread_recv_sem.at[half_doc, y],
            device_id=(2 * home + core, x * NZ + mod(z + offset, NZ)),
            device_id_type=MESH,
        )

    def across_copy(half_index, source_y, offset, index):
        rows = queries.at[index, pl.ds(core * 12 + source_y * 3, 3)]
        return pltpu.make_async_remote_copy(
            src_ref=rows,
            dst_ref=rows,
            send_sem=across_send_sem.at[half_index, source_y, offset - 1],
            recv_sem=across_recv_sem.at[half_index, source_y, offset - 1],
            device_id=(head, mod(x + offset, NX) * NZ + z),
            device_id_type=MESH,
        )

    def share_copy(place, index):
        rows = queries.at[index, pl.ds(core * 12, 12)]
        return pltpu.make_async_remote_copy(
            src_ref=rows,
            dst_ref=rows,
            send_sem=share_send_sem.at[place],
            recv_sem=share_recv_sem.at[place],
            device_id=partner,
            device_id_type=MESH,
        )

    spread_local = pltpu.make_async_copy(
        vectors.at[head], queries.at[x * 2 + half_doc, piece_rows], spread_recv_sem.at[half_doc, y]
    )
    pl.when(at_home)(lambda: spread_local.start())
    pl.when(jnp.logical_not(at_home))(lambda: spread_copy(0).start())
    for offset in (4, 3, 5, 2, 6, 1, 7):
        spread_copy(offset).start()
    crossing = []
    shared = []
    for source_y in range(NY):
        for half_index in range(2):
            pltpu.make_async_copy(
                vectors.at[head],
                queries.at[x * 2 + half_index, pl.ds(core * 12 + source_y * 3, 3)],
                spread_recv_sem.at[half_index, source_y],
            ).wait()
            for offset in (2, 1, 3):
                crossing.append(across_copy(half_index, source_y, offset, x * 2 + half_index))
                crossing[-1].start()
    for half_index in range(2):
        shared.append(share_copy(half_index, x * 2 + half_index))
        shared[-1].start()
    for copy in sent_four:
        copy.wait_recv()
    outs = []
    for block in range(2 * NY):
        place = (block % 2) * 12 + (block // 2) * 3
        outs.append(
            pltpu.make_async_copy(vectors.at[block], query_out.at[pl.ds(place, 3)], load_sem.at[block])
        )
        outs[-1].start()
    for offset in (1, 3, 2):
        for half_index in range(2):
            index = mod(x - offset, NX) * 2 + half_index
            for source_y in range(NY):
                across_copy(half_index, source_y, offset, index).wait_recv()
            shared.append(share_copy(2 * offset + half_index, index))
            shared[-1].start()
    table_copy.wait()
    loads[8].wait()
    for copy in shared:
        copy.wait_recv()

    zeros = jnp.zeros((QLEN, 128), BF16)
    row_index = lax.broadcasted_iota(jnp.int32, (256, 2 * QLEN), 0)
    first_lanes = lax.broadcasted_iota(jnp.int32, (1, 2 * QLEN), 1) < QLEN

    @pl.loop(0, NX * NZ // ROWS)
    def _(step):
        source = lax.div(step * ROWS, NY)
        for row, pair in [(step * ROWS + i, pair) for i in range(ROWS) for pair in range(SLOTS // 2)]:
            found = []
            for slot in (2 * pair, 2 * pair + 1):
                which = jnp.clip(table_smem[row, slot + 8], 0, DOC_DEV - 1)
                request = jnp.clip(table_smem[row, slot], 0, 22)
                query = jnp.concatenate([queries[source, request], queries[source, request + 1]], axis=0)
                found.append((docs[which], query, lengths_ref[which]))
            (doc_a, query_a, len_a), (doc_b, query_b, len_b) = found
            left = jnp.concatenate([doc_a, doc_b], axis=1)
            right = jnp.concatenate(
                [
                    jnp.concatenate([query_a, zeros], axis=1),
                    jnp.concatenate([zeros, query_b], axis=1),
                ],
                axis=0,
            )
            sims = lax.dot_general(left, right, NT, preferred_element_type=F32)
            live = row_index < jnp.where(first_lanes, len_a, len_b)
            best_rows[pair, pl.ds(row, 1), : 2 * QLEN] = jnp.max(
                jnp.where(live, sims, -jnp.inf), axis=0, keepdims=True
            )

    rated = jnp.zeros((NX * NZ, 128), F32)
    for slot in range(SLOTS):
        low = (slot % 2) * QLEN
        value = jnp.sum(best_rows[slot // 2][:, low : low + QLEN], axis=1, keepdims=True)
        rated = rated + jnp.where(lane == places[slot], value, 0.0)
    back_send[...] = rated.reshape(NX * NZ, 1, 128)

    def back_to(row):
        source_x, source_half, source_y = lax.div(row, 8), lax.rem(lax.div(row, NY), 2), lax.rem(row, NY)
        source = source_x * NZ + mod(y - source_x, NY) + 4 * source_half
        return source, source_y

    def back_copy(row):
        source, source_y = back_to(row)
        return pltpu.make_async_remote_copy(
            src_ref=back_send.at[row],
            dst_ref=back_recv.at[doc],
            send_sem=back_send_sem.at[row],
            recv_sem=back_recv_sem.at[doc],
            device_id=(2 * source_y + core, source),
            device_id_type=MESH,
        )

    def is_own(row):
        source, source_y = back_to(row)
        return jnp.logical_and(source == doc, source_y == y)

    @pl.loop(0, NX * NZ)
    def _(row):
        own_row = is_own(row)
        pl.when(own_row)(
            lambda: pltpu.make_async_copy(
                back_send.at[row], back_recv.at[doc], back_recv_sem.at[doc]
            ).start()
        )
        pl.when(jnp.logical_not(own_row))(lambda: back_copy(row).start())

    @pl.loop(0, NX * NZ)
    def _(row):
        pltpu.make_async_copy(back_send.at[0], back_recv.at[row], back_recv_sem.at[row]).wait()

    answer = jnp.broadcast_to(jnp.sum(back_recv[...], axis=0), (8, 128))
    spot = lax.broadcasted_iota(jnp.int32, (8, 128), 0)
    turned = answer
    for i in range(1, 8):
        turned = jnp.where(spot == i, pltpu.roll(answer, 128 - 16 * i, 1), turned)
    score_tile[...] = turned[:, : score_tile.shape[1]]
    outs.append(pltpu.make_async_copy(score_tile, score_out, load_sem.at[8]))
    outs[-1].start()
    for copy in outs:
        copy.wait()

    @pl.loop(0, NX * NZ)
    def _(row):
        pl.when(jnp.logical_not(is_own(row)))(lambda: back_copy(row).wait_send())

    pl.when(jnp.logical_not(at_home))(lambda: cand_copy(0).wait_send())
    pl.loop(1, NX * NZ)(lambda offset: cand_copy(offset).wait_send())
    pl.when(jnp.logical_not(at_home))(lambda: spread_copy(0).wait_send())
    for offset in range(1, NZ):
        spread_copy(offset).wait_send()
    for copy in list(copies.values()) + swaps + [att_copy] + sent_one + sent_two + sent_three + sent_four + crossing + shared:
        copy.wait_send()


def encode(tokens, w_qkv, w_out, w_up, w_down, gain_one, gain_two, rel_table, prompt_cache, w_proj, docs, lengths, named, group_ids):
    plan = plan_gather()
    rows, width = tokens.shape
    half = rows // 2
    part = half // NY
    anywhere = pl.BlockSpec(memory_space=pl.ANY)
    dma = pltpu.SemaphoreType.DMA
    return pl.pallas_call(
        functools.partial(encoder_kernel, plan),
        out_shape=(
            jax.ShapeDtypeStruct((rows // 16, 16, 128), BF16),
            jax.ShapeDtypeStruct(named.shape, F32),
        ),
        in_specs=[anywhere] * 14,
        out_specs=(anywhere, anywhere),
        scratch_shapes=[
            pltpu.SMEM(group_ids.shape, jnp.int32),
            pltpu.VMEM((16, width), F32),
            pltpu.VMEM((width, 128), BF16),
            pltpu.SMEM(lengths.shape, jnp.int32),
            pltpu.VMEM(named.shape, jnp.int32),
            pltpu.VMEM((8, 128), jnp.int32),
            pltpu.VMEM((1, 128), jnp.int32),
            pltpu.VMEM(named.shape, F32),
            pltpu.VMEM((2, 64, PLEN, 128), BF16),
            pltpu.VMEM((rows, width), BF16),
            pltpu.VMEM((3, width, 128), BF16),
            pltpu.VMEM((2, 128, width), BF16),
            pltpu.VMEM((2, width, 512), BF16),
            pltpu.VMEM((2, 512, width), BF16),
            pltpu.VMEM((2, 128, width), BF16),
            pltpu.VMEM((2, rows, 128), BF16),
            pltpu.VMEM((rows, 128), BF16),
            pltpu.VMEM((rows, 128), BF16),
            pltpu.VMEM((rows, 256), F32),
            pltpu.VMEM((2, 256, 128), BF16),
            pltpu.VMEM((2, half, 128), BF16),
            pltpu.VMEM((half, 128), BF16),
            pltpu.VMEM((2, 2, part, 512), BF16),
            pltpu.VMEM((2, 2, 2, part, 512), BF16),
            pltpu.VMEM((2, 2, part, 512), BF16),
            pltpu.VMEM((2, 2, 2, part, 512), BF16),
            pltpu.VMEM((NY, 2, part, 512), BF16),
            pltpu.VMEM((2 * NY, 3, 16, 128), BF16),
            dma((15,)),
            dma((len(plan),)),
            dma((len(plan),)),
            dma((3,)),
            dma((3,)),
            dma((2,)),
            dma((2, 2)),
            dma((2, 2)),
            dma((2, 2, 2)),
            dma((2, 2, 2)),
            dma((2, 2, 2)),
            dma((2, 2, 2)),
            dma((7,)),
            dma((7,)),
            pltpu.VMEM((64, 256, 128), BF16),
            pltpu.VMEM((8, 24, 16, 128), BF16),
            pltpu.VMEM((32, 1, 128), jnp.int32),
            pltpu.VMEM((32, 128), jnp.int32),
            pltpu.SMEM((32, 128), jnp.int32),
            pltpu.VMEM((SLOTS // 2, 32, 128), F32),
            pltpu.VMEM((32, 1, 128), F32),
            pltpu.VMEM((32, 1, 128), F32),
            dma((1,)),
            dma((32,)),
            dma((32,)),
            dma((8,)),
            dma((2, 4)),
            dma((2, 4, 3)),
            dma((2, 4, 3)),
            dma((8,)),
            dma((8,)),
            dma((32,)),
            dma((32,)),
        ],
        compiler_params=pltpu.CompilerParams(collective_id=0, has_side_effects=True),
        name="encoder",
    )(
        group_ids,
        tokens,
        jnp.transpose(w_qkv, (1, 0, 2)),
        w_out,
        w_up,
        w_down,
        gain_one.reshape(1, -1),
        gain_two.reshape(1, -1),
        rel_table,
        prompt_cache.reshape(2, 2, PLEN, 128),
        w_proj,
        docs,
        lengths,
        named,
    )


def body(
    tokens,
    w_qkv,
    w_out,
    w_up,
    w_down,
    gain_one,
    gain_two,
    rel_table,
    prompt_cache,
    w_proj,
    doc_vectors,
    doc_lengths,
    group_ids,
    candidates,
):
    query_vectors, rated = encode(
        tokens,
        w_qkv,
        w_out,
        w_up,
        w_down,
        gain_one,
        gain_two,
        rel_table,
        prompt_cache,
        w_proj,
        doc_vectors,
        doc_lengths,
        candidates.T,
        group_ids,
    )
    return (query_vectors.reshape(tokens.shape[0], 128), rated.T)


def solution(mesh):
    placed = (
        P("doc", None),
        P(None, None, "head"),
        P("head", None),
        P(None, "head"),
        P("head", None),
        P(),
        P(),
        P(),
        P(None, "doc", "head"),
        P(),
        P("doc", None, None),
        P("doc"),
        P("doc"),
        P("doc", "head"),
    )
    return jax.shard_map(
        body,
        mesh=mesh,
        in_specs=placed,
        out_specs=(P("doc", None), P("doc", "head")),
        check_vma=False,
    )
```

```python
import functools
import math

import jax
import jax.numpy as jnp
from jax import lax
from jax.experimental import pallas as pl
from jax.experimental.pallas import tpu as pltpu
from jax.sharding import PartitionSpec as P

HD = 64
RELS = 512
QLEN = 32
PLEN = 64
DOC_DEV = 64
NX = 4
NZ = 8
NY = 4
SLOTS = 6
ROWS = 4
MESH = pl.DeviceIdType.MESH
F32 = jnp.float32
BF16 = jnp.bfloat16
NT = (((1,), (1,)), ((), ()))


def mod(value, size):
    return lax.rem(value + 4 * size, size)


HOP_US = 2.3
ROUTE_US = 0.65
ROWS_US = 256 / 46500.0
Z_FIRST = ((0, 0, 128),)
X_FIRST = ((1, 0, 128),)


class Message:
    def __init__(self, kv, axis, sign, hops, dx, dz, low, rows, parent):
        self.kv, self.axis, self.sign, self.hops = kv, axis, sign, hops
        self.dx, self.dz, self.low, self.rows, self.parent = dx, dz, low, rows, parent
        self.children = []
        self.time = None
        self.index = None


def plan_gather():
    made = []

    def add(*fields):
        made.append(Message(*fields))
        return made[-1]

    def along_x(kv, dz, low, rows, parent, direct):
        out = []
        half = rows // 2
        for sign in (1, -1):
            near = add(kv, "x", sign, 1, sign, dz, low, rows, parent)
            part = low if sign > 0 else low + half
            hops = 2 if direct else 1
            out += [near, add(kv, "x", sign, hops, 2 * sign, dz, part, half, parent if direct else near)]
        return out

    def along_z(kv, dx, low, rows, parent, jump):
        out = []
        half = rows // 2
        for sign in (1, -1):
            one = add(kv, "z", sign, 1, dx, sign, low, rows, parent)
            two = add(kv, "z", sign, 2 if jump else 1, dx, 2 * sign, low, rows, parent if jump else one)
            three = add(kv, "z", sign, 1, dx, 3 * sign, low, rows, two)
            part = low if sign > 0 else low + half
            out += [one, two, three, add(kv, "z", sign, 1, dx, 4 * sign, part, half, three)]
        return out

    for kv, low, rows in Z_FIRST:
        firsts = along_z(kv, 0, low, rows, None, True)
        along_x(kv, 0, low, rows, None, False)
        for first in firsts:
            along_x(kv, first.dz, first.low, first.rows, first, False)
    for kv, low, rows in X_FIRST:
        firsts = along_x(kv, 0, low, rows, None, True)
        along_z(kv, 0, low, rows, None, False)
        for first in firsts:
            along_z(kv, first.dx, first.low, first.rows, first, False)
    for message in made:
        if message.parent is not None:
            message.parent.children.append(message)
    free = {}
    ready = [(0.0, i) for i, m in enumerate(made) if m.parent is None]
    while ready:
        ready.sort()
        start, i = ready.pop(0)
        message = made[i]
        link = (message.axis, message.sign)
        free[link] = max(start, free.get(link, 0.0)) + message.rows * ROWS_US * message.hops
        message.time = free[link] + HOP_US + ROUTE_US * (message.hops - 1)
        ready += [(message.time, made.index(child)) for child in message.children]
    order = sorted(made, key=lambda m: m.time)
    for index, message in enumerate(order):
        message.index = index
    return order


def norm_rows(values, gain):
    centre = values - jnp.mean(values, axis=-1, keepdims=True)
    spread = jnp.mean(centre * centre, axis=-1, keepdims=True)
    return centre * lax.rsqrt(spread + 1e-07) * gain


def gelu(values):
    return 0.5 * values * (1.0 + lax.erf(values * (1.0 / math.sqrt(2.0))))


def encoder_kernel(
    plan,
    group_hbm,
    tokens_hbm,
    w_qkv_hbm,
    w_out_hbm,
    w_up_hbm,
    w_down_hbm,
    gain_one_hbm,
    gain_two_hbm,
    rel_hbm,
    cache_hbm,
    w_proj_hbm,
    docs_hbm,
    lengths_hbm,
    cand_hbm,
    query_out,
    score_out,
    group_ref,
    gains,
    w_proj,
    lengths_ref,
    cand_tile,
    cand_wide,
    cand_mine,
    score_tile,
    cache,
    tokens,
    w_qkv,
    w_out,
    w_up,
    w_down,
    rel,
    q_mask,
    k_own,
    v_own,
    q_rel,
    rel_two,
    att,
    att_send,
    opp_send,
    side_send,
    opp_recv,
    side_recv,
    hidden,
    vectors,
    load_sem,
    gather_send,
    gather_recv,
    swap_send,
    swap_recv,
    att_sem,
    opp_send_sem,
    opp_recv_sem,
    side_send_sem,
    side_recv_sem,
    hid_send_sem,
    hid_recv_sem,
    vec_send_sem,
    vec_recv_sem,
    docs,
    queries,
    near_queries,
    cand_rows,
    table,
    table_smem,
    best_rows,
    back_send,
    back_recv,
    table_sem,
    cand_send_sem,
    cand_recv_sem,
    spread_send_sem,
    spread_recv_sem,
    across_send_sem,
    across_recv_sem,
    share_send_sem,
    share_recv_sem,
    back_send_sem,
    back_recv_sem,
):
    head = lax.axis_index("head")
    doc = lax.axis_index("doc")
    y, core = lax.div(head, 2), lax.rem(head, 2)
    x, z = lax.div(doc, NZ), lax.rem(doc, NZ)
    partner = (2 * y + 1 - core, doc)
    y_up, y_down = mod(y + 1, NY), mod(y - 1, NY)
    y_far = mod(y + 2, NY)

    def at_y(other):
        return (2 * other + core, doc)

    def at_link(axis, sign):
        if axis == "x":
            return (head, mod(x + sign, NX) * NZ + z)
        return (head, x * NZ + mod(z + sign, NZ))

    peers = [partner]
    for other in (y_up, y_down, y_far):
        peers += [(2 * other + core, doc), (2 * other + 1 - core, doc)]
    links = [at_link(axis, sign * hops) for axis in ("x", "z") for sign in (1, -1) for hops in (1, 2)]
    barrier = pltpu.get_barrier_semaphore()
    for device in peers + links:
        pl.semaphore_signal(barrier, inc=1, device_id=device, device_id_type=MESH)

    loads = [
        pltpu.make_async_copy(tokens_hbm, tokens, load_sem.at[0]),
        pltpu.make_async_copy(w_qkv_hbm, w_qkv, load_sem.at[1]),
        pltpu.make_async_copy(rel_hbm.at[pl.ds(RELS // 2 - 96, 128)], rel.at[0], load_sem.at[2]),
        pltpu.make_async_copy(rel_hbm.at[pl.ds(RELS // 2 - 32, 128)], rel.at[1], load_sem.at[3]),
        pltpu.make_async_copy(
            cache_hbm, cache.at[:, pl.ds(doc * 2, 2)], load_sem.at[4]
        ),
        pltpu.make_async_copy(w_out_hbm, w_out.at[core], load_sem.at[5]),
        pltpu.make_async_copy(w_up_hbm, w_up.at[core], load_sem.at[6]),
        pltpu.make_async_copy(w_down_hbm, w_down.at[core], load_sem.at[7]),
        pltpu.make_async_copy(docs_hbm, docs, load_sem.at[8]),
        pltpu.make_async_copy(gain_one_hbm, gains.at[pl.ds(0, 1)], load_sem.at[9]),
        pltpu.make_async_copy(gain_two_hbm, gains.at[pl.ds(8, 1)], load_sem.at[10]),
        pltpu.make_async_copy(w_proj_hbm, w_proj, load_sem.at[11]),
        pltpu.make_async_copy(lengths_hbm, lengths_ref, load_sem.at[12]),
        pltpu.make_async_copy(cand_hbm, cand_tile, load_sem.at[13]),
        pltpu.make_async_copy(group_hbm, group_ref, load_sem.at[14]),
    ]
    for load in loads:
        load.start()
    pl.semaphore_wait(barrier, len(peers) + len(links))

    def gather_copy(message):
        dx, dz = message.dx, message.dz
        if message.axis == "x":
            dx -= message.sign * message.hops
        else:
            dz -= message.sign * message.hops
        block = mod(x - dx, NX) * NZ + mod(z - dz, NZ)
        group, low = block * 2 + message.low // PLEN, message.low % PLEN
        if message.rows == 2 * PLEN:
            target = cache.at[message.kv, pl.ds(group, 2)]
        else:
            target = cache.at[message.kv, group, pl.ds(low, message.rows)]
        source = target
        if message.parent is None:
            source = cache_hbm.at[message.kv]
            if message.rows < 2 * PLEN:
                source = source.at[message.low // PLEN, pl.ds(low, message.rows)]
        return pltpu.make_async_remote_copy(
            src_ref=source,
            dst_ref=target,
            send_sem=gather_send.at[message.index],
            recv_sem=gather_recv.at[message.index],
            device_id=at_link(message.axis, message.sign * message.hops),
            device_id_type=MESH,
        )

    copies = {message.index: gather_copy(message) for message in plan}
    for message in plan:
        if message.parent is None:
            copies[message.index].start()

    swaps = []
    for i, (source, target) in enumerate(((w_out_hbm, w_out), (w_up_hbm, w_up), (w_down_hbm, w_down))):
        swaps.append(
            pltpu.make_async_remote_copy(
                src_ref=source,
                dst_ref=target.at[core],
                send_sem=swap_send.at[i],
                recv_sem=swap_recv.at[i],
                device_id=partner,
                device_id_type=MESH,
            )
        )
        swaps[-1].start()

    loads[0].wait()
    loads[1].wait()
    low_head = lax.broadcasted_iota(jnp.int32, (128, 128), 1) < HD
    for block in range(3):
        rows = slice(block * 128, block * 128 + 128)
        q_made, k_made, v_made = (
            jnp.dot(tokens[rows, :], w_qkv[i], preferred_element_type=F32) for i in range(3)
        )
        q_mask[0, rows, :] = jnp.where(low_head, q_made, 0.0).astype(BF16)
        q_mask[1, rows, :] = jnp.where(low_head, 0.0, q_made).astype(BF16)
        k_own[rows, :] = k_made.astype(BF16)
        v_own[rows, :] = v_made.astype(BF16)
    loads[2].wait()
    loads[3].wait()
    flip = (
        lax.broadcasted_iota(jnp.int32, (128, 128), 0) + lax.broadcasted_iota(jnp.int32, (128, 128), 1)
        == 127
    ).astype(F32).astype(BF16)
    for i in range(2):
        row = jnp.dot(
            rel[i], w_qkv[i], preferred_element_type=F32
        ).astype(BF16)
        turned = jnp.dot(flip, row, preferred_element_type=F32)
        rel_two[i, 0:128, :] = jnp.where(low_head, turned, 0.0).astype(BF16)
        rel_two[i, 128:256, :] = jnp.where(low_head, 0.0, turned).astype(BF16)
    for block in range(3):
        rows = slice(block * 128, block * 128 + 128)
        q_all = q_mask[0, rows, :] + q_mask[1, rows, :]
        q_rel[rows, :] = lax.dot_general(q_all, rel_two[1], NT, preferred_element_type=F32)
    loads[4].wait()
    for i in range(9, 15):
        loads[i].wait()
    cand_wide[...] = jnp.zeros_like(cand_wide)
    cand_wide[:, : cand_tile.shape[1]] = cand_tile[...]
    cand_mine[...] = jnp.sum(pltpu.roll(cand_wide[...], 0, 1, stride=16, stride_axis=0), axis=0, keepdims=True)

    for message in plan:
        copies[message.index].wait_recv()
        for child in message.children:
            copies[child.index].start()

    low_lane = lax.broadcasted_iota(jnp.int32, (96, 128), 1) < QLEN
    low_half = lax.broadcasted_iota(jnp.int32, (QLEN, 128), 1) < HD

    def attend(request):
        group = group_ref[request]
        own = pl.ds(pl.multiple_of(request * QLEN, QLEN), QLEN)
        keys = jnp.concatenate([cache[0, group], k_own[own, :]], axis=0)
        values = jnp.concatenate([cache[1, group], v_own[own, :]], axis=0)
        query = jnp.concatenate([q_mask[0, own, :], q_mask[1, own, :]], axis=0)
        content = lax.dot_general(query, keys, NT, preferred_element_type=F32)
        key_rel = lax.dot_general(keys, rel_two[0], NT, preferred_element_type=F32)
        first = pltpu.roll(key_rel[:, :128], 33, 1, stride=1, stride_axis=0)
        second = pltpu.roll(key_rel[:, 128:], 65, 1, stride=1, stride_axis=0)
        p2c = jnp.transpose(jnp.where(low_lane, first, second))[: 2 * QLEN, :]
        mine = q_rel[own, :]
        c2p = jnp.concatenate(
            [
                pltpu.roll(mine[:, :128], 97, 1, stride=1, stride_axis=0),
                pltpu.roll(mine[:, 128:], 97, 1, stride=1, stride_axis=0),
            ],
            axis=0,
        )[:, :96]
        logits = (content + c2p + p2c) * (1.0 / math.sqrt(3 * HD))
        weights = jnp.exp(logits - jnp.max(logits, axis=-1, keepdims=True))
        total = jnp.sum(weights, axis=-1, keepdims=True)
        out = jnp.dot(weights.astype(BF16), values, preferred_element_type=F32) / total
        return jnp.where(low_half, out[:QLEN], out[QLEN:]).astype(BF16)

    half = tokens.shape[0] // 2
    per_core = half // QLEN
    for i in range(per_core):
        att_send[i * QLEN : i * QLEN + QLEN, :] = attend((1 - core) * per_core + i)
    att_copy = pltpu.make_async_remote_copy(
        src_ref=att_send,
        dst_ref=att.at[core],
        send_sem=att_sem.at[0],
        recv_sem=att_sem.at[1],
        device_id=partner,
        device_id_type=MESH,
    )
    att_copy.start()
    for i in range(per_core):
        att[core, i * QLEN : i * QLEN + QLEN, :] = attend(core * per_core + i)
    att_copy.wait_recv()
    loads[5].wait()
    swaps[0].wait_recv()
    part = half // NY

    def chunk_rows(other):
        return pl.ds(pl.multiple_of(other * part, 16), part)

    def out_part(other):
        rows = chunk_rows(other)
        return jnp.dot(att[0, rows, :], w_out[0], preferred_element_type=F32) + jnp.dot(
            att[1, rows, :], w_out[1], preferred_element_type=F32
        )

    def side_copy(phase, side, piece):
        return pltpu.make_async_remote_copy(
            src_ref=side_send.at[phase, side, piece],
            dst_ref=side_recv.at[phase, side, piece],
            send_sem=side_send_sem.at[phase, side, piece],
            recv_sem=side_recv_sem.at[phase, side, piece],
            device_id=at_y(y_down if side else y_up),
            device_id_type=MESH,
        )

    def far_copy(phase, piece):
        return pltpu.make_async_remote_copy(
            src_ref=opp_send.at[phase, piece],
            dst_ref=opp_recv.at[phase, piece],
            send_sem=opp_send_sem.at[phase, piece],
            recv_sem=opp_recv_sem.at[phase, piece],
            device_id=at_y(y_down if piece else y_up),
            device_id_type=MESH,
        )

    wide = 512

    def reduce_rows(phase, far, up, down, own):
        sent = []
        share = far()
        for piece in range(2):
            opp_send[phase, piece] = share[:, piece * wide : piece * wide + wide].astype(BF16)
            copy = far_copy(phase, piece)
            copy.start()
            sent.append(copy)
        share_up, share_down = up(), down()
        side_send[phase, 0, 1] = share_up[:, wide:].astype(BF16)
        side_send[phase, 1, 0] = share_down[:, :wide].astype(BF16)
        for side, piece in ((0, 1), (1, 0)):
            copy = side_copy(phase, side, piece)
            copy.start()
            sent.append(copy)
        share_own = own()
        far_copy(phase, 0).wait_recv()
        side_send[phase, 0, 0] = (share_up[:, :wide] + opp_recv[phase, 0].astype(F32)).astype(BF16)
        copy = side_copy(phase, 0, 0)
        copy.start()
        sent.append(copy)
        far_copy(phase, 1).wait_recv()
        side_send[phase, 1, 1] = (share_down[:, wide:] + opp_recv[phase, 1].astype(F32)).astype(BF16)
        copy = side_copy(phase, 1, 1)
        copy.start()
        sent.append(copy)
        for side, piece in ((0, 1), (1, 0), (0, 0), (1, 1)):
            side_copy(phase, side, piece).wait_recv()
        halves = [
            share_own[:, piece * wide : piece * wide + wide]
            + side_recv[phase, 0, piece].astype(F32)
            + side_recv[phase, 1, piece].astype(F32)
            for piece in range(2)
        ]
        return jnp.concatenate(halves, axis=1), sent

    total, sent_one = reduce_rows(
        0,
        lambda: out_part(y_far),
        lambda: out_part(y_up),
        lambda: out_part(y_down),
        lambda: out_part(y),
    )
    own_rows = pl.ds(pl.multiple_of(core * half + y * part, 16), part)
    one = norm_rows(tokens[own_rows, :].astype(F32) + total, gains[0:1, :]).astype(BF16)
    for piece in range(2):
        hidden[y, piece] = one[:, piece * wide : piece * wide + wide]

    def hidden_copy(side, hop, piece):
        block = y if hop == 0 else (y_up if side else y_down)
        return pltpu.make_async_remote_copy(
            src_ref=hidden.at[block, piece],
            dst_ref=hidden.at[block, piece],
            send_sem=hid_send_sem.at[side, hop, piece],
            recv_sem=hid_recv_sem.at[side, hop, piece],
            device_id=at_y(y_down if side else y_up),
            device_id_type=MESH,
        )

    sent_two = []

    def send_hidden(side, hop, piece):
        copy = hidden_copy(side, hop, piece)
        copy.start()
        sent_two.append(copy)

    send_hidden(0, 0, 0)
    send_hidden(1, 0, 1)
    send_hidden(0, 0, 1)
    send_hidden(1, 0, 0)
    home = mod(x + z, NY)
    at_home = home == y
    my_row = (x * 2 + lax.div(z, 4)) * NY + y

    def cand_copy(offset):
        return pltpu.make_async_remote_copy(
            src_ref=cand_mine,
            dst_ref=cand_rows.at[my_row],
            send_sem=cand_send_sem.at[offset],
            recv_sem=cand_recv_sem.at[my_row],
            device_id=(2 * home + core, mod(doc + offset, NX * NZ)),
            device_id_type=MESH,
        )

    cand_local = pltpu.make_async_copy(cand_mine, cand_rows.at[my_row], cand_recv_sem.at[my_row])
    for i in (6, 7):
        loads[i].wait()
    swaps[1].wait_recv()
    swaps[2].wait_recv()

    def feed(other):
        rows = jnp.concatenate([hidden[other, 0], hidden[other, 1]], axis=1)
        made = None
        for i in range(2):
            inner = gelu(jnp.dot(rows, w_up[i], preferred_element_type=F32)).astype(BF16)
            term = jnp.dot(inner, w_down[i], preferred_element_type=F32)
            made = term if made is None else made + term
        return made

    feed_own = feed(y)
    pl.when(at_home)(lambda: cand_local.start())
    pl.when(jnp.logical_not(at_home))(lambda: cand_copy(0).start())
    pl.loop(1, NX * NZ)(lambda offset: cand_copy(offset).start())
    hidden_copy(0, 0, 0).wait_recv()
    send_hidden(0, 1, 0)
    hidden_copy(1, 0, 1).wait_recv()
    send_hidden(1, 1, 1)
    hidden_copy(0, 0, 1).wait_recv()
    hidden_copy(1, 0, 0).wait_recv()
    feed_up, feed_down = feed(y_up), feed(y_down)
    hidden_copy(0, 1, 0).wait_recv()
    hidden_copy(1, 1, 1).wait_recv()
    lane = lax.broadcasted_iota(jnp.int32, (NX * NZ, 128), 1)
    table_copy = pltpu.make_async_copy(table, table_smem, table_sem.at[0])

    def slots_then_own():
        @pl.loop(0, NX * NZ)
        def _(row):
            pltpu.make_async_copy(cand_mine, cand_rows.at[row], cand_recv_sem.at[row]).wait()

        named = cand_rows[...].reshape(NX * NZ, 128)
        mine = jnp.logical_and(lax.shift_right_logical(named, 6) == doc, lax.bitwise_and(lane, 15) < 12)
        mine_f = jnp.where(mine, 1.0, 0.0)
        before = (
            lax.broadcasted_iota(jnp.int32, (128, 128), 0) < lax.broadcasted_iota(jnp.int32, (128, 128), 1)
        ).astype(F32).astype(BF16)
        rank = jnp.dot(mine_f.astype(BF16), before, preferred_element_type=F32)
        rows_table = jnp.zeros((NX * NZ, 128), jnp.int32)
        for slot in range(SLOTS):
            chosen = jnp.where(rank == float(slot), mine_f, 0.0)
            some = jnp.sum(chosen, axis=1, keepdims=True)
            place = jnp.sum(chosen * lane.astype(F32), axis=1, keepdims=True).astype(jnp.int32)
            which = jnp.sum(
                chosen * lax.bitwise_and(named, DOC_DEV - 1).astype(F32), axis=1, keepdims=True
            ).astype(jnp.int32)
            rows_table = jnp.where(lane == slot + 16, jnp.where(some > 0.5, place, 127), rows_table)
            rows_table = jnp.where(lane == slot, lax.bitwise_and(place, 15) * 2, rows_table)
            rows_table = jnp.where(lane == slot + 8, which, rows_table)
        table[...] = rows_table
        table_copy.start()
        return feed_own

    total_two, sent_three = reduce_rows(
        1, lambda: feed(y_far), lambda: feed_up, lambda: feed_down, slots_then_own
    )
    two = norm_rows(one.astype(F32) + total_two, gains[8:9, :]).astype(BF16)
    projected = jnp.dot(two, w_proj[...], preferred_element_type=F32)
    unit = projected * lax.rsqrt(jnp.sum(projected * projected, axis=-1, keepdims=True) + 1e-06)
    vectors[head] = unit.astype(BF16).reshape(3, 16, 128)

    half_doc = lax.div(z, 4)
    piece_rows = pl.ds(core * 12 + y * 3, 3)

    def spread_copy(offset):
        return pltpu.make_async_remote_copy(
            src_ref=vectors.at[head],
            dst_ref=near_queries.at[half_doc, piece_rows],
            send_sem=spread_send_sem.at[offset],
            recv_sem=spread_recv_sem.at[half_doc, y],
            device_id=(2 * home + core, x * NZ + mod(z + offset, NZ)),
            device_id_type=MESH,
        )

    def across_copy(half_index, source_y, offset, index):
        rows = pl.ds(core * 12 + source_y * 3, 3)
        return pltpu.make_async_remote_copy(
            src_ref=near_queries.at[half_index, rows],
            dst_ref=queries.at[index, rows],
            send_sem=across_send_sem.at[half_index, source_y, offset - 1],
            recv_sem=across_recv_sem.at[half_index, source_y, offset - 1],
            device_id=(head, mod(x + offset, NX) * NZ + z),
            device_id_type=MESH,
        )

    def share_copy(place, index):
        held = near_queries.at[place] if place < 2 else queries.at[index]
        rows = held.at[pl.ds(core * 12, 12)]
        return pltpu.make_async_remote_copy(
            src_ref=rows,
            dst_ref=rows,
            send_sem=share_send_sem.at[place],
            recv_sem=share_recv_sem.at[place],
            device_id=partner,
            device_id_type=MESH,
        )

    spread_local = pltpu.make_async_copy(
        vectors.at[head], near_queries.at[half_doc, piece_rows], spread_recv_sem.at[half_doc, y]
    )
    pl.when(at_home)(lambda: spread_local.start())
    pl.when(jnp.logical_not(at_home))(lambda: spread_copy(0).start())
    for offset in (4, 3, 5, 2, 6, 1, 7):
        spread_copy(offset).start()
    sent_four = []
    for i, device in enumerate(peers):
        copy = pltpu.make_async_remote_copy(
            src_ref=vectors.at[head],
            dst_ref=vectors.at[head],
            send_sem=vec_send_sem.at[i],
            recv_sem=vec_recv_sem.at[i],
            device_id=device,
            device_id_type=MESH,
        )
        copy.start()
        sent_four.append(copy)
    crossing = []
    shared = []
    ahead = mod(mod(y - x, NY) - z, NZ)
    near = jnp.where(jnp.logical_or(ahead <= 2, ahead >= 6), 0, 1)
    for step, half_index in (
        (0, near),
        (1, near),
        (3, near),
        (0, 1 - near),
        (2, near),
        (1, 1 - near),
        (3, 1 - near),
        (2, 1 - near),
    ):
        source_y = mod(y + step, NY)
        pltpu.make_async_copy(
            vectors.at[head],
            near_queries.at[half_index, pl.ds(core * 12 + source_y * 3, 3)],
            spread_recv_sem.at[half_index, source_y],
        ).wait()
        for offset in (2, 1, 3):
            crossing.append(across_copy(half_index, source_y, offset, x * 2 + half_index))
            crossing[-1].start()
    for half_index in range(2):
        shared.append(share_copy(half_index, x * 2 + half_index))
        shared[-1].start()
    for copy in sent_four:
        copy.wait_recv()
    outs = []
    for block in range(2 * NY):
        place = (block % 2) * 12 + (block // 2) * 3
        outs.append(
            pltpu.make_async_copy(vectors.at[block], query_out.at[pl.ds(place, 3)], load_sem.at[block])
        )
        outs[-1].start()
    table_copy.wait()
    loads[8].wait()

    zeros = jnp.zeros((QLEN, 128), BF16)
    row_index = lax.broadcasted_iota(jnp.int32, (256, 2 * QLEN), 0)
    first_lanes = lax.broadcasted_iota(jnp.int32, (1, 2 * QLEN), 1) < QLEN
    eight_lanes = lax.broadcasted_iota(jnp.int32, (8, 128), 1)

    def back_to(row):
        source_x, source_half, source_y = lax.div(row, 8), lax.rem(lax.div(row, NY), 2), lax.rem(row, NY)
        source = source_x * NZ + mod(y - source_x, NY) + 4 * source_half
        return source, source_y

    def back_copy(row):
        source, source_y = back_to(row)
        return pltpu.make_async_remote_copy(
            src_ref=back_send.at[row],
            dst_ref=back_recv.at[doc],
            send_sem=back_send_sem.at[row],
            recv_sem=back_recv_sem.at[doc],
            device_id=(2 * source_y + core, source),
            device_id_type=MESH,
        )

    def is_own(row):
        source, source_y = back_to(row)
        return jnp.logical_and(source == doc, source_y == y)

    def rate(source_x, local):
        base = source_x * 8

        @pl.loop(0, 8 // ROWS)
        def _(step):
            first = base + step * ROWS
            held = near_queries.at[step] if local else queries.at[lax.div(first, NY)]
            for row, pair in [(first + i, pair) for i in range(ROWS) for pair in range(SLOTS // 2)]:
                found = []
                for slot in (2 * pair, 2 * pair + 1):
                    which = jnp.clip(table_smem[row, slot + 8], 0, DOC_DEV - 1)
                    request = jnp.clip(table_smem[row, slot], 0, 22)
                    query = jnp.concatenate([held[request], held[request + 1]], axis=0)
                    found.append((docs[which], query, lengths_ref[which]))
                (doc_a, query_a, len_a), (doc_b, query_b, len_b) = found
                left = jnp.concatenate([doc_a, doc_b], axis=1)
                right = jnp.concatenate(
                    [
                        jnp.concatenate([query_a, zeros], axis=1),
                        jnp.concatenate([zeros, query_b], axis=1),
                    ],
                    axis=0,
                )
                sims = lax.dot_general(left, right, NT, preferred_element_type=F32)
                live = row_index < jnp.where(first_lanes, len_a, len_b)
                best_rows[pair, pl.ds(row, 1), : 2 * QLEN] = jnp.max(
                    jnp.where(live, sims, -jnp.inf), axis=0, keepdims=True
                )

        eight = pl.ds(pl.multiple_of(base, 8), 8)
        spots = table[eight, :]
        rated = jnp.zeros((8, 128), F32)
        for slot in range(SLOTS):
            low = (slot % 2) * QLEN
            value = jnp.sum(best_rows[slot // 2, eight, low : low + QLEN], axis=1, keepdims=True)
            rated = rated + jnp.where(eight_lanes == spots[:, slot + 16 : slot + 17], value, 0.0)
        back_send[pl.ds(base, 8)] = rated.reshape(8, 1, 128)

    def send_back(source_x, local):
        for step in (2, 1, 3, 0):
            for half_index in range(2):
                row = source_x * 8 + half_index * NY + mod(y + step, NY)
                if local and step == 0:
                    own_row = is_own(row)
                    pl.when(own_row)(
                        lambda row=row: pltpu.make_async_copy(
                            back_send.at[row], back_recv.at[doc], back_recv_sem.at[doc]
                        ).start()
                    )
                    pl.when(jnp.logical_not(own_row))(lambda row=row: back_copy(row).start())
                else:
                    back_copy(row).start()

    for copy in shared:
        copy.wait_recv()
    rate(x, True)
    send_back(x, True)
    for offset in (1, 3, 2):
        for half_index in range(2):
            index = mod(x - offset, NX) * 2 + half_index
            for source_y in range(NY):
                across_copy(half_index, source_y, offset, index).wait_recv()
            shared.append(share_copy(2 * offset + half_index, index))
            shared[-1].start()
    for copy in shared[2:]:
        copy.wait_recv()
    for offset in (2, 1, 3):
        rate(mod(x - offset, NX), False)
        send_back(mod(x - offset, NX), False)

    @pl.loop(0, NX * NZ)
    def _(row):
        pltpu.make_async_copy(back_send.at[0], back_recv.at[row], back_recv_sem.at[row]).wait()

    answer = jnp.broadcast_to(jnp.sum(back_recv[...], axis=0), (8, 128))
    spot = lax.broadcasted_iota(jnp.int32, (8, 128), 0)
    turned = answer
    for i in range(1, 8):
        turned = jnp.where(spot == i, pltpu.roll(answer, 128 - 16 * i, 1), turned)
    score_tile[...] = turned[:, : score_tile.shape[1]]
    outs.append(pltpu.make_async_copy(score_tile, score_out, load_sem.at[8]))
    outs[-1].start()
    for copy in outs:
        copy.wait()

    @pl.loop(0, NX * NZ)
    def _(row):
        pl.when(jnp.logical_not(is_own(row)))(lambda: back_copy(row).wait_send())

    pl.when(jnp.logical_not(at_home))(lambda: cand_copy(0).wait_send())
    pl.loop(1, NX * NZ)(lambda offset: cand_copy(offset).wait_send())
    pl.when(jnp.logical_not(at_home))(lambda: spread_copy(0).wait_send())
    for offset in range(1, NZ):
        spread_copy(offset).wait_send()
    for copy in list(copies.values()) + swaps + [att_copy] + sent_one + sent_two + sent_three + sent_four + crossing + shared:
        copy.wait_send()


def encode(tokens, w_qkv, w_out, w_up, w_down, gain_one, gain_two, rel_table, prompt_cache, w_proj, docs, lengths, named, group_ids):
    plan = plan_gather()
    rows, width = tokens.shape
    half = rows // 2
    part = half // NY
    anywhere = pl.BlockSpec(memory_space=pl.ANY)
    dma = pltpu.SemaphoreType.DMA
    return pl.pallas_call(
        functools.partial(encoder_kernel, plan),
        out_shape=(
            jax.ShapeDtypeStruct((rows // 16, 16, 128), BF16),
            jax.ShapeDtypeStruct(named.shape, F32),
        ),
        in_specs=[anywhere] * 14,
        out_specs=(anywhere, anywhere),
        scratch_shapes=[
            pltpu.SMEM(group_ids.shape, jnp.int32),
            pltpu.VMEM((16, width), F32),
            pltpu.VMEM((width, 128), BF16),
            pltpu.SMEM(lengths.shape, jnp.int32),
            pltpu.VMEM(named.shape, jnp.int32),
            pltpu.VMEM((8, 128), jnp.int32),
            pltpu.VMEM((1, 128), jnp.int32),
            pltpu.VMEM(named.shape, F32),
            pltpu.VMEM((2, 64, PLEN, 128), BF16),
            pltpu.VMEM((rows, width), BF16),
            pltpu.VMEM((3, width, 128), BF16),
            pltpu.VMEM((2, 128, width), BF16),
            pltpu.VMEM((2, width, 512), BF16),
            pltpu.VMEM((2, 512, width), BF16),
            pltpu.VMEM((2, 128, width), BF16),
            pltpu.VMEM((2, rows, 128), BF16),
            pltpu.VMEM((rows, 128), BF16),
            pltpu.VMEM((rows, 128), BF16),
            pltpu.VMEM((rows, 256), F32),
            pltpu.VMEM((2, 256, 128), BF16),
            pltpu.VMEM((2, half, 128), BF16),
            pltpu.VMEM((half, 128), BF16),
            pltpu.VMEM((2, 2, part, 512), BF16),
            pltpu.VMEM((2, 2, 2, part, 512), BF16),
            pltpu.VMEM((2, 2, part, 512), BF16),
            pltpu.VMEM((2, 2, 2, part, 512), BF16),
            pltpu.VMEM((NY, 2, part, 512), BF16),
            pltpu.VMEM((2 * NY, 3, 16, 128), BF16),
            dma((15,)),
            dma((len(plan),)),
            dma((len(plan),)),
            dma((3,)),
            dma((3,)),
            dma((2,)),
            dma((2, 2)),
            dma((2, 2)),
            dma((2, 2, 2)),
            dma((2, 2, 2)),
            dma((2, 2, 2)),
            dma((2, 2, 2)),
            dma((7,)),
            dma((7,)),
            pltpu.VMEM((64, 256, 128), BF16),
            pltpu.VMEM((8, 24, 16, 128), BF16),
            pltpu.VMEM((2, 24, 16, 128), BF16),
            pltpu.VMEM((32, 1, 128), jnp.int32),
            pltpu.VMEM((32, 128), jnp.int32),
            pltpu.SMEM((32, 128), jnp.int32),
            pltpu.VMEM((SLOTS // 2, 32, 128), F32),
            pltpu.VMEM((32, 1, 128), F32),
            pltpu.VMEM((32, 1, 128), F32),
            dma((1,)),
            dma((32,)),
            dma((32,)),
            dma((8,)),
            dma((2, 4)),
            dma((2, 4, 3)),
            dma((2, 4, 3)),
            dma((8,)),
            dma((8,)),
            dma((32,)),
            dma((32,)),
        ],
        compiler_params=pltpu.CompilerParams(collective_id=0, has_side_effects=True),
        name="encoder",
    )(
        group_ids,
        tokens,
        jnp.transpose(w_qkv, (1, 0, 2)),
        w_out,
        w_up,
        w_down,
        gain_one.reshape(1, -1),
        gain_two.reshape(1, -1),
        rel_table,
        prompt_cache.reshape(2, 2, PLEN, 128),
        w_proj,
        docs,
        lengths,
        named,
    )


def body(
    tokens,
    w_qkv,
    w_out,
    w_up,
    w_down,
    gain_one,
    gain_two,
    rel_table,
    prompt_cache,
    w_proj,
    doc_vectors,
    doc_lengths,
    group_ids,
    candidates,
):
    query_vectors, rated = encode(
        tokens,
        w_qkv,
        w_out,
        w_up,
        w_down,
        gain_one,
        gain_two,
        rel_table,
        prompt_cache,
        w_proj,
        doc_vectors,
        doc_lengths,
        candidates.T,
        group_ids,
    )
    return (query_vectors.reshape(tokens.shape[0], 128), rated.T)


def solution(mesh):
    placed = (
        P("doc", None),
        P(None, None, "head"),
        P("head", None),
        P(None, "head"),
        P("head", None),
        P(),
        P(),
        P(),
        P(None, "doc", "head"),
        P(),
        P("doc", None, None),
        P("doc"),
        P("doc"),
        P("doc", "head"),
    )
    return jax.shard_map(
        body,
        mesh=mesh,
        in_specs=placed,
        out_specs=(P("doc", None), P("doc", "head")),
        check_vma=False,
    )
```

```python
import functools
import math

import jax
import jax.numpy as jnp
from jax import lax
from jax.experimental import pallas as pl
from jax.experimental.pallas import tpu as pltpu
from jax.sharding import PartitionSpec as P

HD = 64
RELS = 512
QLEN = 32
PLEN = 64
DOC_DEV = 64
NX = 4
NZ = 8
NY = 4
SLOTS = 6
ROWS = 4
MESH = pl.DeviceIdType.MESH
F32 = jnp.float32
BF16 = jnp.bfloat16
NT = (((1,), (1,)), ((), ()))


def mod(value, size):
    return lax.rem(value + 4 * size, size)


HOP_US = 2.3
ROUTE_US = 0.65
ROWS_US = 256 / 46500.0
Z_FIRST = ((0, 0, 128),)
X_FIRST = ((1, 0, 128),)


class Message:
    def __init__(self, kv, axis, sign, hops, dx, dz, low, rows, parent):
        self.kv, self.axis, self.sign, self.hops = kv, axis, sign, hops
        self.dx, self.dz, self.low, self.rows, self.parent = dx, dz, low, rows, parent
        self.children = []
        self.time = None
        self.index = None


def plan_gather():
    made = []

    def add(*fields):
        made.append(Message(*fields))
        return made[-1]

    def along_x(kv, dz, low, rows, parent, direct):
        out = []
        half = rows // 2
        for sign in (1, -1):
            near = add(kv, "x", sign, 1, sign, dz, low, rows, parent)
            part = low if sign > 0 else low + half
            hops = 2 if direct else 1
            out += [near, add(kv, "x", sign, hops, 2 * sign, dz, part, half, parent if direct else near)]
        return out

    def along_z(kv, dx, low, rows, parent, jump):
        out = []
        half = rows // 2
        for sign in (1, -1):
            one = add(kv, "z", sign, 1, dx, sign, low, rows, parent)
            two = add(kv, "z", sign, 2 if jump else 1, dx, 2 * sign, low, rows, parent if jump else one)
            three = add(kv, "z", sign, 1, dx, 3 * sign, low, rows, two)
            part = low if sign > 0 else low + half
            out += [one, two, three, add(kv, "z", sign, 1, dx, 4 * sign, part, half, three)]
        return out

    for kv, low, rows in Z_FIRST:
        firsts = along_z(kv, 0, low, rows, None, True)
        along_x(kv, 0, low, rows, None, False)
        for first in firsts:
            along_x(kv, first.dz, first.low, first.rows, first, abs(first.dz) == 4)
    for kv, low, rows in X_FIRST:
        firsts = along_x(kv, 0, low, rows, None, True)
        along_z(kv, 0, low, rows, None, False)
        for first in firsts:
            along_z(kv, first.dx, first.low, first.rows, first, False)
    for message in made:
        if message.parent is not None:
            message.parent.children.append(message)
    free = {}
    ready = [(0.0, i) for i, m in enumerate(made) if m.parent is None]
    while ready:
        ready.sort()
        start, i = ready.pop(0)
        message = made[i]
        link = (message.axis, message.sign)
        free[link] = max(start, free.get(link, 0.0)) + message.rows * ROWS_US * message.hops
        message.time = free[link] + HOP_US + ROUTE_US * (message.hops - 1)
        ready += [(message.time, made.index(child)) for child in message.children]
    order = sorted(made, key=lambda m: m.time)
    for index, message in enumerate(order):
        message.index = index
    return order


def norm_rows(values, gain):
    centre = values - jnp.mean(values, axis=-1, keepdims=True)
    spread = jnp.mean(centre * centre, axis=-1, keepdims=True)
    return centre * lax.rsqrt(spread + 1e-07) * gain


def gelu(values):
    return 0.5 * values * (1.0 + lax.erf(values * (1.0 / math.sqrt(2.0))))


def encoder_kernel(
    plan,
    group_hbm,
    tokens_hbm,
    w_qkv_hbm,
    w_out_hbm,
    w_up_hbm,
    w_down_hbm,
    gain_one_hbm,
    gain_two_hbm,
    rel_hbm,
    cache_hbm,
    w_proj_hbm,
    docs_hbm,
    lengths_hbm,
    cand_hbm,
    query_out,
    score_out,
    group_ref,
    gains,
    w_proj,
    lengths_ref,
    cand_tile,
    cand_wide,
    cand_mine,
    score_tile,
    cache_keys,
    cache_values,
    prob,
    sums,
    tokens,
    w_qkv,
    w_out,
    w_up,
    w_down,
    rel,
    q_mask,
    k_own,
    v_own,
    q_rel,
    rel_two,
    att,
    att_send,
    opp_send,
    side_send,
    opp_recv,
    side_recv,
    hidden,
    vectors,
    load_sem,
    gather_send,
    gather_recv,
    swap_send,
    swap_recv,
    att_sem,
    opp_send_sem,
    opp_recv_sem,
    side_send_sem,
    side_recv_sem,
    hid_send_sem,
    hid_recv_sem,
    vec_send_sem,
    vec_recv_sem,
    docs,
    queries,
    near_queries,
    cand_rows,
    table,
    table_smem,
    best_rows,
    back_send,
    back_recv,
    table_sem,
    cand_send_sem,
    cand_recv_sem,
    spread_send_sem,
    spread_recv_sem,
    across_send_sem,
    across_recv_sem,
    share_send_sem,
    share_recv_sem,
    back_send_sem,
    back_recv_sem,
):
    head = lax.axis_index("head")
    doc = lax.axis_index("doc")
    y, core = lax.div(head, 2), lax.rem(head, 2)
    x, z = lax.div(doc, NZ), lax.rem(doc, NZ)
    partner = (2 * y + 1 - core, doc)
    y_up, y_down = mod(y + 1, NY), mod(y - 1, NY)
    y_far = mod(y + 2, NY)

    def at_y(other):
        return (2 * other + core, doc)

    def at_link(axis, sign):
        if axis == "x":
            return (head, mod(x + sign, NX) * NZ + z)
        return (head, x * NZ + mod(z + sign, NZ))

    peers = [partner]
    for other in (y_up, y_down, y_far):
        peers += [(2 * other + core, doc), (2 * other + 1 - core, doc)]
    links = [at_link(axis, sign * hops) for axis in ("x", "z") for sign in (1, -1) for hops in (1, 2)]
    barrier = pltpu.get_barrier_semaphore()
    for device in peers + links:
        pl.semaphore_signal(barrier, inc=1, device_id=device, device_id_type=MESH)

    loads = [
        pltpu.make_async_copy(tokens_hbm, tokens, load_sem.at[0]),
        pltpu.make_async_copy(w_qkv_hbm, w_qkv, load_sem.at[1]),
        pltpu.make_async_copy(rel_hbm.at[pl.ds(RELS // 2 - 96, 128)], rel.at[0], load_sem.at[2]),
        pltpu.make_async_copy(rel_hbm.at[pl.ds(RELS // 2 - 32, 128)], rel.at[1], load_sem.at[3]),
        pltpu.make_async_copy(cache_hbm.at[0], cache_keys.at[pl.ds(doc * 2, 2)], load_sem.at[4]),
        pltpu.make_async_copy(w_out_hbm, w_out.at[core], load_sem.at[5]),
        pltpu.make_async_copy(w_up_hbm, w_up.at[core], load_sem.at[6]),
        pltpu.make_async_copy(w_down_hbm, w_down.at[core], load_sem.at[7]),
        pltpu.make_async_copy(docs_hbm, docs, load_sem.at[8]),
        pltpu.make_async_copy(gain_one_hbm, gains.at[pl.ds(0, 1)], load_sem.at[9]),
        pltpu.make_async_copy(gain_two_hbm, gains.at[pl.ds(8, 1)], load_sem.at[10]),
        pltpu.make_async_copy(w_proj_hbm, w_proj, load_sem.at[11]),
        pltpu.make_async_copy(lengths_hbm, lengths_ref, load_sem.at[12]),
        pltpu.make_async_copy(cand_hbm, cand_tile, load_sem.at[13]),
        pltpu.make_async_copy(group_hbm, group_ref, load_sem.at[14]),
        pltpu.make_async_copy(cache_hbm.at[1], cache_values.at[pl.ds(doc * 2, 2)], load_sem.at[15]),
    ]
    for load in loads:
        load.start()
    pl.semaphore_wait(barrier, len(peers) + len(links))

    def gather_copy(message):
        dx, dz = message.dx, message.dz
        if message.axis == "x":
            dx -= message.sign * message.hops
        else:
            dz -= message.sign * message.hops
        block = mod(x - dx, NX) * NZ + mod(z - dz, NZ)
        group, low = block * 2 + message.low // PLEN, message.low % PLEN
        held = cache_values if message.kv else cache_keys
        if message.rows == 2 * PLEN:
            target = held.at[pl.ds(group, 2)]
        else:
            target = held.at[group, pl.ds(low, message.rows)]
        source = target
        if message.parent is None:
            source = cache_hbm.at[message.kv]
            if message.rows < 2 * PLEN:
                source = source.at[message.low // PLEN, pl.ds(low, message.rows)]
        return pltpu.make_async_remote_copy(
            src_ref=source,
            dst_ref=target,
            send_sem=gather_send.at[message.index],
            recv_sem=gather_recv.at[message.index],
            device_id=at_link(message.axis, message.sign * message.hops),
            device_id_type=MESH,
        )

    copies = {message.index: gather_copy(message) for message in plan}
    for message in plan:
        if message.parent is None:
            copies[message.index].start()

    swaps = []
    for i, (source, target) in enumerate(((w_out_hbm, w_out), (w_up_hbm, w_up), (w_down_hbm, w_down))):
        swaps.append(
            pltpu.make_async_remote_copy(
                src_ref=source,
                dst_ref=target.at[core],
                send_sem=swap_send.at[i],
                recv_sem=swap_recv.at[i],
                device_id=partner,
                device_id_type=MESH,
            )
        )
        swaps[-1].start()

    loads[0].wait()
    loads[1].wait()
    low_head = lax.broadcasted_iota(jnp.int32, (128, 128), 1) < HD
    for block in range(3):
        rows = slice(block * 128, block * 128 + 128)
        q_made, k_made, v_made = (
            jnp.dot(tokens[rows, :], w_qkv[i], preferred_element_type=F32) for i in range(3)
        )
        q_mask[0, rows, :] = jnp.where(low_head, q_made, 0.0).astype(BF16)
        q_mask[1, rows, :] = jnp.where(low_head, 0.0, q_made).astype(BF16)
        k_own[rows, :] = k_made.astype(BF16)
        v_own[rows, :] = v_made.astype(BF16)
    loads[2].wait()
    loads[3].wait()
    flip = (
        lax.broadcasted_iota(jnp.int32, (128, 128), 0) + lax.broadcasted_iota(jnp.int32, (128, 128), 1)
        == 127
    ).astype(F32).astype(BF16)
    for i in range(2):
        row = jnp.dot(
            rel[i], w_qkv[i], preferred_element_type=F32
        ).astype(BF16)
        turned = jnp.dot(flip, row, preferred_element_type=F32)
        rel_two[i, 0:128, :] = jnp.where(low_head, turned, 0.0).astype(BF16)
        rel_two[i, 128:256, :] = jnp.where(low_head, 0.0, turned).astype(BF16)
    for block in range(3):
        rows = slice(block * 128, block * 128 + 128)
        q_all = q_mask[0, rows, :] + q_mask[1, rows, :]
        q_rel[rows, :] = lax.dot_general(q_all, rel_two[1], NT, preferred_element_type=F32)
    loads[4].wait()
    for i in range(9, 16):
        loads[i].wait()
    cand_wide[...] = jnp.zeros_like(cand_wide)
    cand_wide[:, : cand_tile.shape[1]] = cand_tile[...]
    cand_mine[...] = jnp.sum(pltpu.roll(cand_wide[...], 0, 1, stride=16, stride_axis=0), axis=0, keepdims=True)

    for message in plan:
        if message.children:
            copies[message.index].wait_recv()
        for child in message.children:
            copies[child.index].start()
    for message in plan:
        if message.kv == 0 and not message.children:
            copies[message.index].wait_recv()

    low_lane = lax.broadcasted_iota(jnp.int32, (96, 128), 1) < QLEN
    low_half = lax.broadcasted_iota(jnp.int32, (QLEN, 128), 1) < HD

    def weigh(place, request):
        group = group_ref[request]
        own = pl.ds(pl.multiple_of(request * QLEN, QLEN), QLEN)
        keys = jnp.concatenate([cache_keys[group], k_own[own, :]], axis=0)
        query = jnp.concatenate([q_mask[0, own, :], q_mask[1, own, :]], axis=0)
        content = lax.dot_general(query, keys, NT, preferred_element_type=F32)
        key_rel = lax.dot_general(keys, rel_two[0], NT, preferred_element_type=F32)
        first = pltpu.roll(key_rel[:, :128], 33, 1, stride=1, stride_axis=0)
        second = pltpu.roll(key_rel[:, 128:], 65, 1, stride=1, stride_axis=0)
        p2c = jnp.transpose(jnp.where(low_lane, first, second))[: 2 * QLEN, :]
        mine = q_rel[own, :]
        c2p = jnp.concatenate(
            [
                pltpu.roll(mine[:, :128], 97, 1, stride=1, stride_axis=0),
                pltpu.roll(mine[:, 128:], 97, 1, stride=1, stride_axis=0),
            ],
            axis=0,
        )[:, :96]
        logits = (content + c2p + p2c) * (1.0 / math.sqrt(3 * HD))
        weights = jnp.exp(logits - jnp.max(logits, axis=-1, keepdims=True))
        total = jnp.sum(weights, axis=-1, keepdims=True)
        prob[place, :, : PLEN + QLEN] = weights.astype(BF16)
        sums[place] = jnp.broadcast_to(total, (2 * QLEN, 128))

    def blend(place, request):
        own = pl.ds(pl.multiple_of(request * QLEN, QLEN), QLEN)
        values = jnp.concatenate([cache_values[group_ref[request]], v_own[own, :]], axis=0)
        out = jnp.dot(prob[place, :, : PLEN + QLEN], values, preferred_element_type=F32) / sums[place]
        return jnp.where(low_half, out[:QLEN], out[QLEN:]).astype(BF16)

    half = tokens.shape[0] // 2
    per_core = half // QLEN
    for i in range(per_core):
        weigh(i, (1 - core) * per_core + i)
        weigh(per_core + i, core * per_core + i)
    for message in plan:
        if message.kv == 1 and not message.children:
            copies[message.index].wait_recv()
    for i in range(per_core):
        att_send[i * QLEN : i * QLEN + QLEN, :] = blend(i, (1 - core) * per_core + i)
    att_copy = pltpu.make_async_remote_copy(
        src_ref=att_send,
        dst_ref=att.at[core],
        send_sem=att_sem.at[0],
        recv_sem=att_sem.at[1],
        device_id=partner,
        device_id_type=MESH,
    )
    att_copy.start()
    for i in range(per_core):
        att[core, i * QLEN : i * QLEN + QLEN, :] = blend(per_core + i, core * per_core + i)
    att_copy.wait_recv()
    loads[5].wait()
    swaps[0].wait_recv()
    part = half // NY

    def chunk_rows(other):
        return pl.ds(pl.multiple_of(other * part, 16), part)

    def out_part(other):
        rows = chunk_rows(other)
        return jnp.dot(att[0, rows, :], w_out[0], preferred_element_type=F32) + jnp.dot(
            att[1, rows, :], w_out[1], preferred_element_type=F32
        )

    def side_copy(phase, side, piece):
        return pltpu.make_async_remote_copy(
            src_ref=side_send.at[phase, side, piece],
            dst_ref=side_recv.at[phase, side, piece],
            send_sem=side_send_sem.at[phase, side, piece],
            recv_sem=side_recv_sem.at[phase, side, piece],
            device_id=at_y(y_down if side else y_up),
            device_id_type=MESH,
        )

    def far_copy(phase, piece):
        return pltpu.make_async_remote_copy(
            src_ref=opp_send.at[phase, piece],
            dst_ref=opp_recv.at[phase, piece],
            send_sem=opp_send_sem.at[phase, piece],
            recv_sem=opp_recv_sem.at[phase, piece],
            device_id=at_y(y_down if piece else y_up),
            device_id_type=MESH,
        )

    wide = 512

    def reduce_rows(phase, far, up, down, own):
        sent = []
        share = far()
        for piece in range(2):
            opp_send[phase, piece] = share[:, piece * wide : piece * wide + wide].astype(BF16)
            copy = far_copy(phase, piece)
            copy.start()
            sent.append(copy)
        share_up, share_down = up(), down()
        side_send[phase, 0, 1] = share_up[:, wide:].astype(BF16)
        side_send[phase, 1, 0] = share_down[:, :wide].astype(BF16)
        for side, piece in ((0, 1), (1, 0)):
            copy = side_copy(phase, side, piece)
            copy.start()
            sent.append(copy)
        share_own = own()
        far_copy(phase, 0).wait_recv()
        side_send[phase, 0, 0] = (share_up[:, :wide] + opp_recv[phase, 0].astype(F32)).astype(BF16)
        copy = side_copy(phase, 0, 0)
        copy.start()
        sent.append(copy)
        far_copy(phase, 1).wait_recv()
        side_send[phase, 1, 1] = (share_down[:, wide:] + opp_recv[phase, 1].astype(F32)).astype(BF16)
        copy = side_copy(phase, 1, 1)
        copy.start()
        sent.append(copy)
        for side, piece in ((0, 1), (1, 0), (0, 0), (1, 1)):
            side_copy(phase, side, piece).wait_recv()
        halves = [
            share_own[:, piece * wide : piece * wide + wide]
            + side_recv[phase, 0, piece].astype(F32)
            + side_recv[phase, 1, piece].astype(F32)
            for piece in range(2)
        ]
        return jnp.concatenate(halves, axis=1), sent

    total, sent_one = reduce_rows(
        0,
        lambda: out_part(y_far),
        lambda: out_part(y_up),
        lambda: out_part(y_down),
        lambda: out_part(y),
    )
    own_rows = pl.ds(pl.multiple_of(core * half + y * part, 16), part)
    one = norm_rows(tokens[own_rows, :].astype(F32) + total, gains[0:1, :]).astype(BF16)
    for piece in range(2):
        hidden[y, piece] = one[:, piece * wide : piece * wide + wide]

    def hidden_copy(side, hop, piece):
        block = y if hop == 0 else (y_up if side else y_down)
        return pltpu.make_async_remote_copy(
            src_ref=hidden.at[block, piece],
            dst_ref=hidden.at[block, piece],
            send_sem=hid_send_sem.at[side, hop, piece],
            recv_sem=hid_recv_sem.at[side, hop, piece],
            device_id=at_y(y_down if side else y_up),
            device_id_type=MESH,
        )

    sent_two = []

    def send_hidden(side, hop, piece):
        copy = hidden_copy(side, hop, piece)
        copy.start()
        sent_two.append(copy)

    send_hidden(0, 0, 0)
    send_hidden(1, 0, 1)
    send_hidden(0, 0, 1)
    send_hidden(1, 0, 0)
    home = mod(x + z, NY)
    at_home = home == y
    my_row = (x * 2 + lax.div(z, 4)) * NY + y

    def cand_copy(offset):
        return pltpu.make_async_remote_copy(
            src_ref=cand_mine,
            dst_ref=cand_rows.at[my_row],
            send_sem=cand_send_sem.at[offset],
            recv_sem=cand_recv_sem.at[my_row],
            device_id=(2 * home + core, mod(doc + offset, NX * NZ)),
            device_id_type=MESH,
        )

    cand_local = pltpu.make_async_copy(cand_mine, cand_rows.at[my_row], cand_recv_sem.at[my_row])
    for i in (6, 7):
        loads[i].wait()
    swaps[1].wait_recv()
    swaps[2].wait_recv()

    def feed(other):
        rows = jnp.concatenate([hidden[other, 0], hidden[other, 1]], axis=1)
        made = None
        for i in range(2):
            inner = gelu(jnp.dot(rows, w_up[i], preferred_element_type=F32)).astype(BF16)
            term = jnp.dot(inner, w_down[i], preferred_element_type=F32)
            made = term if made is None else made + term
        return made

    feed_own = feed(y)
    pl.when(at_home)(lambda: cand_local.start())
    pl.when(jnp.logical_not(at_home))(lambda: cand_copy(0).start())
    pl.loop(1, NX * NZ)(lambda offset: cand_copy(offset).start())
    hidden_copy(0, 0, 0).wait_recv()
    send_hidden(0, 1, 0)
    hidden_copy(1, 0, 1).wait_recv()
    send_hidden(1, 1, 1)
    hidden_copy(0, 0, 1).wait_recv()
    hidden_copy(1, 0, 0).wait_recv()
    feed_up, feed_down = feed(y_up), feed(y_down)
    hidden_copy(0, 1, 0).wait_recv()
    hidden_copy(1, 1, 1).wait_recv()
    lane = lax.broadcasted_iota(jnp.int32, (NX * NZ, 128), 1)
    table_copy = pltpu.make_async_copy(table, table_smem, table_sem.at[0])

    def slots_then_own():
        @pl.loop(0, NX * NZ)
        def _(row):
            pltpu.make_async_copy(cand_mine, cand_rows.at[row], cand_recv_sem.at[row]).wait()

        named = cand_rows[...].reshape(NX * NZ, 128)
        mine = jnp.logical_and(lax.shift_right_logical(named, 6) == doc, lax.bitwise_and(lane, 15) < 12)
        mine_f = jnp.where(mine, 1.0, 0.0)
        before = (
            lax.broadcasted_iota(jnp.int32, (128, 128), 0) < lax.broadcasted_iota(jnp.int32, (128, 128), 1)
        ).astype(F32).astype(BF16)
        rank = jnp.dot(mine_f.astype(BF16), before, preferred_element_type=F32)
        rows_table = jnp.zeros((NX * NZ, 128), jnp.int32)
        for slot in range(SLOTS):
            chosen = jnp.where(rank == float(slot), mine_f, 0.0)
            some = jnp.sum(chosen, axis=1, keepdims=True)
            place = jnp.sum(chosen * lane.astype(F32), axis=1, keepdims=True).astype(jnp.int32)
            which = jnp.sum(
                chosen * lax.bitwise_and(named, DOC_DEV - 1).astype(F32), axis=1, keepdims=True
            ).astype(jnp.int32)
            rows_table = jnp.where(lane == slot + 16, jnp.where(some > 0.5, place, 127), rows_table)
            rows_table = jnp.where(lane == slot, lax.bitwise_and(place, 15) * 2, rows_table)
            rows_table = jnp.where(lane == slot + 8, which, rows_table)
        table[...] = rows_table
        table_copy.start()
        return feed_own

    total_two, sent_three = reduce_rows(
        1, lambda: feed(y_far), lambda: feed_up, lambda: feed_down, slots_then_own
    )
    two = norm_rows(one.astype(F32) + total_two, gains[8:9, :]).astype(BF16)
    projected = jnp.dot(two, w_proj[...], preferred_element_type=F32)
    unit = projected * lax.rsqrt(jnp.sum(projected * projected, axis=-1, keepdims=True) + 1e-06)
    vectors[head] = unit.astype(BF16).reshape(3, 16, 128)

    half_doc = lax.div(z, 4)
    piece_rows = pl.ds(core * 12 + y * 3, 3)

    def spread_copy(offset):
        return pltpu.make_async_remote_copy(
            src_ref=vectors.at[head],
            dst_ref=near_queries.at[half_doc, piece_rows],
            send_sem=spread_send_sem.at[offset],
            recv_sem=spread_recv_sem.at[half_doc, y],
            device_id=(2 * home + core, x * NZ + mod(z + offset, NZ)),
            device_id_type=MESH,
        )

    def across_copy(half_index, source_y, offset, index):
        rows = pl.ds(core * 12 + source_y * 3, 3)
        return pltpu.make_async_remote_copy(
            src_ref=near_queries.at[half_index, rows],
            dst_ref=queries.at[index, rows],
            send_sem=across_send_sem.at[half_index, source_y, offset - 1],
            recv_sem=across_recv_sem.at[half_index, source_y, offset - 1],
            device_id=(head, mod(x + offset, NX) * NZ + z),
            device_id_type=MESH,
        )

    def share_copy(place, index):
        held = near_queries.at[place] if place < 2 else queries.at[index]
        rows = held.at[pl.ds(core * 12, 12)]
        return pltpu.make_async_remote_copy(
            src_ref=rows,
            dst_ref=rows,
            send_sem=share_send_sem.at[place],
            recv_sem=share_recv_sem.at[place],
            device_id=partner,
            device_id_type=MESH,
        )

    spread_local = pltpu.make_async_copy(
        vectors.at[head], near_queries.at[half_doc, piece_rows], spread_recv_sem.at[half_doc, y]
    )
    pl.when(at_home)(lambda: spread_local.start())
    pl.when(jnp.logical_not(at_home))(lambda: spread_copy(0).start())
    for offset in (4, 3, 5, 2, 6, 1, 7):
        spread_copy(offset).start()
    sent_four = []
    for i, device in enumerate(peers):
        copy = pltpu.make_async_remote_copy(
            src_ref=vectors.at[head],
            dst_ref=vectors.at[head],
            send_sem=vec_send_sem.at[i],
            recv_sem=vec_recv_sem.at[i],
            device_id=device,
            device_id_type=MESH,
        )
        copy.start()
        sent_four.append(copy)
    crossing = []
    shared = []
    ahead = mod(mod(y - x, NY) - z, NZ)
    near = jnp.where(jnp.logical_or(ahead <= 2, ahead >= 6), 0, 1)
    for step, half_index in (
        (0, near),
        (1, near),
        (3, near),
        (0, 1 - near),
        (2, near),
        (1, 1 - near),
        (3, 1 - near),
        (2, 1 - near),
    ):
        source_y = mod(y + step, NY)
        pltpu.make_async_copy(
            vectors.at[head],
            near_queries.at[half_index, pl.ds(core * 12 + source_y * 3, 3)],
            spread_recv_sem.at[half_index, source_y],
        ).wait()
        for offset in (2, 1, 3):
            crossing.append(across_copy(half_index, source_y, offset, x * 2 + half_index))
            crossing[-1].start()
    for half_index in range(2):
        shared.append(share_copy(half_index, x * 2 + half_index))
        shared[-1].start()
    for copy in sent_four:
        copy.wait_recv()
    outs = []
    for block in range(2 * NY):
        place = (block % 2) * 12 + (block // 2) * 3
        outs.append(
            pltpu.make_async_copy(vectors.at[block], query_out.at[pl.ds(place, 3)], load_sem.at[block])
        )
        outs[-1].start()
    table_copy.wait()
    loads[8].wait()

    zeros = jnp.zeros((QLEN, 128), BF16)
    row_index = lax.broadcasted_iota(jnp.int32, (256, 2 * QLEN), 0)
    first_lanes = lax.broadcasted_iota(jnp.int32, (1, 2 * QLEN), 1) < QLEN
    eight_lanes = lax.broadcasted_iota(jnp.int32, (8, 128), 1)

    def back_to(row):
        source_x, source_half, source_y = lax.div(row, 8), lax.rem(lax.div(row, NY), 2), lax.rem(row, NY)
        source = source_x * NZ + mod(y - source_x, NY) + 4 * source_half
        return source, source_y

    def back_copy(row):
        source, source_y = back_to(row)
        return pltpu.make_async_remote_copy(
            src_ref=back_send.at[row],
            dst_ref=back_recv.at[doc],
            send_sem=back_send_sem.at[row],
            recv_sem=back_recv_sem.at[doc],
            device_id=(2 * source_y + core, source),
            device_id_type=MESH,
        )

    def is_own(row):
        source, source_y = back_to(row)
        return jnp.logical_and(source == doc, source_y == y)

    def rate(source_x, local):
        base = source_x * 8

        @pl.loop(0, 8 // ROWS)
        def _(step):
            first = base + step * ROWS
            held = near_queries.at[step] if local else queries.at[lax.div(first, NY)]
            for row, pair in [(first + i, pair) for i in range(ROWS) for pair in range(SLOTS // 2)]:
                found = []
                for slot in (2 * pair, 2 * pair + 1):
                    which = jnp.clip(table_smem[row, slot + 8], 0, DOC_DEV - 1)
                    request = jnp.clip(table_smem[row, slot], 0, 22)
                    query = jnp.concatenate([held[request], held[request + 1]], axis=0)
                    found.append((docs[which], query, lengths_ref[which]))
                (doc_a, query_a, len_a), (doc_b, query_b, len_b) = found
                left = jnp.concatenate([doc_a, doc_b], axis=1)
                right = jnp.concatenate(
                    [
                        jnp.concatenate([query_a, zeros], axis=1),
                        jnp.concatenate([zeros, query_b], axis=1),
                    ],
                    axis=0,
                )
                sims = lax.dot_general(left, right, NT, preferred_element_type=F32)
                live = row_index < jnp.where(first_lanes, len_a, len_b)
                best_rows[pair, pl.ds(row, 1), : 2 * QLEN] = jnp.max(
                    jnp.where(live, sims, -jnp.inf), axis=0, keepdims=True
                )

        eight = pl.ds(pl.multiple_of(base, 8), 8)
        spots = table[eight, :]
        rated = jnp.zeros((8, 128), F32)
        for slot in range(SLOTS):
            low = (slot % 2) * QLEN
            value = jnp.sum(best_rows[slot // 2, eight, low : low + QLEN], axis=1, keepdims=True)
            rated = rated + jnp.where(eight_lanes == spots[:, slot + 16 : slot + 17], value, 0.0)
        back_send[pl.ds(base, 8)] = rated.reshape(8, 1, 128)

    def send_back(source_x, local):
        for step in (2, 1, 3, 0):
            for half_index in range(2):
                row = source_x * 8 + half_index * NY + mod(y + step, NY)
                if local and step == 0:
                    own_row = is_own(row)
                    pl.when(own_row)(
                        lambda row=row: pltpu.make_async_copy(
                            back_send.at[row], back_recv.at[doc], back_recv_sem.at[doc]
                        ).start()
                    )
                    pl.when(jnp.logical_not(own_row))(lambda row=row: back_copy(row).start())
                else:
                    back_copy(row).start()

    for copy in shared:
        copy.wait_recv()
    rate(x, True)
    send_back(x, True)
    for offset in (1, 3, 2):
        for half_index in range(2):
            index = mod(x - offset, NX) * 2 + half_index
            for source_y in range(NY):
                across_copy(half_index, source_y, offset, index).wait_recv()
            shared.append(share_copy(2 * offset + half_index, index))
            shared[-1].start()
    for copy in shared[2:]:
        copy.wait_recv()
    for offset in (2, 1, 3):
        rate(mod(x - offset, NX), False)
        send_back(mod(x - offset, NX), False)

    @pl.loop(0, NX * NZ)
    def _(row):
        pltpu.make_async_copy(back_send.at[0], back_recv.at[row], back_recv_sem.at[row]).wait()

    answer = jnp.broadcast_to(jnp.sum(back_recv[...], axis=0), (8, 128))
    spot = lax.broadcasted_iota(jnp.int32, (8, 128), 0)
    turned = answer
    for i in range(1, 8):
        turned = jnp.where(spot == i, pltpu.roll(answer, 128 - 16 * i, 1), turned)
    score_tile[...] = turned[:, : score_tile.shape[1]]
    outs.append(pltpu.make_async_copy(score_tile, score_out, load_sem.at[8]))
    outs[-1].start()
    for copy in outs:
        copy.wait()

    @pl.loop(0, NX * NZ)
    def _(row):
        pl.when(jnp.logical_not(is_own(row)))(lambda: back_copy(row).wait_send())

    pl.when(jnp.logical_not(at_home))(lambda: cand_copy(0).wait_send())
    pl.loop(1, NX * NZ)(lambda offset: cand_copy(offset).wait_send())
    pl.when(jnp.logical_not(at_home))(lambda: spread_copy(0).wait_send())
    for offset in range(1, NZ):
        spread_copy(offset).wait_send()
    for copy in list(copies.values()) + swaps + [att_copy] + sent_one + sent_two + sent_three + sent_four + crossing + shared:
        copy.wait_send()


def encode(tokens, w_qkv, w_out, w_up, w_down, gain_one, gain_two, rel_table, prompt_cache, w_proj, docs, lengths, named, group_ids):
    plan = plan_gather()
    rows, width = tokens.shape
    half = rows // 2
    part = half // NY
    anywhere = pl.BlockSpec(memory_space=pl.ANY)
    dma = pltpu.SemaphoreType.DMA
    return pl.pallas_call(
        functools.partial(encoder_kernel, plan),
        out_shape=(
            jax.ShapeDtypeStruct((rows // 16, 16, 128), BF16),
            jax.ShapeDtypeStruct(named.shape, F32),
        ),
        in_specs=[anywhere] * 14,
        out_specs=(anywhere, anywhere),
        scratch_shapes=[
            pltpu.SMEM(group_ids.shape, jnp.int32),
            pltpu.VMEM((16, width), F32),
            pltpu.VMEM((width, 128), BF16),
            pltpu.SMEM(lengths.shape, jnp.int32),
            pltpu.VMEM(named.shape, jnp.int32),
            pltpu.VMEM((8, 128), jnp.int32),
            pltpu.VMEM((1, 128), jnp.int32),
            pltpu.VMEM(named.shape, F32),
            pltpu.VMEM((64, PLEN, 128), BF16),
            pltpu.VMEM((64, PLEN, 128), BF16),
            pltpu.VMEM((rows // QLEN, 2 * QLEN, 128), BF16),
            pltpu.VMEM((rows // QLEN, 2 * QLEN, 128), F32),
            pltpu.VMEM((rows, width), BF16),
            pltpu.VMEM((3, width, 128), BF16),
            pltpu.VMEM((2, 128, width), BF16),
            pltpu.VMEM((2, width, 512), BF16),
            pltpu.VMEM((2, 512, width), BF16),
            pltpu.VMEM((2, 128, width), BF16),
            pltpu.VMEM((2, rows, 128), BF16),
            pltpu.VMEM((rows, 128), BF16),
            pltpu.VMEM((rows, 128), BF16),
            pltpu.VMEM((rows, 256), F32),
            pltpu.VMEM((2, 256, 128), BF16),
            pltpu.VMEM((2, half, 128), BF16),
            pltpu.VMEM((half, 128), BF16),
            pltpu.VMEM((2, 2, part, 512), BF16),
            pltpu.VMEM((2, 2, 2, part, 512), BF16),
            pltpu.VMEM((2, 2, part, 512), BF16),
            pltpu.VMEM((2, 2, 2, part, 512), BF16),
            pltpu.VMEM((NY, 2, part, 512), BF16),
            pltpu.VMEM((2 * NY, 3, 16, 128), BF16),
            dma((16,)),
            dma((len(plan),)),
            dma((len(plan),)),
            dma((3,)),
            dma((3,)),
            dma((2,)),
            dma((2, 2)),
            dma((2, 2)),
            dma((2, 2, 2)),
            dma((2, 2, 2)),
            dma((2, 2, 2)),
            dma((2, 2, 2)),
            dma((7,)),
            dma((7,)),
            pltpu.VMEM((64, 256, 128), BF16),
            pltpu.VMEM((8, 24, 16, 128), BF16),
            pltpu.VMEM((2, 24, 16, 128), BF16),
            pltpu.VMEM((32, 1, 128), jnp.int32),
            pltpu.VMEM((32, 128), jnp.int32),
            pltpu.SMEM((32, 128), jnp.int32),
            pltpu.VMEM((SLOTS // 2, 32, 128), F32),
            pltpu.VMEM((32, 1, 128), F32),
            pltpu.VMEM((32, 1, 128), F32),
            dma((1,)),
            dma((32,)),
            dma((32,)),
            dma((8,)),
            dma((2, 4)),
            dma((2, 4, 3)),
            dma((2, 4, 3)),
            dma((8,)),
            dma((8,)),
            dma((32,)),
            dma((32,)),
        ],
        compiler_params=pltpu.CompilerParams(collective_id=0, has_side_effects=True),
        name="encoder",
    )(
        group_ids,
        tokens,
        jnp.transpose(w_qkv, (1, 0, 2)),
        w_out,
        w_up,
        w_down,
        gain_one.reshape(1, -1),
        gain_two.reshape(1, -1),
        rel_table,
        prompt_cache.reshape(2, 2, PLEN, 128),
        w_proj,
        docs,
        lengths,
        named,
    )


def body(
    tokens,
    w_qkv,
    w_out,
    w_up,
    w_down,
    gain_one,
    gain_two,
    rel_table,
    prompt_cache,
    w_proj,
    doc_vectors,
    doc_lengths,
    group_ids,
    candidates,
):
    query_vectors, rated = encode(
        tokens,
        w_qkv,
        w_out,
        w_up,
        w_down,
        gain_one,
        gain_two,
        rel_table,
        prompt_cache,
        w_proj,
        doc_vectors,
        doc_lengths,
        candidates.T,
        group_ids,
    )
    return (query_vectors.reshape(tokens.shape[0], 128), rated.T)


def solution(mesh):
    placed = (
        P("doc", None),
        P(None, None, "head"),
        P("head", None),
        P(None, "head"),
        P("head", None),
        P(),
        P(),
        P(),
        P(None, "doc", "head"),
        P(),
        P("doc", None, None),
        P("doc"),
        P("doc"),
        P("doc", "head"),
    )
    return jax.shard_map(
        body,
        mesh=mesh,
        in_specs=placed,
        out_specs=(P("doc", None), P("doc", "head")),
        check_vma=False,
    )
```

```python
import functools
import math

import jax
import jax.numpy as jnp
from jax import lax
from jax.experimental import pallas as pl
from jax.experimental.pallas import tpu as pltpu
from jax.sharding import PartitionSpec as P

HD = 64
RELS = 512
QLEN = 32
PLEN = 64
DOC_DEV = 64
NX = 4
NZ = 8
NY = 4
SLOTS = 6
MESH = pl.DeviceIdType.MESH
F32 = jnp.float32
BF16 = jnp.bfloat16
NT = (((1,), (1,)), ((), ()))


def mod(value, size):
    return lax.rem(value + 4 * size, size)


HOP_US = 2.3
ROUTE_US = 0.65
ROWS_US = 256 / 46500.0
Z_FIRST = ((0, 0, 128),)
X_FIRST = ((1, 0, 128),)


class Message:
    def __init__(self, kv, axis, sign, hops, dx, dz, low, rows, parent):
        self.kv, self.axis, self.sign, self.hops = kv, axis, sign, hops
        self.dx, self.dz, self.low, self.rows, self.parent = dx, dz, low, rows, parent
        self.children = []
        self.time = None
        self.index = None


def plan_gather():
    made = []

    def add(*fields):
        made.append(Message(*fields))
        return made[-1]

    def along_x(kv, dz, low, rows, parent, direct):
        out = []
        half = rows // 2
        for sign in (1, -1):
            near = add(kv, "x", sign, 1, sign, dz, low, rows, parent)
            part = low if sign > 0 else low + half
            hops = 2 if direct else 1
            out += [near, add(kv, "x", sign, hops, 2 * sign, dz, part, half, parent if direct else near)]
        return out

    def along_z(kv, dx, low, rows, parent, jump):
        out = []
        half = rows // 2
        for sign in (1, -1):
            one = add(kv, "z", sign, 1, dx, sign, low, rows, parent)
            two = add(kv, "z", sign, 2 if jump else 1, dx, 2 * sign, low, rows, parent if jump else one)
            three = add(kv, "z", sign, 1, dx, 3 * sign, low, rows, two)
            part = low if sign > 0 else low + half
            out += [one, two, three, add(kv, "z", sign, 1, dx, 4 * sign, part, half, three)]
        return out

    for kv, low, rows in Z_FIRST:
        firsts = along_z(kv, 0, low, rows, None, True)
        along_x(kv, 0, low, rows, None, False)
        for first in firsts:
            along_x(kv, first.dz, first.low, first.rows, first, abs(first.dz) == 4)
    for kv, low, rows in X_FIRST:
        firsts = along_x(kv, 0, low, rows, None, True)
        along_z(kv, 0, low, rows, None, False)
        for first in firsts:
            along_z(kv, first.dx, first.low, first.rows, first, False)
    for message in made:
        if message.parent is not None:
            message.parent.children.append(message)
    free = {}
    ready = [(0.0, i) for i, m in enumerate(made) if m.parent is None]
    while ready:
        ready.sort()
        start, i = ready.pop(0)
        message = made[i]
        link = (message.axis, message.sign)
        free[link] = max(start, free.get(link, 0.0)) + message.rows * ROWS_US * message.hops
        message.time = free[link] + HOP_US + ROUTE_US * (message.hops - 1)
        ready += [(message.time, made.index(child)) for child in message.children]
    order = sorted(made, key=lambda m: m.time)
    for index, message in enumerate(order):
        message.index = index
    return order


def norm_rows(values, gain):
    centre = values - jnp.mean(values, axis=-1, keepdims=True)
    spread = jnp.mean(centre * centre, axis=-1, keepdims=True)
    return centre * lax.rsqrt(spread + 1e-07) * gain


def gelu(values):
    return 0.5 * values * (1.0 + lax.erf(values * (1.0 / math.sqrt(2.0))))


def encoder_kernel(
    plan,
    group_hbm,
    tokens_hbm,
    w_qkv_hbm,
    w_out_hbm,
    w_up_hbm,
    w_down_hbm,
    gain_one_hbm,
    gain_two_hbm,
    rel_hbm,
    cache_hbm,
    w_proj_hbm,
    docs_hbm,
    lengths_hbm,
    cand_hbm,
    query_out,
    score_out,
    group_ref,
    gains,
    w_proj,
    lengths_ref,
    cand_tile,
    cand_wide,
    cand_mine,
    score_tile,
    cache_keys,
    cache_values,
    prob,
    sums,
    tokens,
    w_qkv,
    w_out,
    w_up,
    w_down,
    rel,
    q_mask,
    k_own,
    v_own,
    q_rel,
    rel_two,
    att,
    att_send,
    opp_send,
    side_send,
    opp_recv,
    side_recv,
    hidden,
    vectors,
    load_sem,
    gather_send,
    gather_recv,
    swap_send,
    swap_recv,
    att_sem,
    opp_send_sem,
    opp_recv_sem,
    side_send_sem,
    side_recv_sem,
    hid_send_sem,
    hid_recv_sem,
    vec_send_sem,
    vec_recv_sem,
    docs,
    queries,
    near_queries,
    cand_rows,
    table,
    table_smem,
    best_rows,
    back_send,
    back_recv,
    table_sem,
    cand_send_sem,
    cand_recv_sem,
    spread_send_sem,
    spread_recv_sem,
    across_send_sem,
    across_recv_sem,
    share_send_sem,
    share_recv_sem,
    back_send_sem,
    back_recv_sem,
):
    head = lax.axis_index("head")
    doc = lax.axis_index("doc")
    y, core = lax.div(head, 2), lax.rem(head, 2)
    x, z = lax.div(doc, NZ), lax.rem(doc, NZ)
    partner = (2 * y + 1 - core, doc)
    y_up, y_down = mod(y + 1, NY), mod(y - 1, NY)
    y_far = mod(y + 2, NY)

    def at_y(other):
        return (2 * other + core, doc)

    def at_link(axis, sign):
        if axis == "x":
            return (head, mod(x + sign, NX) * NZ + z)
        return (head, x * NZ + mod(z + sign, NZ))

    peers = [partner]
    for other in (y_up, y_down, y_far):
        peers += [(2 * other + core, doc), (2 * other + 1 - core, doc)]
    links = [at_link(axis, sign * hops) for axis in ("x", "z") for sign in (1, -1) for hops in (1, 2)]
    barrier = pltpu.get_barrier_semaphore()
    for device in peers + links:
        pl.semaphore_signal(barrier, inc=1, device_id=device, device_id_type=MESH)

    loads = [
        pltpu.make_async_copy(tokens_hbm, tokens, load_sem.at[0]),
        pltpu.make_async_copy(w_qkv_hbm, w_qkv, load_sem.at[1]),
        pltpu.make_async_copy(rel_hbm.at[pl.ds(RELS // 2 - 96, 128)], rel.at[0], load_sem.at[2]),
        pltpu.make_async_copy(rel_hbm.at[pl.ds(RELS // 2 - 32, 128)], rel.at[1], load_sem.at[3]),
        pltpu.make_async_copy(cache_hbm.at[0], cache_keys.at[pl.ds(doc * 2, 2)], load_sem.at[4]),
        pltpu.make_async_copy(w_out_hbm, w_out.at[core], load_sem.at[5]),
        pltpu.make_async_copy(w_up_hbm, w_up.at[core], load_sem.at[6]),
        pltpu.make_async_copy(w_down_hbm, w_down.at[core], load_sem.at[7]),
        pltpu.make_async_copy(docs_hbm, docs, load_sem.at[8]),
        pltpu.make_async_copy(gain_one_hbm, gains.at[pl.ds(0, 1)], load_sem.at[9]),
        pltpu.make_async_copy(gain_two_hbm, gains.at[pl.ds(8, 1)], load_sem.at[10]),
        pltpu.make_async_copy(w_proj_hbm, w_proj, load_sem.at[11]),
        pltpu.make_async_copy(lengths_hbm, lengths_ref, load_sem.at[12]),
        pltpu.make_async_copy(cand_hbm, cand_tile, load_sem.at[13]),
        pltpu.make_async_copy(group_hbm, group_ref, load_sem.at[14]),
        pltpu.make_async_copy(cache_hbm.at[1], cache_values.at[pl.ds(doc * 2, 2)], load_sem.at[15]),
    ]
    for load in loads:
        load.start()
    pl.semaphore_wait(barrier, len(peers) + len(links))

    def gather_copy(message):
        dx, dz = message.dx, message.dz
        if message.axis == "x":
            dx -= message.sign * message.hops
        else:
            dz -= message.sign * message.hops
        block = mod(x - dx, NX) * NZ + mod(z - dz, NZ)
        group, low = block * 2 + message.low // PLEN, message.low % PLEN
        held = cache_values if message.kv else cache_keys
        if message.rows == 2 * PLEN:
            target = held.at[pl.ds(group, 2)]
        else:
            target = held.at[group, pl.ds(low, message.rows)]
        source = target
        if message.parent is None:
            source = cache_hbm.at[message.kv]
            if message.rows < 2 * PLEN:
                source = source.at[message.low // PLEN, pl.ds(low, message.rows)]
        return pltpu.make_async_remote_copy(
            src_ref=source,
            dst_ref=target,
            send_sem=gather_send.at[message.index],
            recv_sem=gather_recv.at[message.index],
            device_id=at_link(message.axis, message.sign * message.hops),
            device_id_type=MESH,
        )

    copies = {message.index: gather_copy(message) for message in plan}
    for message in plan:
        if message.parent is None:
            copies[message.index].start()

    swaps = []
    for i, (source, target) in enumerate(((w_out_hbm, w_out), (w_up_hbm, w_up), (w_down_hbm, w_down))):
        swaps.append(
            pltpu.make_async_remote_copy(
                src_ref=source,
                dst_ref=target.at[core],
                send_sem=swap_send.at[i],
                recv_sem=swap_recv.at[i],
                device_id=partner,
                device_id_type=MESH,
            )
        )
        swaps[-1].start()

    loads[0].wait()
    loads[1].wait()
    low_head = lax.broadcasted_iota(jnp.int32, (128, 128), 1) < HD
    for block in range(3):
        rows = slice(block * 128, block * 128 + 128)
        q_made, k_made, v_made = (
            jnp.dot(tokens[rows, :], w_qkv[i], preferred_element_type=F32) for i in range(3)
        )
        q_mask[0, rows, :] = jnp.where(low_head, q_made, 0.0).astype(BF16)
        q_mask[1, rows, :] = jnp.where(low_head, 0.0, q_made).astype(BF16)
        k_own[rows, :] = k_made.astype(BF16)
        v_own[rows, :] = v_made.astype(BF16)
    loads[2].wait()
    loads[3].wait()
    flip = (
        lax.broadcasted_iota(jnp.int32, (128, 128), 0) + lax.broadcasted_iota(jnp.int32, (128, 128), 1)
        == 127
    ).astype(F32).astype(BF16)
    for i in range(2):
        row = jnp.dot(
            rel[i], w_qkv[i], preferred_element_type=F32
        ).astype(BF16)
        turned = jnp.dot(flip, row, preferred_element_type=F32)
        rel_two[i, 0:128, :] = jnp.where(low_head, turned, 0.0).astype(BF16)
        rel_two[i, 128:256, :] = jnp.where(low_head, 0.0, turned).astype(BF16)
    for block in range(3):
        rows = slice(block * 128, block * 128 + 128)
        q_all = q_mask[0, rows, :] + q_mask[1, rows, :]
        q_rel[rows, :] = lax.dot_general(q_all, rel_two[1], NT, preferred_element_type=F32)
    loads[4].wait()
    for i in range(9, 16):
        loads[i].wait()
    cand_wide[...] = jnp.zeros_like(cand_wide)
    cand_wide[:, : cand_tile.shape[1]] = cand_tile[...]
    cand_mine[...] = jnp.sum(pltpu.roll(cand_wide[...], 0, 1, stride=16, stride_axis=0), axis=0, keepdims=True)

    for message in plan:
        if message.children:
            copies[message.index].wait_recv()
        for child in message.children:
            copies[child.index].start()
    for message in plan:
        if message.kv == 0 and not message.children:
            copies[message.index].wait_recv()

    low_lane = lax.broadcasted_iota(jnp.int32, (96, 128), 1) < QLEN
    low_half = lax.broadcasted_iota(jnp.int32, (QLEN, 128), 1) < HD

    def weigh(place, request):
        group = group_ref[request]
        own = pl.ds(pl.multiple_of(request * QLEN, QLEN), QLEN)
        keys = jnp.concatenate([cache_keys[group], k_own[own, :]], axis=0)
        query = jnp.concatenate([q_mask[0, own, :], q_mask[1, own, :]], axis=0)
        content = lax.dot_general(query, keys, NT, preferred_element_type=F32)
        key_rel = lax.dot_general(keys, rel_two[0], NT, preferred_element_type=F32)
        first = pltpu.roll(key_rel[:, :128], 33, 1, stride=1, stride_axis=0)
        second = pltpu.roll(key_rel[:, 128:], 65, 1, stride=1, stride_axis=0)
        p2c = jnp.transpose(jnp.where(low_lane, first, second))[: 2 * QLEN, :]
        mine = q_rel[own, :]
        c2p = jnp.concatenate(
            [
                pltpu.roll(mine[:, :128], 97, 1, stride=1, stride_axis=0),
                pltpu.roll(mine[:, 128:], 97, 1, stride=1, stride_axis=0),
            ],
            axis=0,
        )[:, :96]
        logits = (content + c2p + p2c) * (1.0 / math.sqrt(3 * HD))
        weights = jnp.exp(logits - jnp.max(logits, axis=-1, keepdims=True))
        total = jnp.sum(weights, axis=-1, keepdims=True)
        prob[place, :, : PLEN + QLEN] = weights.astype(BF16)
        sums[place] = jnp.broadcast_to(total, (2 * QLEN, 128))

    def blend(place, request):
        own = pl.ds(pl.multiple_of(request * QLEN, QLEN), QLEN)
        values = jnp.concatenate([cache_values[group_ref[request]], v_own[own, :]], axis=0)
        out = jnp.dot(prob[place, :, : PLEN + QLEN], values, preferred_element_type=F32) / sums[place]
        return jnp.where(low_half, out[:QLEN], out[QLEN:]).astype(BF16)

    half = tokens.shape[0] // 2
    per_core = half // QLEN
    for i in range(per_core):
        weigh(i, (1 - core) * per_core + i)
        weigh(per_core + i, core * per_core + i)
    for message in plan:
        if message.kv == 1 and not message.children:
            copies[message.index].wait_recv()
    for i in range(per_core):
        att_send[i * QLEN : i * QLEN + QLEN, :] = blend(i, (1 - core) * per_core + i)
    att_copy = pltpu.make_async_remote_copy(
        src_ref=att_send,
        dst_ref=att.at[core],
        send_sem=att_sem.at[0],
        recv_sem=att_sem.at[1],
        device_id=partner,
        device_id_type=MESH,
    )
    att_copy.start()
    for i in range(per_core):
        att[core, i * QLEN : i * QLEN + QLEN, :] = blend(per_core + i, core * per_core + i)
    att_copy.wait_recv()
    loads[5].wait()
    swaps[0].wait_recv()
    part = half // NY

    def chunk_rows(other):
        return pl.ds(pl.multiple_of(other * part, 16), part)

    def out_part(other):
        rows = chunk_rows(other)
        return jnp.dot(att[0, rows, :], w_out[0], preferred_element_type=F32) + jnp.dot(
            att[1, rows, :], w_out[1], preferred_element_type=F32
        )

    def side_copy(phase, side, piece):
        return pltpu.make_async_remote_copy(
            src_ref=side_send.at[phase, side, piece],
            dst_ref=side_recv.at[phase, side, piece],
            send_sem=side_send_sem.at[phase, side, piece],
            recv_sem=side_recv_sem.at[phase, side, piece],
            device_id=at_y(y_down if side else y_up),
            device_id_type=MESH,
        )

    def far_copy(phase, piece):
        return pltpu.make_async_remote_copy(
            src_ref=opp_send.at[phase, piece],
            dst_ref=opp_recv.at[phase, piece],
            send_sem=opp_send_sem.at[phase, piece],
            recv_sem=opp_recv_sem.at[phase, piece],
            device_id=at_y(y_down if piece else y_up),
            device_id_type=MESH,
        )

    wide = 512

    def reduce_rows(phase, far, up, down, own):
        sent = []
        share = far()
        for piece in range(2):
            opp_send[phase, piece] = share[:, piece * wide : piece * wide + wide].astype(BF16)
            copy = far_copy(phase, piece)
            copy.start()
            sent.append(copy)
        share_up, share_down = up(), down()
        side_send[phase, 0, 1] = share_up[:, wide:].astype(BF16)
        side_send[phase, 1, 0] = share_down[:, :wide].astype(BF16)
        for side, piece in ((0, 1), (1, 0)):
            copy = side_copy(phase, side, piece)
            copy.start()
            sent.append(copy)
        share_own = own()
        far_copy(phase, 0).wait_recv()
        side_send[phase, 0, 0] = (share_up[:, :wide] + opp_recv[phase, 0].astype(F32)).astype(BF16)
        copy = side_copy(phase, 0, 0)
        copy.start()
        sent.append(copy)
        far_copy(phase, 1).wait_recv()
        side_send[phase, 1, 1] = (share_down[:, wide:] + opp_recv[phase, 1].astype(F32)).astype(BF16)
        copy = side_copy(phase, 1, 1)
        copy.start()
        sent.append(copy)
        for side, piece in ((0, 1), (1, 0), (0, 0), (1, 1)):
            side_copy(phase, side, piece).wait_recv()
        halves = [
            share_own[:, piece * wide : piece * wide + wide]
            + side_recv[phase, 0, piece].astype(F32)
            + side_recv[phase, 1, piece].astype(F32)
            for piece in range(2)
        ]
        return jnp.concatenate(halves, axis=1), sent

    total, sent_one = reduce_rows(
        0,
        lambda: out_part(y_far),
        lambda: out_part(y_up),
        lambda: out_part(y_down),
        lambda: out_part(y),
    )
    own_rows = pl.ds(pl.multiple_of(core * half + y * part, 16), part)
    one = norm_rows(tokens[own_rows, :].astype(F32) + total, gains[0:1, :]).astype(BF16)
    for piece in range(2):
        hidden[y, piece] = one[:, piece * wide : piece * wide + wide]

    def hidden_copy(side, hop, piece):
        block = y if hop == 0 else (y_up if side else y_down)
        return pltpu.make_async_remote_copy(
            src_ref=hidden.at[block, piece],
            dst_ref=hidden.at[block, piece],
            send_sem=hid_send_sem.at[side, hop, piece],
            recv_sem=hid_recv_sem.at[side, hop, piece],
            device_id=at_y(y_down if side else y_up),
            device_id_type=MESH,
        )

    sent_two = []

    def send_hidden(side, hop, piece):
        copy = hidden_copy(side, hop, piece)
        copy.start()
        sent_two.append(copy)

    send_hidden(0, 0, 0)
    send_hidden(1, 0, 1)
    send_hidden(0, 0, 1)
    send_hidden(1, 0, 0)
    home = mod(x + z, NY)
    at_home = home == y
    my_row = (x * 2 + lax.div(z, 4)) * NY + y

    def cand_copy(offset):
        return pltpu.make_async_remote_copy(
            src_ref=cand_mine,
            dst_ref=cand_rows.at[my_row],
            send_sem=cand_send_sem.at[offset],
            recv_sem=cand_recv_sem.at[my_row],
            device_id=(2 * home + core, mod(doc + offset, NX * NZ)),
            device_id_type=MESH,
        )

    cand_local = pltpu.make_async_copy(cand_mine, cand_rows.at[my_row], cand_recv_sem.at[my_row])
    for i in (6, 7):
        loads[i].wait()
    swaps[1].wait_recv()
    swaps[2].wait_recv()

    def feed(other):
        rows = jnp.concatenate([hidden[other, 0], hidden[other, 1]], axis=1)
        made = None
        for i in range(2):
            inner = gelu(jnp.dot(rows, w_up[i], preferred_element_type=F32)).astype(BF16)
            term = jnp.dot(inner, w_down[i], preferred_element_type=F32)
            made = term if made is None else made + term
        return made

    feed_own = feed(y)
    pl.when(at_home)(lambda: cand_local.start())
    pl.when(jnp.logical_not(at_home))(lambda: cand_copy(0).start())
    pl.loop(1, NX * NZ)(lambda offset: cand_copy(offset).start())
    hidden_copy(0, 0, 0).wait_recv()
    send_hidden(0, 1, 0)
    hidden_copy(1, 0, 1).wait_recv()
    send_hidden(1, 1, 1)
    hidden_copy(0, 0, 1).wait_recv()
    hidden_copy(1, 0, 0).wait_recv()
    feed_up, feed_down = feed(y_up), feed(y_down)
    hidden_copy(0, 1, 0).wait_recv()
    hidden_copy(1, 1, 1).wait_recv()
    lane = lax.broadcasted_iota(jnp.int32, (NX * NZ, 128), 1)
    table_copy = pltpu.make_async_copy(table, table_smem, table_sem.at[0])

    def slots_then_own():
        @pl.loop(0, NX * NZ)
        def _(row):
            pltpu.make_async_copy(cand_mine, cand_rows.at[row], cand_recv_sem.at[row]).wait()

        named = cand_rows[...].reshape(NX * NZ, 128)
        mine = jnp.logical_and(lax.shift_right_logical(named, 6) == doc, lax.bitwise_and(lane, 15) < 12)
        mine_f = jnp.where(mine, 1.0, 0.0)
        before = (
            lax.broadcasted_iota(jnp.int32, (128, 128), 0) < lax.broadcasted_iota(jnp.int32, (128, 128), 1)
        ).astype(F32).astype(BF16)
        rank = jnp.dot(mine_f.astype(BF16), before, preferred_element_type=F32)
        rows_table = jnp.zeros((NX * NZ, 128), jnp.int32)
        for slot in range(SLOTS):
            chosen = jnp.where(rank == float(slot), mine_f, 0.0)
            some = jnp.sum(chosen, axis=1, keepdims=True)
            place = jnp.sum(chosen * lane.astype(F32), axis=1, keepdims=True).astype(jnp.int32)
            which = jnp.sum(
                chosen * lax.bitwise_and(named, DOC_DEV - 1).astype(F32), axis=1, keepdims=True
            ).astype(jnp.int32)
            rows_table = jnp.where(lane == slot + 16, jnp.where(some > 0.5, place, 127), rows_table)
            rows_table = jnp.where(lane == slot, lax.bitwise_and(place, 15) * 2, rows_table)
            rows_table = jnp.where(lane == slot + 8, which, rows_table)
        table[...] = rows_table
        table_copy.start()
        return feed_own

    total_two, sent_three = reduce_rows(
        1, lambda: feed(y_far), lambda: feed_up, lambda: feed_down, slots_then_own
    )
    two = norm_rows(one.astype(F32) + total_two, gains[8:9, :]).astype(BF16)
    projected = jnp.dot(two, w_proj[...], preferred_element_type=F32)
    unit = projected * lax.rsqrt(jnp.sum(projected * projected, axis=-1, keepdims=True) + 1e-06)
    vectors[head] = unit.astype(BF16).reshape(3, 16, 128)

    half_doc = lax.div(z, 4)
    piece_rows = pl.ds(core * 12 + y * 3, 3)

    def spread_copy(offset):
        return pltpu.make_async_remote_copy(
            src_ref=vectors.at[head],
            dst_ref=near_queries.at[half_doc, piece_rows],
            send_sem=spread_send_sem.at[offset],
            recv_sem=spread_recv_sem.at[half_doc, y],
            device_id=(2 * home + core, x * NZ + mod(z + offset, NZ)),
            device_id_type=MESH,
        )

    def across_copy(half_index, source_y, offset, index):
        rows = pl.ds(core * 12 + source_y * 3, 3)
        return pltpu.make_async_remote_copy(
            src_ref=near_queries.at[half_index, rows],
            dst_ref=queries.at[index, rows],
            send_sem=across_send_sem.at[half_index, source_y, offset - 1],
            recv_sem=across_recv_sem.at[half_index, source_y, offset - 1],
            device_id=(head, mod(x + offset, NX) * NZ + z),
            device_id_type=MESH,
        )

    def share_copy(place, index):
        held = near_queries.at[place] if place < 2 else queries.at[index]
        rows = held.at[pl.ds(core * 12, 12)]
        return pltpu.make_async_remote_copy(
            src_ref=rows,
            dst_ref=rows,
            send_sem=share_send_sem.at[place],
            recv_sem=share_recv_sem.at[place],
            device_id=partner,
            device_id_type=MESH,
        )

    spread_local = pltpu.make_async_copy(
        vectors.at[head], near_queries.at[half_doc, piece_rows], spread_recv_sem.at[half_doc, y]
    )
    pl.when(at_home)(lambda: spread_local.start())
    pl.when(jnp.logical_not(at_home))(lambda: spread_copy(0).start())
    for offset in (4, 3, 5, 2, 6, 1, 7):
        spread_copy(offset).start()
    sent_four = []
    for i, device in enumerate(peers):
        copy = pltpu.make_async_remote_copy(
            src_ref=vectors.at[head],
            dst_ref=vectors.at[head],
            send_sem=vec_send_sem.at[i],
            recv_sem=vec_recv_sem.at[i],
            device_id=device,
            device_id_type=MESH,
        )
        copy.start()
        sent_four.append(copy)
    crossing = []
    shared = []
    ahead = mod(mod(y - x, NY) - z, NZ)
    near = jnp.where(jnp.logical_or(ahead <= 2, ahead >= 6), 0, 1)
    for step, half_index in (
        (0, near),
        (1, near),
        (3, near),
        (0, 1 - near),
        (2, near),
        (1, 1 - near),
        (3, 1 - near),
        (2, 1 - near),
    ):
        source_y = mod(y + step, NY)
        pltpu.make_async_copy(
            vectors.at[head],
            near_queries.at[half_index, pl.ds(core * 12 + source_y * 3, 3)],
            spread_recv_sem.at[half_index, source_y],
        ).wait()
        for offset in (2, 1, 3):
            crossing.append(across_copy(half_index, source_y, offset, x * 2 + half_index))
            crossing[-1].start()
    for half_index in range(2):
        shared.append(share_copy(half_index, x * 2 + half_index))
        shared[-1].start()
    for copy in sent_four:
        copy.wait_recv()
    outs = []
    for block in range(2 * NY):
        place = (block % 2) * 12 + (block // 2) * 3
        outs.append(
            pltpu.make_async_copy(vectors.at[block], query_out.at[pl.ds(place, 3)], load_sem.at[block])
        )
        outs[-1].start()
    table_copy.wait()
    loads[8].wait()

    zeros = jnp.zeros((QLEN, 128), BF16)
    row_index = lax.broadcasted_iota(jnp.int32, (256, 2 * QLEN), 0)
    first_lanes = lax.broadcasted_iota(jnp.int32, (1, 2 * QLEN), 1) < QLEN
    eight_lanes = lax.broadcasted_iota(jnp.int32, (8, 128), 1)

    def back_to(row):
        source_x, source_half, source_y = lax.div(row, 8), lax.rem(lax.div(row, NY), 2), lax.rem(row, NY)
        source = source_x * NZ + mod(y - source_x, NY) + 4 * source_half
        return source, source_y

    def back_copy(row):
        source, source_y = back_to(row)
        return pltpu.make_async_remote_copy(
            src_ref=back_send.at[row],
            dst_ref=back_recv.at[doc],
            send_sem=back_send_sem.at[row],
            recv_sem=back_recv_sem.at[doc],
            device_id=(2 * source_y + core, source),
            device_id_type=MESH,
        )

    def is_own(row):
        source, source_y = back_to(row)
        return jnp.logical_and(source == doc, source_y == y)

    def rate(source_x, local):
        base = source_x * 8

        for i, pair in [(i, pair) for i in range(8) for pair in range(SLOTS // 2)]:
            row = base + i
            held = near_queries.at[i // NY] if local else queries.at[source_x * 2 + i // NY]
            found = []
            for slot in (2 * pair, 2 * pair + 1):
                which = jnp.clip(table_smem[row, slot + 8], 0, DOC_DEV - 1)
                request = jnp.clip(table_smem[row, slot], 0, 22)
                query = jnp.concatenate([held[request], held[request + 1]], axis=0)
                found.append((docs[which], query, lengths_ref[which]))
            (doc_a, query_a, len_a), (doc_b, query_b, len_b) = found
            left = jnp.concatenate([doc_a, doc_b], axis=1)
            right = jnp.concatenate(
                [
                    jnp.concatenate([query_a, zeros], axis=1),
                    jnp.concatenate([zeros, query_b], axis=1),
                ],
                axis=0,
            )
            sims = lax.dot_general(left, right, NT, preferred_element_type=F32)
            live = row_index < jnp.where(first_lanes, len_a, len_b)
            best_rows[pair, pl.ds(row, 1), : 2 * QLEN] = jnp.max(
                jnp.where(live, sims, -jnp.inf), axis=0, keepdims=True
            )

        eight = pl.ds(pl.multiple_of(base, 8), 8)
        spots = table[eight, :]
        rated = jnp.zeros((8, 128), F32)
        for slot in range(SLOTS):
            low = (slot % 2) * QLEN
            value = jnp.sum(best_rows[slot // 2, eight, low : low + QLEN], axis=1, keepdims=True)
            rated = rated + jnp.where(eight_lanes == spots[:, slot + 16 : slot + 17], value, 0.0)
        back_send[pl.ds(base, 8)] = rated.reshape(8, 1, 128)

    def send_back(source_x, local):
        for step in (2, 1, 3, 0):
            for half_index in range(2):
                row = source_x * 8 + half_index * NY + mod(y + step, NY)
                if local and step == 0:
                    own_row = is_own(row)
                    pl.when(own_row)(
                        lambda row=row: pltpu.make_async_copy(
                            back_send.at[row], back_recv.at[doc], back_recv_sem.at[doc]
                        ).start()
                    )
                    pl.when(jnp.logical_not(own_row))(lambda row=row: back_copy(row).start())
                else:
                    back_copy(row).start()

    for copy in shared:
        copy.wait_recv()
    rate(x, True)
    send_back(x, True)
    for offset in (1, 3, 2):
        for half_index in range(2):
            index = mod(x - offset, NX) * 2 + half_index
            for source_y in range(NY):
                across_copy(half_index, source_y, offset, index).wait_recv()
            shared.append(share_copy(2 * offset + half_index, index))
            shared[-1].start()
    for copy in shared[2:]:
        copy.wait_recv()
    for offset in (2, 1, 3):
        rate(mod(x - offset, NX), False)
        send_back(mod(x - offset, NX), False)

    @pl.loop(0, NX * NZ)
    def _(row):
        pltpu.make_async_copy(back_send.at[0], back_recv.at[row], back_recv_sem.at[row]).wait()

    answer = jnp.broadcast_to(jnp.sum(back_recv[...], axis=0), (8, 128))
    spot = lax.broadcasted_iota(jnp.int32, (8, 128), 0)
    turned = answer
    for i in range(1, 8):
        turned = jnp.where(spot == i, pltpu.roll(answer, 128 - 16 * i, 1), turned)
    score_tile[...] = turned[:, : score_tile.shape[1]]
    outs.append(pltpu.make_async_copy(score_tile, score_out, load_sem.at[8]))
    outs[-1].start()
    for copy in outs:
        copy.wait()

    @pl.loop(0, NX * NZ)
    def _(row):
        pl.when(jnp.logical_not(is_own(row)))(lambda: back_copy(row).wait_send())

    pl.when(jnp.logical_not(at_home))(lambda: cand_copy(0).wait_send())
    pl.loop(1, NX * NZ)(lambda offset: cand_copy(offset).wait_send())
    pl.when(jnp.logical_not(at_home))(lambda: spread_copy(0).wait_send())
    for offset in range(1, NZ):
        spread_copy(offset).wait_send()
    for copy in list(copies.values()) + swaps + [att_copy] + sent_one + sent_two + sent_three + sent_four + crossing + shared:
        copy.wait_send()


def encode(tokens, w_qkv, w_out, w_up, w_down, gain_one, gain_two, rel_table, prompt_cache, w_proj, docs, lengths, named, group_ids):
    plan = plan_gather()
    rows, width = tokens.shape
    half = rows // 2
    part = half // NY
    anywhere = pl.BlockSpec(memory_space=pl.ANY)
    dma = pltpu.SemaphoreType.DMA
    return pl.pallas_call(
        functools.partial(encoder_kernel, plan),
        out_shape=(
            jax.ShapeDtypeStruct((rows // 16, 16, 128), BF16),
            jax.ShapeDtypeStruct(named.shape, F32),
        ),
        in_specs=[anywhere] * 14,
        out_specs=(anywhere, anywhere),
        scratch_shapes=[
            pltpu.SMEM(group_ids.shape, jnp.int32),
            pltpu.VMEM((16, width), F32),
            pltpu.VMEM((width, 128), BF16),
            pltpu.SMEM(lengths.shape, jnp.int32),
            pltpu.VMEM(named.shape, jnp.int32),
            pltpu.VMEM((8, 128), jnp.int32),
            pltpu.VMEM((1, 128), jnp.int32),
            pltpu.VMEM(named.shape, F32),
            pltpu.VMEM((64, PLEN, 128), BF16),
            pltpu.VMEM((64, PLEN, 128), BF16),
            pltpu.VMEM((rows // QLEN, 2 * QLEN, 128), BF16),
            pltpu.VMEM((rows // QLEN, 2 * QLEN, 128), F32),
            pltpu.VMEM((rows, width), BF16),
            pltpu.VMEM((3, width, 128), BF16),
            pltpu.VMEM((2, 128, width), BF16),
            pltpu.VMEM((2, width, 512), BF16),
            pltpu.VMEM((2, 512, width), BF16),
            pltpu.VMEM((2, 128, width), BF16),
            pltpu.VMEM((2, rows, 128), BF16),
            pltpu.VMEM((rows, 128), BF16),
            pltpu.VMEM((rows, 128), BF16),
            pltpu.VMEM((rows, 256), F32),
            pltpu.VMEM((2, 256, 128), BF16),
            pltpu.VMEM((2, half, 128), BF16),
            pltpu.VMEM((half, 128), BF16),
            pltpu.VMEM((2, 2, part, 512), BF16),
            pltpu.VMEM((2, 2, 2, part, 512), BF16),
            pltpu.VMEM((2, 2, part, 512), BF16),
            pltpu.VMEM((2, 2, 2, part, 512), BF16),
            pltpu.VMEM((NY, 2, part, 512), BF16),
            pltpu.VMEM((2 * NY, 3, 16, 128), BF16),
            dma((16,)),
            dma((len(plan),)),
            dma((len(plan),)),
            dma((3,)),
            dma((3,)),
            dma((2,)),
            dma((2, 2)),
            dma((2, 2)),
            dma((2, 2, 2)),
            dma((2, 2, 2)),
            dma((2, 2, 2)),
            dma((2, 2, 2)),
            dma((7,)),
            dma((7,)),
            pltpu.VMEM((64, 256, 128), BF16),
            pltpu.VMEM((8, 24, 16, 128), BF16),
            pltpu.VMEM((2, 24, 16, 128), BF16),
            pltpu.VMEM((32, 1, 128), jnp.int32),
            pltpu.VMEM((32, 128), jnp.int32),
            pltpu.SMEM((32, 128), jnp.int32),
            pltpu.VMEM((SLOTS // 2, 32, 128), F32),
            pltpu.VMEM((32, 1, 128), F32),
            pltpu.VMEM((32, 1, 128), F32),
            dma((1,)),
            dma((32,)),
            dma((32,)),
            dma((8,)),
            dma((2, 4)),
            dma((2, 4, 3)),
            dma((2, 4, 3)),
            dma((8,)),
            dma((8,)),
            dma((32,)),
            dma((32,)),
        ],
        compiler_params=pltpu.CompilerParams(collective_id=0, has_side_effects=True),
        name="encoder",
    )(
        group_ids,
        tokens,
        jnp.transpose(w_qkv, (1, 0, 2)),
        w_out,
        w_up,
        w_down,
        gain_one.reshape(1, -1),
        gain_two.reshape(1, -1),
        rel_table,
        prompt_cache.reshape(2, 2, PLEN, 128),
        w_proj,
        docs,
        lengths,
        named,
    )


def body(
    tokens,
    w_qkv,
    w_out,
    w_up,
    w_down,
    gain_one,
    gain_two,
    rel_table,
    prompt_cache,
    w_proj,
    doc_vectors,
    doc_lengths,
    group_ids,
    candidates,
):
    query_vectors, rated = encode(
        tokens,
        w_qkv,
        w_out,
        w_up,
        w_down,
        gain_one,
        gain_two,
        rel_table,
        prompt_cache,
        w_proj,
        doc_vectors,
        doc_lengths,
        candidates.T,
        group_ids,
    )
    return (query_vectors.reshape(tokens.shape[0], 128), rated.T)


def solution(mesh):
    placed = (
        P("doc", None),
        P(None, None, "head"),
        P("head", None),
        P(None, "head"),
        P("head", None),
        P(),
        P(),
        P(),
        P(None, "doc", "head"),
        P(),
        P("doc", None, None),
        P("doc"),
        P("doc"),
        P("doc", "head"),
    )
    return jax.shard_map(
        body,
        mesh=mesh,
        in_specs=placed,
        out_specs=(P("doc", None), P("doc", "head")),
        check_vma=False,
    )
```

```python
import functools
import math

import jax
import jax.numpy as jnp
from jax import lax
from jax.experimental import pallas as pl
from jax.experimental.pallas import tpu as pltpu
from jax.sharding import PartitionSpec as P

HD = 64
RELS = 512
QLEN = 32
PLEN = 64
DOC_DEV = 64
NX = 4
NZ = 8
NY = 4
SLOTS = 6
MESH = pl.DeviceIdType.MESH
F32 = jnp.float32
BF16 = jnp.bfloat16
NT = (((1,), (1,)), ((), ()))


def mod(value, size):
    return lax.rem(value + 4 * size, size)


HOP_US = 2.3
ROUTE_US = 0.65
ROWS_US = 256 / 46500.0
Z_FIRST = ((0, 0, 128),)
X_FIRST = ((1, 0, 128),)


class Message:
    def __init__(self, kv, axis, sign, hops, dx, dz, low, rows, parent):
        self.kv, self.axis, self.sign, self.hops = kv, axis, sign, hops
        self.dx, self.dz, self.low, self.rows, self.parent = dx, dz, low, rows, parent
        self.children = []
        self.time = None
        self.index = None


def plan_gather():
    made = []

    def add(*fields):
        made.append(Message(*fields))
        return made[-1]

    def along_x(kv, dz, low, rows, parent, direct):
        out = []
        half = rows // 2
        for sign in (1, -1):
            near = add(kv, "x", sign, 1, sign, dz, low, rows, parent)
            part = low if sign > 0 else low + half
            hops = 2 if direct else 1
            out += [near, add(kv, "x", sign, hops, 2 * sign, dz, part, half, parent if direct else near)]
        return out

    def along_z(kv, dx, low, rows, parent, jump):
        out = []
        half = rows // 2
        for sign in (1, -1):
            one = add(kv, "z", sign, 1, dx, sign, low, rows, parent)
            two = add(kv, "z", sign, 2 if jump else 1, dx, 2 * sign, low, rows, parent if jump else one)
            three = add(kv, "z", sign, 1, dx, 3 * sign, low, rows, two)
            part = low if sign > 0 else low + half
            out += [one, two, three, add(kv, "z", sign, 1, dx, 4 * sign, part, half, three)]
        return out

    for kv, low, rows in Z_FIRST:
        firsts = along_z(kv, 0, low, rows, None, True)
        along_x(kv, 0, low, rows, None, False)
        for first in firsts:
            along_x(kv, first.dz, first.low, first.rows, first, abs(first.dz) == 4)
    for kv, low, rows in X_FIRST:
        firsts = along_x(kv, 0, low, rows, None, True)
        along_z(kv, 0, low, rows, None, False)
        for first in firsts:
            along_z(kv, first.dx, first.low, first.rows, first, False)
    for message in made:
        if message.parent is not None:
            message.parent.children.append(message)
    free = {}
    ready = [(0.0, i) for i, m in enumerate(made) if m.parent is None]
    while ready:
        ready.sort()
        start, i = ready.pop(0)
        message = made[i]
        link = (message.axis, message.sign)
        free[link] = max(start, free.get(link, 0.0)) + message.rows * ROWS_US * message.hops
        message.time = free[link] + HOP_US + ROUTE_US * (message.hops - 1)
        ready += [(message.time, made.index(child)) for child in message.children]
    order = sorted(made, key=lambda m: m.time)
    for index, message in enumerate(order):
        message.index = index
    return order


def norm_rows(values, gain):
    centre = values - jnp.mean(values, axis=-1, keepdims=True)
    spread = jnp.mean(centre * centre, axis=-1, keepdims=True)
    return centre * lax.rsqrt(spread + 1e-07) * gain


def gelu(values):
    return 0.5 * values * (1.0 + lax.erf(values * (1.0 / math.sqrt(2.0))))


def encoder_kernel(
    plan,
    group_hbm,
    tokens_hbm,
    w_qkv_hbm,
    w_out_hbm,
    w_up_hbm,
    w_down_hbm,
    gain_one_hbm,
    gain_two_hbm,
    rel_hbm,
    cache_hbm,
    w_proj_hbm,
    docs_hbm,
    lengths_hbm,
    cand_hbm,
    query_out,
    score_out,
    group_ref,
    gains,
    w_proj,
    lengths_ref,
    cand_tile,
    cand_wide,
    cand_mine,
    score_tile,
    cache_keys,
    cache_values,
    prob,
    sums,
    tokens,
    w_qkv,
    w_out,
    w_up,
    w_down,
    rel,
    q_mask,
    k_own,
    v_own,
    q_rel,
    rel_two,
    att,
    att_send,
    opp_send,
    side_send,
    opp_recv,
    side_recv,
    hidden,
    vectors,
    load_sem,
    gather_send,
    gather_recv,
    swap_send,
    swap_recv,
    att_sem,
    opp_send_sem,
    opp_recv_sem,
    side_send_sem,
    side_recv_sem,
    hid_send_sem,
    hid_recv_sem,
    vec_send_sem,
    vec_recv_sem,
    docs,
    queries,
    near_queries,
    cand_rows,
    table,
    table_smem,
    best_rows,
    back_send,
    back_recv,
    table_sem,
    cand_send_sem,
    cand_recv_sem,
    spread_send_sem,
    spread_recv_sem,
    across_send_sem,
    across_recv_sem,
    share_send_sem,
    share_recv_sem,
    back_send_sem,
    back_recv_sem,
):
    head = lax.axis_index("head")
    doc = lax.axis_index("doc")
    y, core = lax.div(head, 2), lax.rem(head, 2)
    x, z = lax.div(doc, NZ), lax.rem(doc, NZ)
    partner = (2 * y + 1 - core, doc)
    y_up, y_down = mod(y + 1, NY), mod(y - 1, NY)
    y_far = mod(y + 2, NY)

    def at_y(other):
        return (2 * other + core, doc)

    def at_link(axis, sign):
        if axis == "x":
            return (head, mod(x + sign, NX) * NZ + z)
        return (head, x * NZ + mod(z + sign, NZ))

    peers = [partner]
    for other in (y_up, y_down, y_far):
        peers += [(2 * other + core, doc), (2 * other + 1 - core, doc)]
    links = [at_link(axis, sign * hops) for axis in ("x", "z") for sign in (1, -1) for hops in (1, 2)]
    barrier = pltpu.get_barrier_semaphore()
    for device in peers + links:
        pl.semaphore_signal(barrier, inc=1, device_id=device, device_id_type=MESH)

    loads = [
        pltpu.make_async_copy(tokens_hbm, tokens, load_sem.at[0]),
        pltpu.make_async_copy(w_qkv_hbm, w_qkv, load_sem.at[1]),
        pltpu.make_async_copy(rel_hbm.at[pl.ds(RELS // 2 - 96, 128)], rel.at[0], load_sem.at[2]),
        pltpu.make_async_copy(rel_hbm.at[pl.ds(RELS // 2 - 32, 128)], rel.at[1], load_sem.at[3]),
        pltpu.make_async_copy(cache_hbm.at[0], cache_keys.at[pl.ds(doc * 2, 2)], load_sem.at[4]),
        pltpu.make_async_copy(w_out_hbm, w_out.at[core], load_sem.at[5]),
        pltpu.make_async_copy(w_up_hbm, w_up.at[core], load_sem.at[6]),
        pltpu.make_async_copy(w_down_hbm, w_down.at[core], load_sem.at[7]),
        pltpu.make_async_copy(docs_hbm, docs, load_sem.at[8]),
        pltpu.make_async_copy(gain_one_hbm, gains.at[pl.ds(0, 1)], load_sem.at[9]),
        pltpu.make_async_copy(gain_two_hbm, gains.at[pl.ds(8, 1)], load_sem.at[10]),
        pltpu.make_async_copy(w_proj_hbm, w_proj, load_sem.at[11]),
        pltpu.make_async_copy(lengths_hbm, lengths_ref, load_sem.at[12]),
        pltpu.make_async_copy(cand_hbm, cand_tile, load_sem.at[13]),
        pltpu.make_async_copy(group_hbm, group_ref, load_sem.at[14]),
        pltpu.make_async_copy(cache_hbm.at[1], cache_values.at[pl.ds(doc * 2, 2)], load_sem.at[15]),
    ]
    for load in loads:
        load.start()
    pl.semaphore_wait(barrier, len(peers) + len(links))

    def gather_copy(message):
        dx, dz = message.dx, message.dz
        if message.axis == "x":
            dx -= message.sign * message.hops
        else:
            dz -= message.sign * message.hops
        block = mod(x - dx, NX) * NZ + mod(z - dz, NZ)
        group, low = block * 2 + message.low // PLEN, message.low % PLEN
        held = cache_values if message.kv else cache_keys
        if message.rows == 2 * PLEN:
            target = held.at[pl.ds(group, 2)]
        else:
            target = held.at[group, pl.ds(low, message.rows)]
        source = target
        if message.parent is None:
            source = cache_hbm.at[message.kv]
            if message.rows < 2 * PLEN:
                source = source.at[message.low // PLEN, pl.ds(low, message.rows)]
        return pltpu.make_async_remote_copy(
            src_ref=source,
            dst_ref=target,
            send_sem=gather_send.at[message.index],
            recv_sem=gather_recv.at[message.index],
            device_id=at_link(message.axis, message.sign * message.hops),
            device_id_type=MESH,
        )

    copies = {message.index: gather_copy(message) for message in plan}
    for message in plan:
        if message.parent is None:
            copies[message.index].start()

    swaps = []
    for i, (source, target) in enumerate(((w_out_hbm, w_out), (w_up_hbm, w_up), (w_down_hbm, w_down))):
        swaps.append(
            pltpu.make_async_remote_copy(
                src_ref=source,
                dst_ref=target.at[core],
                send_sem=swap_send.at[i],
                recv_sem=swap_recv.at[i],
                device_id=partner,
                device_id_type=MESH,
            )
        )
        swaps[-1].start()

    loads[0].wait()
    loads[1].wait()
    low_head = lax.broadcasted_iota(jnp.int32, (128, 128), 1) < HD
    for block in range(3):
        rows = slice(block * 128, block * 128 + 128)
        q_made, k_made, v_made = (
            jnp.dot(tokens[rows, :], w_qkv[i], preferred_element_type=F32) for i in range(3)
        )
        q_mask[0, rows, :] = jnp.where(low_head, q_made, 0.0).astype(BF16)
        q_mask[1, rows, :] = jnp.where(low_head, 0.0, q_made).astype(BF16)
        k_own[rows, :] = k_made.astype(BF16)
        v_own[rows, :] = v_made.astype(BF16)
    loads[2].wait()
    loads[3].wait()
    flip = (
        lax.broadcasted_iota(jnp.int32, (128, 128), 0) + lax.broadcasted_iota(jnp.int32, (128, 128), 1)
        == 127
    ).astype(F32).astype(BF16)
    for i in range(2):
        row = jnp.dot(
            rel[i], w_qkv[i], preferred_element_type=F32
        ).astype(BF16)
        turned = jnp.dot(flip, row, preferred_element_type=F32)
        rel_two[i, 0:128, :] = jnp.where(low_head, turned, 0.0).astype(BF16)
        rel_two[i, 128:256, :] = jnp.where(low_head, 0.0, turned).astype(BF16)
    for block in range(3):
        rows = slice(block * 128, block * 128 + 128)
        q_all = q_mask[0, rows, :] + q_mask[1, rows, :]
        q_rel[rows, :] = lax.dot_general(q_all, rel_two[1], NT, preferred_element_type=F32)
    loads[4].wait()
    for i in range(9, 16):
        loads[i].wait()
    cand_wide[...] = jnp.zeros_like(cand_wide)
    cand_wide[:, : cand_tile.shape[1]] = cand_tile[...]
    cand_mine[...] = jnp.sum(pltpu.roll(cand_wide[...], 0, 1, stride=16, stride_axis=0), axis=0, keepdims=True)

    for message in plan:
        if message.children:
            copies[message.index].wait_recv()
        for child in message.children:
            copies[child.index].start()
    for message in plan:
        if message.kv == 0 and not message.children:
            copies[message.index].wait_recv()

    low_lane = lax.broadcasted_iota(jnp.int32, (96, 128), 1) < QLEN
    low_half = lax.broadcasted_iota(jnp.int32, (QLEN, 128), 1) < HD

    def weigh(place, request):
        group = group_ref[request]
        own = pl.ds(pl.multiple_of(request * QLEN, QLEN), QLEN)
        keys = jnp.concatenate([cache_keys[group], k_own[own, :]], axis=0)
        query = jnp.concatenate([q_mask[0, own, :], q_mask[1, own, :]], axis=0)
        content = lax.dot_general(query, keys, NT, preferred_element_type=F32)
        key_rel = lax.dot_general(keys, rel_two[0], NT, preferred_element_type=F32)
        first = pltpu.roll(key_rel[:, :128], 33, 1, stride=1, stride_axis=0)
        second = pltpu.roll(key_rel[:, 128:], 65, 1, stride=1, stride_axis=0)
        p2c = jnp.transpose(jnp.where(low_lane, first, second))[: 2 * QLEN, :]
        mine = q_rel[own, :]
        c2p = jnp.concatenate(
            [
                pltpu.roll(mine[:, :128], 97, 1, stride=1, stride_axis=0),
                pltpu.roll(mine[:, 128:], 97, 1, stride=1, stride_axis=0),
            ],
            axis=0,
        )[:, :96]
        logits = (content + c2p + p2c) * (1.0 / math.sqrt(3 * HD))
        weights = jnp.exp(logits - jnp.max(logits, axis=-1, keepdims=True))
        total = jnp.sum(weights, axis=-1, keepdims=True)
        prob[place, :, : PLEN + QLEN] = weights.astype(BF16)
        sums[place] = jnp.broadcast_to(total, (2 * QLEN, 128))

    def blend(place, request):
        own = pl.ds(pl.multiple_of(request * QLEN, QLEN), QLEN)
        values = jnp.concatenate([cache_values[group_ref[request]], v_own[own, :]], axis=0)
        out = jnp.dot(prob[place, :, : PLEN + QLEN], values, preferred_element_type=F32) / sums[place]
        return jnp.where(low_half, out[:QLEN], out[QLEN:]).astype(BF16)

    half = tokens.shape[0] // 2
    per_core = half // QLEN
    for i in range(per_core):
        weigh(i, (1 - core) * per_core + i)
        weigh(per_core + i, core * per_core + i)
    for message in plan:
        if message.kv == 1 and not message.children:
            copies[message.index].wait_recv()
    for i in range(per_core):
        att_send[i * QLEN : i * QLEN + QLEN, :] = blend(i, (1 - core) * per_core + i)
    att_copy = pltpu.make_async_remote_copy(
        src_ref=att_send,
        dst_ref=att.at[core],
        send_sem=att_sem.at[0],
        recv_sem=att_sem.at[1],
        device_id=partner,
        device_id_type=MESH,
    )
    att_copy.start()
    for i in range(per_core):
        att[core, i * QLEN : i * QLEN + QLEN, :] = blend(per_core + i, core * per_core + i)
    att_copy.wait_recv()
    loads[5].wait()
    swaps[0].wait_recv()
    part = half // NY

    def chunk_rows(other):
        return pl.ds(pl.multiple_of(other * part, 16), part)

    def out_part(other):
        rows = chunk_rows(other)
        return jnp.dot(att[0, rows, :], w_out[0], preferred_element_type=F32) + jnp.dot(
            att[1, rows, :], w_out[1], preferred_element_type=F32
        )

    def side_copy(phase, side, piece):
        return pltpu.make_async_remote_copy(
            src_ref=side_send.at[phase, side, piece],
            dst_ref=side_recv.at[phase, side, piece],
            send_sem=side_send_sem.at[phase, side, piece],
            recv_sem=side_recv_sem.at[phase, side, piece],
            device_id=at_y(y_down if side else y_up),
            device_id_type=MESH,
        )

    def far_copy(phase, piece):
        return pltpu.make_async_remote_copy(
            src_ref=opp_send.at[phase, piece],
            dst_ref=opp_recv.at[phase, piece],
            send_sem=opp_send_sem.at[phase, piece],
            recv_sem=opp_recv_sem.at[phase, piece],
            device_id=at_y(y_down if piece else y_up),
            device_id_type=MESH,
        )

    wide = 512

    def reduce_rows(phase, far, up, down, own):
        sent = []
        share = far()
        for piece in range(2):
            opp_send[phase, piece] = share[:, piece * wide : piece * wide + wide].astype(BF16)
            copy = far_copy(phase, piece)
            copy.start()
            sent.append(copy)
        share_up, share_down = up(), down()
        side_send[phase, 0, 1] = share_up[:, wide:].astype(BF16)
        side_send[phase, 1, 0] = share_down[:, :wide].astype(BF16)
        for side, piece in ((0, 1), (1, 0)):
            copy = side_copy(phase, side, piece)
            copy.start()
            sent.append(copy)
        share_own = own()
        far_copy(phase, 0).wait_recv()
        side_send[phase, 0, 0] = (share_up[:, :wide] + opp_recv[phase, 0].astype(F32)).astype(BF16)
        copy = side_copy(phase, 0, 0)
        copy.start()
        sent.append(copy)
        far_copy(phase, 1).wait_recv()
        side_send[phase, 1, 1] = (share_down[:, wide:] + opp_recv[phase, 1].astype(F32)).astype(BF16)
        copy = side_copy(phase, 1, 1)
        copy.start()
        sent.append(copy)
        for side, piece in ((0, 1), (1, 0), (0, 0), (1, 1)):
            side_copy(phase, side, piece).wait_recv()
        halves = [
            share_own[:, piece * wide : piece * wide + wide]
            + side_recv[phase, 0, piece].astype(F32)
            + side_recv[phase, 1, piece].astype(F32)
            for piece in range(2)
        ]
        return jnp.concatenate(halves, axis=1), sent

    total, sent_one = reduce_rows(
        0,
        lambda: out_part(y_far),
        lambda: out_part(y_up),
        lambda: out_part(y_down),
        lambda: out_part(y),
    )
    own_rows = pl.ds(pl.multiple_of(core * half + y * part, 16), part)
    one = norm_rows(tokens[own_rows, :].astype(F32) + total, gains[0:1, :]).astype(BF16)
    for piece in range(2):
        hidden[y, piece] = one[:, piece * wide : piece * wide + wide]

    def hidden_copy(side, hop, piece):
        block = y if hop == 0 else (y_up if side else y_down)
        return pltpu.make_async_remote_copy(
            src_ref=hidden.at[block, piece],
            dst_ref=hidden.at[block, piece],
            send_sem=hid_send_sem.at[side, hop, piece],
            recv_sem=hid_recv_sem.at[side, hop, piece],
            device_id=at_y(y_down if side else y_up),
            device_id_type=MESH,
        )

    sent_two = []

    def send_hidden(side, hop, piece):
        copy = hidden_copy(side, hop, piece)
        copy.start()
        sent_two.append(copy)

    send_hidden(0, 0, 0)
    send_hidden(1, 0, 1)
    send_hidden(0, 0, 1)
    send_hidden(1, 0, 0)
    home = mod(x + z, NY)
    at_home = home == y
    my_row = (x * 2 + lax.div(z, 4)) * NY + y

    def cand_copy(offset):
        return pltpu.make_async_remote_copy(
            src_ref=cand_mine,
            dst_ref=cand_rows.at[my_row],
            send_sem=cand_send_sem.at[offset],
            recv_sem=cand_recv_sem.at[my_row],
            device_id=(2 * home + core, mod(doc + offset, NX * NZ)),
            device_id_type=MESH,
        )

    cand_local = pltpu.make_async_copy(cand_mine, cand_rows.at[my_row], cand_recv_sem.at[my_row])
    for i in (6, 7):
        loads[i].wait()
    swaps[1].wait_recv()
    swaps[2].wait_recv()

    def feed(other):
        rows = jnp.concatenate([hidden[other, 0], hidden[other, 1]], axis=1)
        made = None
        for i in range(2):
            inner = gelu(jnp.dot(rows, w_up[i], preferred_element_type=F32)).astype(BF16)
            term = jnp.dot(inner, w_down[i], preferred_element_type=F32)
            made = term if made is None else made + term
        return made

    feed_own = feed(y)
    pl.when(at_home)(lambda: cand_local.start())
    pl.when(jnp.logical_not(at_home))(lambda: cand_copy(0).start())
    pl.loop(1, NX * NZ)(lambda offset: cand_copy(offset).start())
    hidden_copy(0, 0, 0).wait_recv()
    send_hidden(0, 1, 0)
    hidden_copy(1, 0, 1).wait_recv()
    send_hidden(1, 1, 1)
    hidden_copy(0, 0, 1).wait_recv()
    hidden_copy(1, 0, 0).wait_recv()
    feed_up, feed_down = feed(y_up), feed(y_down)
    hidden_copy(0, 1, 0).wait_recv()
    hidden_copy(1, 1, 1).wait_recv()
    lane = lax.broadcasted_iota(jnp.int32, (NX * NZ, 128), 1)
    table_copy = pltpu.make_async_copy(table, table_smem, table_sem.at[0])

    def slots_then_own():
        @pl.loop(0, NX * NZ)
        def _(row):
            pltpu.make_async_copy(cand_mine, cand_rows.at[row], cand_recv_sem.at[row]).wait()

        named = cand_rows[...].reshape(NX * NZ, 128)
        mine = jnp.logical_and(lax.shift_right_logical(named, 6) == doc, lax.bitwise_and(lane, 15) < 12)
        mine_f = jnp.where(mine, 1.0, 0.0)
        before = (
            lax.broadcasted_iota(jnp.int32, (128, 128), 0) < lax.broadcasted_iota(jnp.int32, (128, 128), 1)
        ).astype(F32).astype(BF16)
        rank = jnp.dot(mine_f.astype(BF16), before, preferred_element_type=F32)
        rows_table = jnp.zeros((NX * NZ, 128), jnp.int32)
        for slot in range(SLOTS):
            chosen = jnp.where(rank == float(slot), mine_f, 0.0)
            some = jnp.sum(chosen, axis=1, keepdims=True)
            place = jnp.sum(chosen * lane.astype(F32), axis=1, keepdims=True).astype(jnp.int32)
            which = jnp.sum(
                chosen * lax.bitwise_and(named, DOC_DEV - 1).astype(F32), axis=1, keepdims=True
            ).astype(jnp.int32)
            rows_table = jnp.where(lane == slot + 16, jnp.where(some > 0.5, place, 127), rows_table)
            rows_table = jnp.where(lane == slot, lax.bitwise_and(place, 15) * 2, rows_table)
            rows_table = jnp.where(lane == slot + 8, which, rows_table)
        table[...] = rows_table
        table_copy.start()
        return feed_own

    total_two, sent_three = reduce_rows(
        1, lambda: feed(y_far), lambda: feed_up, lambda: feed_down, slots_then_own
    )
    two = norm_rows(one.astype(F32) + total_two, gains[8:9, :]).astype(BF16)
    projected = jnp.dot(two, w_proj[...], preferred_element_type=F32)
    unit = projected * lax.rsqrt(jnp.sum(projected * projected, axis=-1, keepdims=True) + 1e-06)
    vectors[head] = unit.astype(BF16).reshape(3, 16, 128)

    half_doc = lax.div(z, 4)
    piece_rows = pl.ds(core * 12 + y * 3, 3)

    def spread_copy(offset):
        return pltpu.make_async_remote_copy(
            src_ref=vectors.at[head],
            dst_ref=near_queries.at[half_doc, piece_rows],
            send_sem=spread_send_sem.at[offset],
            recv_sem=spread_recv_sem.at[half_doc, y],
            device_id=(2 * home + core, x * NZ + mod(z + offset, NZ)),
            device_id_type=MESH,
        )

    def across_copy(half_index, source_y, offset, index):
        rows = pl.ds(core * 12 + source_y * 3, 3)
        return pltpu.make_async_remote_copy(
            src_ref=near_queries.at[half_index, rows],
            dst_ref=queries.at[index, rows],
            send_sem=across_send_sem.at[half_index, source_y, offset - 1],
            recv_sem=across_recv_sem.at[half_index, source_y, offset - 1],
            device_id=(head, mod(x + offset, NX) * NZ + z),
            device_id_type=MESH,
        )

    def share_copy(place, index):
        held = near_queries.at[place] if place < 2 else queries.at[index]
        rows = held.at[pl.ds(core * 12, 12)]
        return pltpu.make_async_remote_copy(
            src_ref=rows,
            dst_ref=rows,
            send_sem=share_send_sem.at[place],
            recv_sem=share_recv_sem.at[place],
            device_id=partner,
            device_id_type=MESH,
        )

    spread_local = pltpu.make_async_copy(
        vectors.at[head], near_queries.at[half_doc, piece_rows], spread_recv_sem.at[half_doc, y]
    )
    pl.when(at_home)(lambda: spread_local.start())
    pl.when(jnp.logical_not(at_home))(lambda: spread_copy(0).start())
    for offset in (4, 3, 5, 2, 6, 1, 7):
        spread_copy(offset).start()
    sent_four = []
    for i, device in enumerate(peers):
        copy = pltpu.make_async_remote_copy(
            src_ref=vectors.at[head],
            dst_ref=vectors.at[head],
            send_sem=vec_send_sem.at[i],
            recv_sem=vec_recv_sem.at[i],
            device_id=device,
            device_id_type=MESH,
        )
        copy.start()
        sent_four.append(copy)
    crossing = []
    shared = []
    ahead = mod(mod(y - x, NY) - z, NZ)
    near = jnp.where(jnp.logical_or(ahead <= 2, ahead >= 6), 0, 1)
    for step, half_index in (
        (0, near),
        (1, near),
        (3, near),
        (0, 1 - near),
        (2, near),
        (1, 1 - near),
        (3, 1 - near),
        (2, 1 - near),
    ):
        source_y = mod(y + step, NY)
        pltpu.make_async_copy(
            vectors.at[head],
            near_queries.at[half_index, pl.ds(core * 12 + source_y * 3, 3)],
            spread_recv_sem.at[half_index, source_y],
        ).wait()
        for offset in (2, 1, 3):
            crossing.append(across_copy(half_index, source_y, offset, x * 2 + half_index))
            crossing[-1].start()
    for half_index in range(2):
        shared.append(share_copy(half_index, x * 2 + half_index))
        shared[-1].start()
    for copy in sent_four:
        copy.wait_recv()
    outs = []
    for block in range(2 * NY):
        place = (block % 2) * 12 + (block // 2) * 3
        outs.append(
            pltpu.make_async_copy(vectors.at[block], query_out.at[pl.ds(place, 3)], load_sem.at[block])
        )
        outs[-1].start()
    table_copy.wait()
    loads[8].wait()

    zeros = jnp.zeros((QLEN, 128), BF16)
    row_index = lax.broadcasted_iota(jnp.int32, (256, 2 * QLEN), 0)
    first_lanes = lax.broadcasted_iota(jnp.int32, (1, 2 * QLEN), 1) < QLEN
    eight_lanes = lax.broadcasted_iota(jnp.int32, (8, 128), 1)

    def back_to(row):
        source_x, source_half, source_y = lax.div(row, 8), lax.rem(lax.div(row, NY), 2), lax.rem(row, NY)
        source = source_x * NZ + mod(y - source_x, NY) + 4 * source_half
        return source, source_y

    def back_copy(row):
        source, source_y = back_to(row)
        return pltpu.make_async_remote_copy(
            src_ref=back_send.at[row],
            dst_ref=back_recv.at[doc],
            send_sem=back_send_sem.at[row],
            recv_sem=back_recv_sem.at[doc],
            device_id=(2 * source_y + core, source),
            device_id_type=MESH,
        )

    def is_own(row):
        source, source_y = back_to(row)
        return jnp.logical_and(source == doc, source_y == y)

    def rate(source_x, local):
        base = source_x * 8

        for i, pair in [(i, pair) for i in range(8) for pair in range(SLOTS // 2)]:
            row = base + i
            held = near_queries.at[i // NY] if local else queries.at[source_x * 2 + i // NY]
            found = []
            for slot in (2 * pair, 2 * pair + 1):
                which = jnp.clip(table_smem[row, slot + 8], 0, DOC_DEV - 1)
                request = jnp.clip(table_smem[row, slot], 0, 22)
                query = jnp.concatenate([held[request], held[request + 1]], axis=0)
                found.append((docs[which], query, lengths_ref[which]))
            (doc_a, query_a, len_a), (doc_b, query_b, len_b) = found
            left = jnp.concatenate([doc_a, doc_b], axis=1)
            right = jnp.concatenate(
                [
                    jnp.concatenate([query_a, zeros], axis=1),
                    jnp.concatenate([zeros, query_b], axis=1),
                ],
                axis=0,
            )
            sims = lax.dot_general(left, right, NT, preferred_element_type=F32)
            live = row_index < jnp.where(first_lanes, len_a, len_b)
            best_rows[pair, pl.ds(row, 1), : 2 * QLEN] = jnp.max(
                jnp.where(live, sims, -jnp.inf), axis=0, keepdims=True
            )

        eight = pl.ds(pl.multiple_of(base, 8), 8)
        spots = table[eight, :]
        rated = jnp.zeros((8, 128), F32)
        for slot in range(SLOTS):
            low = (slot % 2) * QLEN
            value = jnp.sum(best_rows[slot // 2, eight, low : low + QLEN], axis=1, keepdims=True)
            rated = rated + jnp.where(eight_lanes == spots[:, slot + 16 : slot + 17], value, 0.0)
        back_send[pl.ds(base, 8)] = rated.reshape(8, 1, 128)

    def send_back(source_x, local):
        for step in (2, 1, 3, 0):
            for half_index in range(2):
                row = source_x * 8 + half_index * NY + mod(y + step, NY)
                if local and step == 0:
                    own_row = is_own(row)
                    pl.when(own_row)(
                        lambda row=row: pltpu.make_async_copy(
                            back_send.at[row], back_recv.at[doc], back_recv_sem.at[doc]
                        ).start()
                    )
                    pl.when(jnp.logical_not(own_row))(lambda row=row: back_copy(row).start())
                else:
                    back_copy(row).start()

    for copy in shared:
        copy.wait_recv()
    rate(x, True)
    send_back(x, True)
    for offset in (1, 3, 2):
        for half_index in range(2):
            index = mod(x - offset, NX) * 2 + half_index
            for source_y in range(NY):
                across_copy(half_index, source_y, offset, index).wait_recv()
            shared.append(share_copy(2 * offset + half_index, index))
            shared[-1].start()
    for copy in shared[2:]:
        copy.wait_recv()
    for offset in (2, 1, 3):
        rate(mod(x - offset, NX), False)
        send_back(mod(x - offset, NX), False)

    pl.when(jnp.logical_not(at_home))(lambda: cand_copy(0).wait_send())
    pl.loop(1, NX * NZ)(lambda offset: cand_copy(offset).wait_send())
    pl.when(jnp.logical_not(at_home))(lambda: spread_copy(0).wait_send())
    for offset in range(1, NZ):
        spread_copy(offset).wait_send()
    for copy in list(copies.values()) + swaps + [att_copy] + sent_one + sent_two + sent_three + sent_four + crossing + shared:
        copy.wait_send()

    for copy in outs:
        copy.wait()

    @pl.loop(0, NX * NZ)
    def _(row):
        pltpu.make_async_copy(back_send.at[0], back_recv.at[row], back_recv_sem.at[row]).wait()

    answer = jnp.broadcast_to(jnp.sum(back_recv[...], axis=0), (8, 128))
    spot = lax.broadcasted_iota(jnp.int32, (8, 128), 0)
    turned = answer
    for i in range(1, 8):
        turned = jnp.where(spot == i, pltpu.roll(answer, 128 - 16 * i, 1), turned)
    score_tile[...] = turned[:, : score_tile.shape[1]]
    outs.append(pltpu.make_async_copy(score_tile, score_out, load_sem.at[8]))
    outs[-1].start()

    @pl.loop(0, NX * NZ)
    def _(row):
        pl.when(jnp.logical_not(is_own(row)))(lambda: back_copy(row).wait_send())
    outs[-1].wait()


def encode(tokens, w_qkv, w_out, w_up, w_down, gain_one, gain_two, rel_table, prompt_cache, w_proj, docs, lengths, named, group_ids):
    plan = plan_gather()
    rows, width = tokens.shape
    half = rows // 2
    part = half // NY
    anywhere = pl.BlockSpec(memory_space=pl.ANY)
    dma = pltpu.SemaphoreType.DMA
    return pl.pallas_call(
        functools.partial(encoder_kernel, plan),
        out_shape=(
            jax.ShapeDtypeStruct((rows // 16, 16, 128), BF16),
            jax.ShapeDtypeStruct(named.shape, F32),
        ),
        in_specs=[anywhere] * 14,
        out_specs=(anywhere, anywhere),
        scratch_shapes=[
            pltpu.SMEM(group_ids.shape, jnp.int32),
            pltpu.VMEM((16, width), F32),
            pltpu.VMEM((width, 128), BF16),
            pltpu.SMEM(lengths.shape, jnp.int32),
            pltpu.VMEM(named.shape, jnp.int32),
            pltpu.VMEM((8, 128), jnp.int32),
            pltpu.VMEM((1, 128), jnp.int32),
            pltpu.VMEM(named.shape, F32),
            pltpu.VMEM((64, PLEN, 128), BF16),
            pltpu.VMEM((64, PLEN, 128), BF16),
            pltpu.VMEM((rows // QLEN, 2 * QLEN, 128), BF16),
            pltpu.VMEM((rows // QLEN, 2 * QLEN, 128), F32),
            pltpu.VMEM((rows, width), BF16),
            pltpu.VMEM((3, width, 128), BF16),
            pltpu.VMEM((2, 128, width), BF16),
            pltpu.VMEM((2, width, 512), BF16),
            pltpu.VMEM((2, 512, width), BF16),
            pltpu.VMEM((2, 128, width), BF16),
            pltpu.VMEM((2, rows, 128), BF16),
            pltpu.VMEM((rows, 128), BF16),
            pltpu.VMEM((rows, 128), BF16),
            pltpu.VMEM((rows, 256), F32),
            pltpu.VMEM((2, 256, 128), BF16),
            pltpu.VMEM((2, half, 128), BF16),
            pltpu.VMEM((half, 128), BF16),
            pltpu.VMEM((2, 2, part, 512), BF16),
            pltpu.VMEM((2, 2, 2, part, 512), BF16),
            pltpu.VMEM((2, 2, part, 512), BF16),
            pltpu.VMEM((2, 2, 2, part, 512), BF16),
            pltpu.VMEM((NY, 2, part, 512), BF16),
            pltpu.VMEM((2 * NY, 3, 16, 128), BF16),
            dma((16,)),
            dma((len(plan),)),
            dma((len(plan),)),
            dma((3,)),
            dma((3,)),
            dma((2,)),
            dma((2, 2)),
            dma((2, 2)),
            dma((2, 2, 2)),
            dma((2, 2, 2)),
            dma((2, 2, 2)),
            dma((2, 2, 2)),
            dma((7,)),
            dma((7,)),
            pltpu.VMEM((64, 256, 128), BF16),
            pltpu.VMEM((8, 24, 16, 128), BF16),
            pltpu.VMEM((2, 24, 16, 128), BF16),
            pltpu.VMEM((32, 1, 128), jnp.int32),
            pltpu.VMEM((32, 128), jnp.int32),
            pltpu.SMEM((32, 128), jnp.int32),
            pltpu.VMEM((SLOTS // 2, 32, 128), F32),
            pltpu.VMEM((32, 1, 128), F32),
            pltpu.VMEM((32, 1, 128), F32),
            dma((1,)),
            dma((32,)),
            dma((32,)),
            dma((8,)),
            dma((2, 4)),
            dma((2, 4, 3)),
            dma((2, 4, 3)),
            dma((8,)),
            dma((8,)),
            dma((32,)),
            dma((32,)),
        ],
        compiler_params=pltpu.CompilerParams(collective_id=0, has_side_effects=True),
        name="encoder",
    )(
        group_ids,
        tokens,
        jnp.transpose(w_qkv, (1, 0, 2)),
        w_out,
        w_up,
        w_down,
        gain_one.reshape(1, -1),
        gain_two.reshape(1, -1),
        rel_table,
        prompt_cache.reshape(2, 2, PLEN, 128),
        w_proj,
        docs,
        lengths,
        named,
    )


def body(
    tokens,
    w_qkv,
    w_out,
    w_up,
    w_down,
    gain_one,
    gain_two,
    rel_table,
    prompt_cache,
    w_proj,
    doc_vectors,
    doc_lengths,
    group_ids,
    candidates,
):
    query_vectors, rated = encode(
        tokens,
        w_qkv,
        w_out,
        w_up,
        w_down,
        gain_one,
        gain_two,
        rel_table,
        prompt_cache,
        w_proj,
        doc_vectors,
        doc_lengths,
        candidates.T,
        group_ids,
    )
    return (query_vectors.reshape(tokens.shape[0], 128), rated.T)


def solution(mesh):
    placed = (
        P("doc", None),
        P(None, None, "head"),
        P("head", None),
        P(None, "head"),
        P("head", None),
        P(),
        P(),
        P(),
        P(None, "doc", "head"),
        P(),
        P("doc", None, None),
        P("doc"),
        P("doc"),
        P("doc", "head"),
    )
    return jax.shard_map(
        body,
        mesh=mesh,
        in_specs=placed,
        out_specs=(P("doc", None), P("doc", "head")),
        check_vma=False,
    )
```
